256 devices in a mesh: group: 16 (over y, x_hi, core), band: 16 (over z, x_lo).
Axes of the slice: x: 4 (x_hi: 2, x_lo: 2; x = x_hi * 2 + x_lo), y: 4, z: 8, core: 2. Of those that a mesh axis runs over, the one named last changes fastest.
Arguments:
- station_rows: int32 [16, 384, 128], P('group', 'band'), may hold values from 0 to 3
- station_lons: int32 [16, 384, 128], P('group', 'band'), may hold values from 0 to 1439
- station_obs: float32 [16, 384, 128], P('group', 'band'), may hold values from -6 to 6
- station_live: int32 [16, 384, 128], P('group', 'band'), may hold values 0 or 1
- block_band: int32 [16, 384, 1], P('group', 'band'), may hold values from 0 to 15; in each aligned block of 24 rows (0 to 23, 24 to 47, ..., all dimensions but the last counted through in order) at most 3 rows name the same one
- truth_field: float32 [16, 64, 1440], P('group', 'band'), may hold values from -6 to 6
- length_scales: float32 [4], replicated, may hold values from 1.5 to 6
- w_in: bfloat16 [3, 3, 32, 8], replicated, may hold values from -0.75 to 0.75
- w_down: bfloat16 [4, 4, 32, 32], replicated, may hold values from -0.25 to 0.25
- w_mid: bfloat16 [3, 3, 32, 32], replicated, may hold values from -0.375 to 0.375
- w_up: bfloat16 [3, 3, 32, 64], replicated, may hold values from -0.25 to 0.25
- w_head: bfloat16 [2, 32], replicated, may hold values from -1 to 1
Outputs:
- mean_field: float32 [16, 64, 1440], P('group', 'band')
- grad_in: float32 [3, 3, 32, 8], replicated
- grad_down: float32 [4, 4, 32, 32], replicated
- grad_mid: float32 [3, 3, 32, 32], replicated
- grad_up: float32 [3, 3, 32, 64], replicated
- grad_head: float32 [2, 32], replicated
The draws below stay inside these ranges and needn't reach their ends.
Inputs may be any that keep to these rules, and one draw needn't show every extreme that they name: `block_band`: among the 24 blocks of one device no band is named by more than 3 blocks, and that number is reached.
All inputs are finite; a program needn't handle non-finite values. No bound on the sum of `station_live` on one device may be relied on, other than what follows from the above.
Results may differ from the reference program's by a relative error of at most 0.0025.
The reference program's roundings to bfloat16 on the way count: a program that leaves them out, or rounds other values in their place, can miss the bound.
Values may be sent and summed in bfloat16 or wider, within the bound.
A program may use at most 64 MiB of HBM per device.

```python
import math
import jax
import jax.numpy as jnp
import numpy as np
from jax import lax

C = 32
SCALES = 4
LON = 1440
BS = 128
ROWS_DEV = 4
NBLK = 24
SC = 8
CAP = 3
DATES = 16
LAT = 64
BLOCKS = 384
N_BAND = 16


def plant(drawn, stream_key, smallest, top_value):
    dims = drawn.shape
    index_at = [jax.random.randint(jax.random.fold_in(stream_key, axis), (), 0, dims[axis]) for axis in range(len(dims))]
    drawn = drawn.at[tuple(index_at)].set(smallest)
    longest = dims.index(max(dims))
    index_at[longest] = (index_at[longest] + 1) % dims[longest]
    return drawn.at[tuple(index_at)].set(top_value)


def block_scale(rng, extent, cuts, least, largest):
    gain, own = 1.0, jax.random.fold_in(rng, 6)
    for position, shards_of in cuts:
        steps = jnp.exp(jax.random.uniform(jax.random.fold_in(own, position), (shards_of,), jnp.float32, least / len(cuts), largest / len(cuts)))
        gain = gain * jnp.repeat(steps, extent[position] // shards_of).reshape([-1 if axis == position else 1 for axis in range(len(extent))])
    return gain


def deal_out(stream_key, own, number, rows, count, top, reach, slope):
    sequence = jax.random.permutation(stream_key, count)
    packed, ordinary = portions_of(count, rows * top, reach, slope, True), portions_of(count, rows * top, reach, slope, False)
    places = jnp.arange(count)

    def named(lengths, turn):
        used = int((lengths > 0).sum())
        fixed = max(1, used // 4)
        passed = fixed + (places - fixed + turn * (used - fixed)) % max(1, count - fixed)
        return jnp.zeros((count,), jnp.int32).at[sequence[jnp.where(places < fixed, places, passed)]].set(jnp.asarray(lengths, jnp.int32))

    lengths = jnp.where(number % 4 == 0, named(packed, number // 4), named(ordinary, number - number // 4 - 1))
    mixed = jax.random.permutation(jax.random.fold_in(own, 3), count)
    donor, sink = mixed[0:count // 2 * 2:2], mixed[1:count // 2 * 2:2]
    room = jnp.minimum(lengths[donor] - 1, reach - lengths[sink]) // 2
    room = jnp.where((donor == sequence[0]) | (sink == sequence[0]) | (lengths[sink] == 0), 0, jnp.maximum(room, 0))
    passed = jax.random.randint(jax.random.fold_in(own, 4), (count // 2,), 0, 1 << 20) % (room + 1)
    lengths = lengths.at[donor].add(-passed).at[sink].add(passed)
    items = jnp.searchsorted(jnp.cumsum(lengths), jnp.arange(rows * top), side="right").astype(jnp.int32)
    grid = items.reshape(top, rows).T
    grid = grid[jax.random.permutation(jax.random.fold_in(own, 1), rows)]
    turn = jax.random.randint(jax.random.fold_in(own, 2), (rows, 1), 0, top)
    return jnp.take_along_axis(grid, (jnp.arange(top)[None, :] + turn) % top, axis=1)


def portions_of(count, total, reach, skew, full):
    loads = [(1 << 20) // math.isqrt(grade ** skew) + 1 for grade in range(1, count + 1)]
    largest = reach if full else min(reach, max(-(-total // count), total * loads[0] // sum(loads)))
    least = 1 if total - largest >= count - 1 else 0
    holding, rest = [largest] + [least] * (count - 1), total - largest - least * (count - 1)
    while rest > 0:
        candidates = [i for i in range(1, count) if holding[i] < largest] or [i for i in range(1, count) if holding[i] < reach]
        whole, left = sum([loads[i] for i in candidates]), rest
        for i in candidates:
            extra = min(reach - holding[i], max(1, left * loads[i] // whole), rest)
            holding[i] = holding[i] + extra
            rest = rest - extra
    return np.array(holding)


def scatter_about(rng, dims, scale, most, split=(), held_as=jnp.bfloat16):
    values = scale * jax.random.normal(rng, dims, jnp.float32)
    if split:
        values = values * block_scale(rng, dims, split, -0.22, 0.18)
    return jnp.clip(values, -most, most).astype(held_as)


def setup_inputs(seed: int = 0) -> dict:
    arg_keys = jax.random.split(jax.random.key(seed), 13)
    station_rows = plant(jax.random.randint(arg_keys[0], (DATES, BLOCKS, BS), 0, ROWS_DEV), jax.random.fold_in(arg_keys[0], 1), 0, ROWS_DEV - 1).astype(jnp.int32)
    station_lons = plant(jax.random.randint(arg_keys[1], (DATES, BLOCKS, BS), 0, LON), jax.random.fold_in(arg_keys[1], 1), 0, LON - 1).astype(jnp.int32)
    station_obs = scatter_about(arg_keys[2], (DATES, BLOCKS, BS), 1.0, 6.0, ((0, 16), (1, 16)), jnp.float32)
    station_live = plant((jax.random.randint(arg_keys[3], (DATES, BLOCKS, BS), 0, 4) < 3).astype(jnp.int32), jax.random.fold_in(arg_keys[3], 1), 0, 1)
    block_band_keys = jax.random.split(jax.random.fold_in(arg_keys[4], 1), DATES * BLOCKS // NBLK)
    block_band_turns = jax.random.permutation(jax.random.fold_in(arg_keys[4], 3), DATES * BLOCKS // NBLK)
    block_band = jax.vmap(lambda own, number: deal_out(jax.random.fold_in(arg_keys[4], 2), own, number, NBLK, N_BAND, 1, CAP, 2))(block_band_keys, block_band_turns).reshape((DATES, BLOCKS, 1))
    truth_field = scatter_about(arg_keys[5], (DATES, LAT, LON), 1.0, 6.0, ((0, 16), (1, 16)), jnp.float32)
    length_scales = jnp.clip(jnp.exp(jax.random.uniform(arg_keys[6], (SCALES,), jnp.float32, math.log(1.5), math.log(6.0))), 1.5, 6.0)
    w_in = scatter_about(arg_keys[7], (3, 3, C, SC), (9 * SC) ** -0.5, 0.75)
    w_down = scatter_about(arg_keys[8], (4, 4, C, C), (16 * C) ** -0.5, 0.25)
    w_mid = scatter_about(arg_keys[9], (3, 3, C, C), (9 * C) ** -0.5, 0.375)
    w_up = scatter_about(arg_keys[10], (3, 3, C, 2 * C), (18 * C) ** -0.5, 0.25)
    w_head = scatter_about(arg_keys[11], (2, C), C ** -0.5, 1.0)
    return {"station_rows": station_rows, "station_lons": station_lons, "station_obs": station_obs, "station_live": station_live, "block_band": block_band, "truth_field": truth_field, "length_scales": length_scales, "w_in": w_in, "w_down": w_down, "w_mid": w_mid, "w_up": w_up, "w_head": w_head}


PHASES = (((1, 0), (3, -1)), ((0, 1), (2, 0)))


def widen(values):
    return lax.optimization_barrier(values).astype(jnp.float32)


def contract(form, first, second):
    return jnp.einsum(form, widen(first), widen(second))


def wrap_cols(values, left_count, right_count):
    total_cols = values.shape[-1]
    return jnp.concatenate([values[..., total_cols - left_count:], values, values[..., :right_count]], axis=-1)


def zero_rims(values, margin):
    zeros = jnp.zeros((margin,) + values.shape[1:], values.dtype)
    return jnp.concatenate([zeros, values, zeros], axis=0)


def conv_three(padded, weight, dilate):
    row_count = padded.shape[0] - 2 * dilate
    widened = wrap_cols(padded, dilate, dilate)
    col_count = widened.shape[-1] - 2 * dilate
    summed = None
    for tap_row in range(3):
        for tap_col in range(3):
            window = widened[tap_row * dilate:tap_row * dilate + row_count, :, tap_col * dilate:tap_col * dilate + col_count]
            contrib = contract("oc,rcl->rol", weight[tap_row, tap_col], window)
            summed = contrib if summed is None else summed + contrib
    return summed


def grad_three(padded, grad_out, dilate):
    row_count = grad_out.shape[0]
    col_count = grad_out.shape[-1]
    widened = wrap_cols(padded, dilate, dilate)
    pieces = []
    for tap_row in range(3):
        for tap_col in range(3):
            window = widened[tap_row * dilate:tap_row * dilate + row_count, :, tap_col * dilate:tap_col * dilate + col_count]
            pieces.append(contract("rol,rcl->oc", grad_out, window))
    stacked = jnp.stack(pieces)
    return stacked.reshape((3, 3) + stacked.shape[1:])


def conv_down(padded, weight):
    row_count = (padded.shape[0] - 2) // 2
    widened = wrap_cols(padded, 1, 1)
    col_count = (widened.shape[-1] - 2) // 2
    summed = None
    for tap_row in range(4):
        for tap_col in range(4):
            window = widened[tap_row:tap_row + 2 * row_count - 1:2, :, tap_col:tap_col + 2 * col_count - 1:2]
            contrib = contract("oc,rcl->rol", weight[tap_row, tap_col], window)
            summed = contrib if summed is None else summed + contrib
    return summed


def grad_strided(padded, grad_out):
    row_count = grad_out.shape[0]
    col_count = grad_out.shape[-1]
    widened = wrap_cols(padded, 1, 1)
    pieces = []
    for tap_row in range(4):
        for tap_col in range(4):
            window = widened[tap_row:tap_row + 2 * row_count - 1:2, :, tap_col:tap_col + 2 * col_count - 1:2]
            pieces.append(contract("rol,rcl->oc", grad_out, window))
    stacked = jnp.stack(pieces)
    return stacked.reshape((4, 4) + stacked.shape[1:])


def back_down(grad_pad, weight):
    row_count = grad_pad.shape[0] - 2
    widened = wrap_cols(grad_pad, 1, 1)
    col_count = widened.shape[-1] - 2
    phase_rows = []
    for phase_row in range(2):
        phase_cols = []
        for phase_col in range(2):
            summed = None
            for tap_row, shift_row in PHASES[phase_row]:
                for tap_col, shift_col in PHASES[phase_col]:
                    window = widened[1 + shift_row:1 + shift_row + row_count, :, 1 + shift_col:1 + shift_col + col_count]
                    contrib = contract("oc,rol->rcl", weight[tap_row, tap_col], window)
                    summed = contrib if summed is None else summed + contrib
            phase_cols.append(summed)
        phase_rows.append(jnp.stack(phase_cols, axis=-1))
    stacked = jnp.stack(phase_rows, axis=1)
    return stacked.reshape(2 * row_count, stacked.shape[2], 2 * col_count)


def flipped(weight):
    return jnp.transpose(weight[::-1, ::-1], (0, 1, 3, 2))


def silu_slope(pre_act):
    squash = jax.nn.sigmoid(pre_act)
    return squash * (1.0 + pre_act * (1.0 - squash))


def station_terms(row_pos, lon_pos, observed, alive, length_scales, row_count, lon_count):
    grid_rows = jnp.arange(row_count).astype(jnp.float32)
    grid_lons = jnp.arange(lon_count).astype(jnp.float32)
    row_gap = grid_rows[None, None, :] - row_pos[:, :, None]
    lon_gap = jnp.abs(grid_lons[None, None, :] - lon_pos[:, :, None])
    lon_gap = jnp.minimum(lon_gap, lon_count - lon_gap)
    factors = jnp.stack([alive, alive * observed], axis=2)
    per_scale = []
    for scale_index in range(length_scales.shape[0]):
        spread = length_scales[scale_index]
        left_side = (factors[:, :, :, None] * jnp.exp(-0.5 * (row_gap / spread) ** 2)[:, :, None, :]).astype(jnp.bfloat16)
        right_side = jnp.exp(-0.5 * (lon_gap / spread) ** 2).astype(jnp.bfloat16)
        per_scale.append(contract("bskr,bsl->brkl", left_side, right_side))
    stacked = jnp.stack(per_scale, axis=2)
    return stacked.reshape(stacked.shape[0], row_count, 2 * length_scales.shape[0], lon_count)


def features_of(sums):
    density = sums[:, 0::2]
    signal = sums[:, 1::2]
    scaled = jnp.stack([density / (1.0 + density), signal / (1.0 + density)], axis=2)
    return scaled.reshape(sums.shape).astype(jnp.bfloat16)


def network(features, truth_date, w_in, w_down, w_mid, w_up, w_head, cell_count):
    feat_pad = zero_rims(features, 1)
    pre_one = conv_three(feat_pad, w_in, 1)
    hidden_one = jax.nn.silu(pre_one).astype(jnp.bfloat16)
    one_pad = zero_rims(hidden_one, 1)
    pre_two = conv_down(one_pad, w_down)
    hidden_two = jax.nn.silu(pre_two).astype(jnp.bfloat16)
    two_pad = zero_rims(hidden_two, 2)
    pre_three = conv_three(two_pad, w_mid, 2)
    hidden_three = jax.nn.silu(pre_three).astype(jnp.bfloat16)
    upsampled = jnp.repeat(jnp.repeat(hidden_three, 2, axis=0), 2, axis=2)
    joined_pad = jnp.concatenate([zero_rims(upsampled, 1), one_pad], axis=1)
    pre_four = conv_three(joined_pad, w_up, 1)
    hidden_four = jax.nn.silu(pre_four).astype(jnp.bfloat16)
    head_out = contract("kc,rcl->rkl", w_head, hidden_four)
    mean_field = head_out[:, 0]
    raw_spread = head_out[:, 1]
    noise_scale = 0.1 + jax.nn.softplus(raw_spread)
    scaled_error = (mean_field - truth_date) / noise_scale
    grad_mean = scaled_error / (noise_scale * cell_count)
    grad_raw = (1.0 - scaled_error * scaled_error) / (noise_scale * cell_count) * jax.nn.sigmoid(raw_spread)
    grad_head_out = jnp.stack([grad_mean, grad_raw], axis=1).astype(jnp.bfloat16)
    grad_head = contract("rkl,rcl->kc", grad_head_out, hidden_four)
    grad_hidden_four = contract("kc,rkl->rcl", w_head, grad_head_out)
    grad_pre_four = (grad_hidden_four * silu_slope(pre_four)).astype(jnp.bfloat16)
    grad_up = grad_three(joined_pad, grad_pre_four, 1)
    grad_joined = conv_three(zero_rims(grad_pre_four, 1), flipped(w_up), 1).astype(jnp.bfloat16)
    grad_joined = lax.optimization_barrier(grad_joined)
    channels = hidden_one.shape[1]
    grad_upsampled = grad_joined[:, :channels].astype(jnp.float32)
    half_rows = hidden_three.shape[0]
    half_cols = hidden_three.shape[2]
    grad_hidden_three = grad_upsampled.reshape(half_rows, 2, channels, half_cols, 2).sum(axis=(1, 4))
    grad_pre_three = (grad_hidden_three * silu_slope(pre_three)).astype(jnp.bfloat16)
    grad_mid = grad_three(two_pad, grad_pre_three, 2)
    grad_hidden_two = conv_three(zero_rims(grad_pre_three, 2), flipped(w_mid), 2)
    grad_pre_two = (grad_hidden_two * silu_slope(pre_two)).astype(jnp.bfloat16)
    grad_down = grad_strided(one_pad, grad_pre_two)
    grad_hidden_one = back_down(zero_rims(grad_pre_two, 1), w_down) + grad_joined[:, channels:].astype(jnp.float32)
    grad_pre_one = (grad_hidden_one * silu_slope(pre_one)).astype(jnp.bfloat16)
    grad_in = grad_three(feat_pad, grad_pre_one, 1)
    return mean_field, (grad_in, grad_down, grad_mid, grad_up, grad_head)


def date_sums(rows_date, lons_date, obs_date, live_date, band_date, length_scales):
    def one_group(running, group):
        rows_group, lons_group, obs_group, live_group, band_group = group
        terms = station_terms(rows_group.astype(jnp.float32), lons_group.astype(jnp.float32), obs_group, live_group.astype(jnp.float32), length_scales, ROWS_DEV, LON)
        running = running + jax.ops.segment_sum(terms, band_group, num_segments=N_BAND)
        return running, None

    grouped = tuple(values.reshape((N_BAND, NBLK) + values.shape[1:]) for values in (rows_date, lons_date, obs_date, live_date, band_date[:, 0]))
    initial = jnp.zeros((N_BAND, ROWS_DEV, SC, LON), jnp.float32)
    running, _ = lax.scan(one_group, initial, grouped)
    return running.reshape(LAT, SC, LON)


def reference(station_rows, station_lons, station_obs, station_live, block_band, truth_field, length_scales, w_in, w_down, w_mid, w_up, w_head):
    def one_date(inputs):
        rows_date, lons_date, obs_date, live_date, band_date, truth_date = inputs
        sums = date_sums(rows_date, lons_date, obs_date, live_date, band_date, length_scales)
        features = features_of(sums)
        return network(features, truth_date, w_in, w_down, w_mid, w_up, w_head, float(LAT * LON))

    mean_fields, grads = lax.map(one_date, (station_rows, station_lons, station_obs, station_live, block_band, truth_field))
    return (mean_fields, jnp.sum(grads[0], axis=0), jnp.sum(grads[1], axis=0), jnp.sum(grads[2], axis=0), jnp.sum(grads[3], axis=0), jnp.sum(grads[4], axis=0))
```

```python
import functools

import jax
import jax.numpy as jnp
from jax import lax
from jax.experimental import pallas as pl
from jax.experimental.pallas import tpu as pltpu
from jax.sharding import PartitionSpec as P

MESH = pl.DeviceIdType.MESH
LANES = 128

PHASES = (((1, 0), (3, -1)), ((0, 1), (2, 0)))


def extended(cells, sides, width):
    for axis, dim in sides:
        count = lax.axis_size(axis)
        ends = count - 1
        head = lax.slice_in_dim(cells, 0, width, axis=dim)
        tail = lax.slice_in_dim(cells, cells.shape[dim] - width, cells.shape[dim], axis=dim)
        cells = jnp.concatenate(
            [
                lax.ppermute(tail, axis, [(i, (i + 1) % count) for i in range(ends)]),
                cells,
                lax.ppermute(head, axis, [((i + 1) % count, i) for i in range(ends)]),
            ],
            axis=dim,
        )
    return cells


def wrap_cols(values, left_count, right_count):
    total_cols = values.shape[-1]
    return jnp.concatenate(
        [values[..., total_cols - left_count :], values, values[..., :right_count]], axis=-1
    )


def band_rims(values, margin):
    return extended(values, (("band", 0),), margin)


def conv_three(padded, weight, dilate):
    row_count = padded.shape[0] - 2 * dilate
    widened = wrap_cols(padded, dilate, dilate)
    col_count = widened.shape[-1] - 2 * dilate
    summed = None
    for tap_row in range(3):
        for tap_col in range(3):
            window = widened[
                tap_row * dilate : tap_row * dilate + row_count,
                :,
                tap_col * dilate : tap_col * dilate + col_count,
            ]
            contrib = jnp.einsum(
                "oc,rcl->rol", weight[tap_row, tap_col], window, preferred_element_type=jnp.float32
            )
            summed = contrib if summed is None else summed + contrib
    return summed


def grad_three(padded, grad_out, dilate):
    row_count = grad_out.shape[0]
    col_count = grad_out.shape[-1]
    widened = wrap_cols(padded, dilate, dilate)
    pieces = []
    for tap_row in range(3):
        for tap_col in range(3):
            window = widened[
                tap_row * dilate : tap_row * dilate + row_count,
                :,
                tap_col * dilate : tap_col * dilate + col_count,
            ]
            pieces.append(
                jnp.einsum("rol,rcl->oc", grad_out, window, preferred_element_type=jnp.float32)
            )
    stacked = jnp.stack(pieces)
    return stacked.reshape((3, 3) + stacked.shape[1:])


def conv_down(padded, weight):
    row_count = (padded.shape[0] - 2) // 2
    widened = wrap_cols(padded, 1, 1)
    col_count = (widened.shape[-1] - 2) // 2
    summed = None
    for tap_row in range(4):
        for tap_col in range(4):
            window = widened[
                tap_row : tap_row + 2 * row_count - 1 : 2,
                :,
                tap_col : tap_col + 2 * col_count - 1 : 2,
            ]
            contrib = jnp.einsum(
                "oc,rcl->rol", weight[tap_row, tap_col], window, preferred_element_type=jnp.float32
            )
            summed = contrib if summed is None else summed + contrib
    return summed


def grad_strided(padded, grad_out):
    row_count = grad_out.shape[0]
    col_count = grad_out.shape[-1]
    widened = wrap_cols(padded, 1, 1)
    pieces = []
    for tap_row in range(4):
        for tap_col in range(4):
            window = widened[
                tap_row : tap_row + 2 * row_count - 1 : 2,
                :,
                tap_col : tap_col + 2 * col_count - 1 : 2,
            ]
            pieces.append(
                jnp.einsum("rol,rcl->oc", grad_out, window, preferred_element_type=jnp.float32)
            )
    stacked = jnp.stack(pieces)
    return stacked.reshape((4, 4) + stacked.shape[1:])


def back_down(grad_pad, weight):
    row_count = grad_pad.shape[0] - 2
    widened = wrap_cols(grad_pad, 1, 1)
    col_count = widened.shape[-1] - 2
    phase_rows = []
    for phase_row in range(2):
        phase_cols = []
        for phase_col in range(2):
            summed = None
            for tap_row, shift_row in PHASES[phase_row]:
                for tap_col, shift_col in PHASES[phase_col]:
                    window = widened[
                        1 + shift_row : 1 + shift_row + row_count,
                        :,
                        1 + shift_col : 1 + shift_col + col_count,
                    ]
                    contrib = jnp.einsum(
                        "oc,rol->rcl",
                        weight[tap_row, tap_col],
                        window,
                        preferred_element_type=jnp.float32,
                    )
                    summed = contrib if summed is None else summed + contrib
            phase_cols.append(summed)
        phase_rows.append(jnp.stack(phase_cols, axis=-1))
    stacked = jnp.stack(phase_rows, axis=1)
    return stacked.reshape(2 * row_count, stacked.shape[2], 2 * col_count)


def flipped(weight):
    return jnp.transpose(weight[::-1, ::-1], (0, 1, 3, 2))


def silu_slope(pre_act):
    squash = jax.nn.sigmoid(pre_act)
    return squash * (1.0 + pre_act * (1.0 - squash))


def station_terms(slot_data, length_scales, row_count, lon_count):
    row_pos = slot_data[:, :, 0]
    lon_pos = slot_data[:, :, 1]
    observed = slot_data[:, :, 2]
    alive = slot_data[:, :, 3]
    grid_rows = jnp.arange(row_count).astype(jnp.float32)
    grid_lons = jnp.arange(lon_count).astype(jnp.float32)
    row_gap = grid_rows[None, None, None, :] - row_pos[..., None]
    lon_gap = jnp.abs(grid_lons[None, None, None, :] - lon_pos[..., None])
    lon_gap = jnp.minimum(lon_gap, lon_count - lon_gap)
    factors = jnp.stack([alive, alive * observed], axis=3)
    per_scale = []
    for scale_index in range(length_scales.shape[0]):
        spread = length_scales[scale_index]
        left_side = (
            factors[..., None] * jnp.exp(-0.5 * (row_gap / spread) ** 2)[:, :, :, None, :]
        ).astype(jnp.bfloat16)
        right_side = jnp.exp(-0.5 * (lon_gap / spread) ** 2).astype(jnp.bfloat16)
        per_scale.append(
            jnp.einsum(
                "gqskr,gqsl->grkl", left_side, right_side, preferred_element_type=jnp.float32
            )
        )
    stacked = jnp.stack(per_scale, axis=2)
    return stacked.reshape(stacked.shape[0], row_count, 2 * length_scales.shape[0], lon_count)


def slot_blocks(payload, own_bands, band_count, capacity):
    member = (own_bands[:, None] == jnp.arange(band_count, dtype=jnp.int32)[None, :]).astype(
        jnp.int32
    )
    earlier = jnp.cumsum(member, axis=0) - member
    slot_index = jnp.sum(earlier * member, axis=1)
    outgoing = jnp.zeros((band_count, capacity) + payload.shape[1:], jnp.float32)
    return outgoing.at[own_bands, slot_index].set(payload)


def features_of(sums):
    density = sums[:, 0::2]
    signal = sums[:, 1::2]
    scaled = jnp.stack([density / (1.0 + density), signal / (1.0 + density)], axis=2)
    return scaled.reshape(sums.shape).astype(jnp.bfloat16)


def network(features, truth_date, w_in, w_down, w_mid, w_up, w_head, cell_count):
    feat_pad = band_rims(features, 1)
    pre_one = conv_three(feat_pad, w_in, 1)
    hidden_one = jax.nn.silu(pre_one).astype(jnp.bfloat16)
    one_pad = band_rims(hidden_one, 1)
    pre_two = conv_down(one_pad, w_down)
    hidden_two = jax.nn.silu(pre_two).astype(jnp.bfloat16)
    two_pad = band_rims(hidden_two, 2)
    pre_three = conv_three(two_pad, w_mid, 2)
    hidden_three = jax.nn.silu(pre_three).astype(jnp.bfloat16)
    upsampled = jnp.repeat(jnp.repeat(hidden_three, 2, axis=0), 2, axis=2)
    joined_pad = jnp.concatenate([band_rims(upsampled, 1), one_pad], axis=1)
    pre_four = conv_three(joined_pad, w_up, 1)
    hidden_four = jax.nn.silu(pre_four).astype(jnp.bfloat16)
    head_out = jnp.einsum("kc,rcl->rkl", w_head, hidden_four, preferred_element_type=jnp.float32)
    mean_field = head_out[:, 0]
    raw_spread = head_out[:, 1]
    noise_scale = 0.1 + jax.nn.softplus(raw_spread)
    scaled_error = (mean_field - truth_date) / noise_scale
    grad_mean = scaled_error / (noise_scale * cell_count)
    grad_raw = (
        (1.0 - scaled_error * scaled_error)
        / (noise_scale * cell_count)
        * jax.nn.sigmoid(raw_spread)
    )
    grad_head_out = jnp.stack([grad_mean, grad_raw], axis=1).astype(jnp.bfloat16)
    grad_head = jnp.einsum(
        "rkl,rcl->kc", grad_head_out, hidden_four, preferred_element_type=jnp.float32
    )
    grad_hidden_four = jnp.einsum(
        "kc,rkl->rcl", w_head, grad_head_out, preferred_element_type=jnp.float32
    )
    grad_pre_four = (grad_hidden_four * silu_slope(pre_four)).astype(jnp.bfloat16)
    grad_up = grad_three(joined_pad, grad_pre_four, 1)
    grad_joined = conv_three(band_rims(grad_pre_four, 1), flipped(w_up), 1).astype(jnp.bfloat16)
    grad_joined = lax.optimization_barrier(grad_joined)
    channels = hidden_one.shape[1]
    grad_upsampled = grad_joined[:, :channels].astype(jnp.float32)
    half_rows = hidden_three.shape[0]
    half_cols = hidden_three.shape[2]
    grad_hidden_three = grad_upsampled.reshape(half_rows, 2, channels, half_cols, 2).sum(
        axis=(1, 4)
    )
    grad_pre_three = (grad_hidden_three * silu_slope(pre_three)).astype(jnp.bfloat16)
    grad_mid = grad_three(two_pad, grad_pre_three, 2)
    grad_hidden_two = conv_three(band_rims(grad_pre_three, 2), flipped(w_mid), 2)
    grad_pre_two = (grad_hidden_two * silu_slope(pre_two)).astype(jnp.bfloat16)
    grad_down = grad_strided(one_pad, grad_pre_two)
    grad_hidden_one = back_down(band_rims(grad_pre_two, 1), w_down) + grad_joined[
        :, channels:
    ].astype(jnp.float32)
    grad_pre_one = (grad_hidden_one * silu_slope(pre_one)).astype(jnp.bfloat16)
    grad_in = grad_three(feat_pad, grad_pre_one, 1)
    return (mean_field, (grad_in, grad_down, grad_mid, grad_up, grad_head))


def total_kernel(n_group, n_band, x_ref, o_ref, got, part, full, s1, r1, s2, r2, s3, r3):
    g = lax.axis_index("group")
    b = lax.axis_index("band")
    barrier = pltpu.get_barrier_semaphore()
    for k in range(1, n_group):
        pl.semaphore_signal(
            barrier, inc=1, device_id=(lax.rem(g + k, n_group), b), device_id_type=MESH
        )
    for k in range(1, n_band):
        pl.semaphore_signal(
            barrier, inc=1, device_id=(g, lax.rem(b + k, n_band)), device_id_type=MESH
        )
    pl.semaphore_wait(barrier, n_group + n_band - 2)

    def to_group(k, source, target, send, recv):
        peer = lax.rem(g + k, n_group)
        return pltpu.make_async_remote_copy(
            src_ref=source(peer),
            dst_ref=target.at[g],
            send_sem=send.at[k],
            recv_sem=recv.at[g],
            device_id=(peer, b),
            device_id_type=MESH,
        )

    def from_group(k, target, send, recv):
        peer = lax.rem(g + n_group - k, n_group)
        return pltpu.make_async_remote_copy(
            src_ref=target.at[peer],
            dst_ref=target.at[peer],
            send_sem=send.at[k],
            recv_sem=recv.at[peer],
            device_id=(peer, b),
            device_id_type=MESH,
        )

    firsts = [to_group(k, lambda t: x_ref.at[t], got, s1, r1) for k in range(1, n_group)]
    for copy in firsts:
        copy.start()
    got[g] = x_ref[g]
    for k in range(1, n_group):
        from_group(k, got, s1, r1).wait_recv()
    summed = got[0]
    for i in range(1, n_group):
        summed = summed + got[i]
    part[b] = summed
    seconds = []
    for k in range(1, n_band):
        peer = lax.rem(b + k, n_band)
        seconds.append(
            pltpu.make_async_remote_copy(
                src_ref=part.at[b],
                dst_ref=part.at[b],
                send_sem=s2.at[k],
                recv_sem=r2.at[b],
                device_id=(g, peer),
                device_id_type=MESH,
            )
        )
    for copy in seconds:
        copy.start()
    for k in range(1, n_band):
        peer = lax.rem(b + n_band - k, n_band)
        pltpu.make_async_remote_copy(
            src_ref=part.at[peer],
            dst_ref=part.at[peer],
            send_sem=s2.at[k],
            recv_sem=r2.at[peer],
            device_id=(g, peer),
            device_id_type=MESH,
        ).wait_recv()
    summed = part[0]
    for i in range(1, n_band):
        summed = summed + part[i]
    full[g] = summed
    thirds = [to_group(k, lambda t: full.at[g], full, s3, r3) for k in range(1, n_group)]
    for copy in thirds:
        copy.start()
    for k in range(1, n_group):
        from_group(k, full, s3, r3).wait_recv()
    o_ref[...] = full[...]
    for copy in firsts + seconds + thirds:
        copy.wait_send()


def grand_total(grads):
    n_group, n_band = lax.axis_size("group"), lax.axis_size("band")
    flat = jnp.concatenate([grad.reshape(-1) for grad in grads])
    rows = -(-flat.shape[0] // (n_group * 8 * LANES)) * 8
    flat = jnp.pad(flat, (0, n_group * rows * LANES - flat.shape[0]))
    block = (n_group, rows, LANES)
    dma = pltpu.SemaphoreType.DMA
    summed = pl.pallas_call(
        functools.partial(total_kernel, n_group, n_band),
        out_shape=jax.ShapeDtypeStruct(block, jnp.float32),
        in_specs=[pl.BlockSpec(memory_space=pltpu.VMEM)],
        out_specs=pl.BlockSpec(memory_space=pltpu.VMEM),
        scratch_shapes=[
            pltpu.VMEM(block, jnp.float32),
            pltpu.VMEM((n_band, rows, LANES), jnp.float32),
            pltpu.VMEM(block, jnp.float32),
            dma((n_group,)),
            dma((n_group,)),
            dma((n_band,)),
            dma((n_band,)),
            dma((n_group,)),
            dma((n_group,)),
        ],
        compiler_params=pltpu.CompilerParams(collective_id=0, has_side_effects=True),
    )(flat.reshape(block))
    summed = summed.reshape(-1)
    totals, start = [], 0
    for grad in grads:
        totals.append(lax.slice_in_dim(summed, start, start + grad.size).reshape(grad.shape))
        start += grad.size
    return totals


def local(
    station_rows,
    station_lons,
    station_obs,
    station_live,
    block_band,
    truth_field,
    length_scales,
    w_in,
    w_down,
    w_mid,
    w_up,
    w_head,
):
    band_count = lax.axis_size("band")
    block_count = station_rows.shape[1]
    row_count = truth_field.shape[1]
    lon_count = truth_field.shape[2]
    capacity = max(2, (2 * block_count + band_count - 1) // band_count)
    payload = jnp.stack(
        [
            station_rows[0].astype(jnp.float32),
            station_lons[0].astype(jnp.float32),
            station_obs[0],
            station_live[0].astype(jnp.float32),
        ],
        axis=1,
    )
    own_bands = block_band[0, :, 0]
    outgoing = slot_blocks(payload, own_bands, band_count, capacity)
    incoming = lax.all_to_all(outgoing, "band", split_axis=0, concat_axis=0, tiled=True)
    flat_slots = incoming.reshape((1, band_count * capacity) + incoming.shape[2:])
    grid_sums = station_terms(flat_slots, length_scales, row_count, lon_count)[0]
    features = features_of(grid_sums)
    cell_count = float(row_count * band_count * lon_count)
    mean_field, grads = network(
        features, truth_field[0], w_in, w_down, w_mid, w_up, w_head, cell_count
    )
    totals = grand_total(grads)
    return (mean_field[None], totals[0], totals[1], totals[2], totals[3], totals[4])


def solution(mesh):
    return jax.shard_map(
        local,
        mesh=mesh,
        in_specs=(
            P("group", "band", None),
            P("group", "band", None),
            P("group", "band", None),
            P("group", "band", None),
            P("group", "band", None),
            P("group", "band", None),
            P(),
            P(),
            P(),
            P(),
            P(),
            P(),
        ),
        out_specs=(P("group", "band", None), P(), P(), P(), P(), P()),
        check_vma=False,
    )
```

```python
import functools

import jax
import jax.numpy as jnp
from jax import lax
from jax.experimental import pallas as pl
from jax.experimental.pallas import tpu as pltpu
from jax.sharding import PartitionSpec as P

MESH = pl.DeviceIdType.MESH
F32 = jnp.float32
BF16 = jnp.bfloat16
PHASES = (((1, 0), (3, -1)), ((0, 1), (2, 0)))
ROWS = 4
LON = 1440
HALF = 720
NBLK = 24
CAP = 3
LANES = 128
CELL = 120
SLABS = 12
CELLS = 92160.0
VMEM_LIMIT = 56 * 1024 * 1024


def dot(first, second):
    return lax.dot_general(first, second, (((1,), (0,)), ((), ())), preferred_element_type=F32)


def dot_t(first, second):
    return lax.dot_general(first, second, (((1,), (1,)), ((), ())), preferred_element_type=F32)


def iota(shape, dim):
    return lax.broadcasted_iota(jnp.int32, shape, dim)


def eye(size):
    return (iota((size, size), 0) == iota((size, size), 1)).astype(F32).astype(BF16)


def later(values, count):
    width = values.shape[-1]
    return jnp.concatenate([values[:, width - count :], values[:, : width - count]], axis=1)


def earlier(values, count):
    return jnp.concatenate([values[:, count:], values[:, :count]], axis=1)


def thirds(values):
    high = values.astype(BF16).astype(F32)
    rest = values - high
    middle = rest.astype(BF16).astype(F32)
    return high, middle, rest - middle


def sigmoid(values):
    return 1.0 / (1.0 + jnp.exp(-values))


def slope(values):
    squash = sigmoid(values)
    return squash * (1.0 + values * (1.0 - squash))


def as_scale(flag):
    return flag.astype(jnp.int32).astype(F32)


def step_kernel(
    n_group,
    n_band,
    rows_ref,
    lons_ref,
    obs_ref,
    live_ref,
    truth_ref,
    w_in,
    w_down,
    w_mid,
    w_up,
    w_head,
    band_ref,
    ell_ref,
    mean_out,
    in_out,
    down_out,
    mid_out,
    up_out,
    head_out,
    picked,
    outbox,
    inbox,
    hist,
    gauss,
    feats32,
    own_f,
    far_f,
    x_f,
    x_one,
    pre_one,
    x_two,
    pre_two,
    pre_three,
    x_three,
    pre_four,
    h_four,
    g_four,
    far_four,
    x_gfour,
    big_a,
    big_b,
    gj_one,
    g_three,
    far_three,
    x_gthree,
    g_two,
    far_two,
    x_gtwo,
    g_one,
    wb_in,
    wb_down,
    wb_mid,
    wb_up3,
    wb_up1,
    db_up,
    db_mid,
    db_down,
    grads,
    got,
    part,
    full,
    s_a,
    r_a,
    s_f,
    r_f,
    s_4,
    r_4,
    s_3,
    r_3,
    s_2,
    r_2,
    s_g1,
    r_g1,
    s_b,
    r_b,
    s_g2,
    r_g2,
):
    g = lax.axis_index("group")
    b = lax.axis_index("band")
    barrier = pltpu.get_barrier_semaphore()
    for k in range(1, n_group):
        pl.semaphore_signal(
            barrier, inc=1, device_id=(lax.rem(g + k, n_group), b), device_id_type=MESH
        )
    for k in range(1, n_band):
        pl.semaphore_signal(
            barrier, inc=1, device_id=(g, lax.rem(b + k, n_band)), device_id_type=MESH
        )

    def band_peer(k):
        return lax.rem(b + n_band + k, n_band)

    def group_peer(k):
        return lax.rem(g + n_group + k, n_group)

    sent = []
    chunk = 48 // n_group

    def send(source, target, send_sem, recv_sem, device):
        copy = pltpu.make_async_remote_copy(
            src_ref=source,
            dst_ref=target,
            send_sem=send_sem,
            recv_sem=recv_sem,
            device_id=device,
            device_id_type=MESH,
        )
        copy.start()
        sent.append(copy)

    def arrive(target, send_sem, recv_sem, device):
        pltpu.make_async_remote_copy(
            src_ref=target,
            dst_ref=target,
            send_sem=send_sem,
            recv_sem=recv_sem,
            device_id=device,
            device_id_type=MESH,
        ).wait_recv()

    slot_rows = iota((n_band * CAP, LANES), 0)
    slot_band, slot_place = slot_rows // CAP, slot_rows % CAP
    seen = jnp.zeros((n_band * CAP, LANES), jnp.int32)
    chosen = [jnp.zeros((n_band * CAP, LANES), F32) for _ in range(4)]
    for block in range(NBLK):
        mine = slot_band == band_ref[0, block, 0]
        here = jnp.logical_and(mine, seen == slot_place)
        fields = (
            rows_ref[0, block : block + 1, :].astype(F32),
            lons_ref[0, block : block + 1, :].astype(F32),
            obs_ref[0, block : block + 1, :],
            live_ref[0, block : block + 1, :].astype(F32),
        )
        chosen = [jnp.where(here, new, old) for new, old in zip(fields, chosen)]
        seen = seen + mine.astype(jnp.int32)
    for field in range(4):
        picked[field] = chosen[field]
    for q in range(n_band):
        for field in range(4):
            outbox[q, CAP * field : CAP * field + CAP, :] = picked[
                field, CAP * q : CAP * q + CAP, :
            ]

    pl.semaphore_wait(barrier, n_group + n_band - 2)
    for k in range(1, n_band):
        peer = band_peer(k)
        send(outbox.at[peer], inbox.at[b], s_a.at[k], r_a.at[b], (g, peer))
    inbox[b] = outbox[b]

    wide = (2 * LANES, 2 * LANES)
    row_id, col_id = iota(wide, 0), iota(wide, 1)
    base = (
        2 * (col_id % LANES) + col_id // LANES - row_id % LANES + CELL * (row_id // LANES)
    ).astype(F32)
    coefs = []
    for scale in range(4):
        ell = jnp.full((1, 2 * LANES), ell_ref[scale], F32)
        coefs.append(-0.5 / (ell * ell))

    def gauss_step(e, carry):
        gap = jnp.abs(base + (2 * CELL * e).astype(F32))
        gap = jnp.minimum(gap, LON - gap)
        square = gap * gap
        cols = pl.ds(pl.multiple_of(e * 2 * LANES, 2 * LANES), 2 * LANES)
        for scale in range(4):
            gauss[scale, :, cols] = jnp.exp(square * coefs[scale]).astype(BF16)
        return carry

    lax.fori_loop(0, SLABS // 2, gauss_step, 0)

    for ref in (wb_in, wb_down, wb_mid, wb_up3, wb_up1, db_up, db_mid, db_down):
        ref[...] = jnp.zeros_like(ref)
    turned_up = dot_t(eye(64), w_up[...].reshape(288, 64)).astype(BF16)
    turned_mid = dot_t(eye(32), w_mid[...].reshape(288, 32)).astype(BF16)
    turned_down = dot_t(eye(32), w_down[...].reshape(512, 32)).astype(BF16)
    for a in range(3):
        for t in range(3):
            block = w_in[a, t]
            for i in range(3):
                for p in range(2):
                    row, col = (2 * i + p) * 32, (i + a) * 32 + (t + p) * 8
                    wb_in[row : row + 32, col : col + 8] = block
            upper, lower = w_up[a, t, :, :32], w_up[a, t, :, 32:]
            at = ((2 - a) * 3 + 2 - t) * 32
            for i in range(2):
                for p in range(2):
                    row, col = (2 * i + p) * 32, (i + a) * 128 + (t + p) * 32
                    wb_up3[row : row + 32, col : col + 32] = upper
                    wb_up1[row : row + 32, col : col + 32] = lower
                    db_up[2 * row : 2 * row + 64, col : col + 32] = turned_up[:, at : at + 32]
                row, col = i * 32, (i + 2 * a) * 96 + t * 32
                wb_mid[row : row + 32, col : col + 32] = w_mid[a, t]
                db_mid[row : row + 32, col : col + 32] = turned_mid[:, at : at + 32]
    for a in range(4):
        for t in range(4):
            for m in range(2):
                col = (2 * m + a) * 128 + t * 32
                wb_down[m * 32 : m * 32 + 32, col : col + 32] = w_down[a, t]
    for m in range(2):
        for s in range(2):
            for p in range(2):
                row = ((2 * m + s) * 2 + p) * 32
                for a, up_down in PHASES[s]:
                    for t, left_right in PHASES[p]:
                        col = (m + up_down + 1) * 96 + (left_right + 1) * 32
                        at = (a * 4 + t) * 32
                        db_down[row : row + 32, col : col + 32] = turned_down[:, at : at + 32]
    head_row, head_col = iota((8, 256), 0), iota((8, 256), 1)
    matches = (head_col // 32) == (head_row % 4) * 2 + head_row // 4
    parts = []
    for k in range(2):
        line = jnp.concatenate([w_head[k : k + 1, :].astype(F32)] * 8, axis=1)
        parts.append(jnp.where(matches, line, 0.0))
    wb_head = jnp.concatenate(parts, axis=0).astype(BF16)
    db_head = dot_t(eye(256), wb_head).astype(BF16)

    weave = (col_id == 2 * (row_id % LANES) + row_id // LANES).astype(F32).astype(BF16)
    truth = jnp.concatenate([truth_ref[0], jnp.zeros((ROWS, LON), F32)], axis=0)
    truth = jnp.concatenate([truth, jnp.zeros((8, 96), F32)], axis=1)
    cuts = thirds(truth)
    lines = [cut[:, 256 * j : 256 * j + 256] for j in range(6) for cut in cuts]
    split = dot_t(jnp.concatenate(lines, axis=0).astype(BF16), weave)
    even, odd = [], []
    for j in range(6):
        one = split[24 * j : 24 * j + 8] + split[24 * j + 8 : 24 * j + 16]
        one = one + split[24 * j + 16 : 24 * j + 24]
        even.append(one[:, :LANES])
        odd.append(one[:, LANES:])
    truth_eo = jnp.concatenate(
        [jnp.concatenate(even, axis=1)[:ROWS], jnp.concatenate(odd, axis=1)[:ROWS]], axis=0
    )[:, :HALF]

    for k in range(1, n_band):
        peer = band_peer(-k)
        arrive(inbox.at[peer], s_a.at[k], r_a.at[peer], (g, peer))

    left_id = iota((32, LANES), 0)
    left_row = (left_id % 4).astype(F32)
    with_obs = (left_id // 4) % 2 == 1
    left_coef = jnp.zeros((32, LANES), F32)
    for scale in range(4):
        left_coef = jnp.where(left_id // 8 == scale, coefs[scale][:, :LANES], left_coef)
    lane_cell = iota((LANES, LANES), 0).astype(F32)
    hist[...] = jnp.zeros_like(hist)

    def hist_step(it, carry):
        lefts, rights = [], []
        for u in range(2):
            fields = inbox[2 * it + u]
            for slot in range(CAP):
                row = fields[slot : slot + 1]
                lon = fields[CAP + slot : CAP + slot + 1]
                seen_value = fields[2 * CAP + slot : 2 * CAP + slot + 1]
                alive = fields[3 * CAP + slot : 3 * CAP + slot + 1]
                slab = jnp.floor((lon + 0.5) * (1.0 / CELL))
                cell = lon - CELL * slab
                gap = left_row - row
                factor = jnp.where(with_obs, alive * seen_value, alive)
                left = factor * jnp.exp(gap * gap * left_coef)
                lefts.append(
                    jnp.concatenate(
                        [jnp.where(slab == float(h), left, 0.0) for h in range(SLABS)], axis=0
                    ).astype(BF16)
                )
                rights.append(jnp.where(lane_cell == cell, 1.0, 0.0).astype(BF16))
        hist[...] += dot_t(jnp.concatenate(lefts, axis=1), jnp.concatenate(rights, axis=1))
        return carry

    lax.fori_loop(0, n_band // 2, hist_step, 0)

    cuts = thirds(hist[...])
    for scale in range(4):
        lines = []
        for j in range(6):
            now, before = (2 * j) * 32 + 8 * scale, ((2 * j - 1) % SLABS) * 32 + 8 * scale
            for cut in cuts:
                lines.append(jnp.concatenate([cut[now : now + 8], cut[before : before + 8]], axis=1))
        spread = dot(jnp.concatenate(lines, axis=0).astype(BF16), gauss[scale])
        even, odd = [], []
        for j in range(6):
            total = None
            for e in range(6):
                at = 24 * ((j - e) % 6)
                for third in range(3):
                    piece = spread[at + 8 * third : at + 8 * third + 8, 256 * e : 256 * e + 256]
                    total = piece if total is None else total + piece
            even.append(total[:, :CELL])
            odd.append(total[:, LANES : LANES + CELL])
        for p, pieces in enumerate((even, odd)):
            sums = jnp.concatenate(pieces, axis=1)
            density, signal = sums[:4], sums[4:]
            base_p = 1.0 + density
            first, second = density / base_p, signal / base_p
            for r in range(ROWS):
                at = 8 * p + 2 * scale
                feats32[r, at : at + 1, :] = first[r : r + 1]
                feats32[r, at + 1 : at + 2, :] = second[r : r + 1]
    for r in range(ROWS):
        own_f[r] = feats32[r].astype(BF16)

    reach = (-2, -1, 1, 2)
    for n, k in enumerate(reach):
        send(own_f, far_f.at[3 - n], s_f.at[n], r_f.at[3 - n], (g, band_peer(k)))

    def feature_taps(source, scale):
        values = source.astype(F32) if scale is None else source.astype(F32) * scale
        even, odd = values[:8], values[8:]
        return jnp.concatenate([later(odd, 1), even, odd, earlier(even, 1)], axis=0).astype(BF16)

    for r in range(ROWS):
        x_f[8 + r] = feature_taps(own_f[r], None)
    for n, k in enumerate(reach):
        arrive(far_f.at[n], s_f.at[n], r_f.at[n], (g, band_peer(k)))
    for n, k in enumerate(reach):
        there = as_scale(jnp.logical_and(b + k >= 0, b + k < n_band))
        start = (0, 4, 12, 16)[n]
        for r in range(ROWS):
            x_f[start + r] = feature_taps(far_f[n, r], there)

    def one_step(it, carry):
        window = x_f[pl.ds(3 * it, 5)].reshape(160, HALF)
        value = dot(wb_in[...], window)
        for i in range(3):
            row = 3 * it + i
            place = ROWS * b + row - 7
            inside = as_scale(jnp.logical_and(place >= 0, place < ROWS * n_band))
            here = value[64 * i : 64 * i + 64]
            pre_one[row] = here
            hidden = (here * sigmoid(here) * inside).astype(BF16)
            even, odd = hidden[:32], hidden[32:]
            x_one[row, 0:32] = later(odd, 1)
            x_one[row, 32:64] = even
            x_one[row, 64:96] = odd
            x_one[row, 96:128] = earlier(even, 1)
        return carry

    lax.fori_loop(0, 6, one_step, 0)

    def two_step(it, carry):
        value = dot(wb_down[...], x_one[pl.ds(4 * it, 6)].reshape(768, HALF))
        for m in range(2):
            row = 2 * it + m
            place = 2 * b + row - 3
            inside = as_scale(jnp.logical_and(place >= 0, place < 2 * n_band))
            here = value[32 * m : 32 * m + 32]
            pre_two[row] = here
            hidden = (here * sigmoid(here) * inside).astype(BF16)
            x_two[row, 0:32] = later(hidden, 2)
            x_two[row, 32:64] = hidden
            x_two[row, 64:96] = earlier(hidden, 2)
        return carry

    lax.fori_loop(0, 4, two_step, 0)

    for it in range(2):
        value = dot(wb_mid[...], x_two[2 * it : 2 * it + 6].reshape(576, HALF))
        for m in range(2):
            row = 2 * it + m
            place = 2 * b + row - 1
            inside = as_scale(jnp.logical_and(place >= 0, place < 2 * n_band))
            here = value[32 * m : 32 * m + 32]
            pre_three[row] = here
            hidden = (here * sigmoid(here) * inside).astype(BF16)
            before, after = later(hidden, 1), earlier(hidden, 1)
            for target in ((0,), (1, 2), (3, 4), (5,))[row]:
                x_three[target, 0:32] = before
                x_three[target, 32:64] = hidden
                x_three[target, 64:96] = hidden
                x_three[target, 96:128] = after

    def four_step(it, carry):
        value = dot(wb_up3[...], x_three[pl.ds(2 * it, 4)].reshape(512, HALF))
        value = value + dot(wb_up1[...], x_one[pl.ds(2 * it + 6, 4)].reshape(512, HALF))
        rows = pl.ds(pl.multiple_of(128 * it, 128), 128)
        pre_four[rows, :] = value
        h_four[rows, :] = (value * sigmoid(value)).astype(BF16)
        return carry

    lax.fori_loop(0, 2, four_step, 0)

    head = dot(wb_head, h_four[...])
    mean, raw = head[:8], head[8:]
    noise = 0.1 + jnp.maximum(raw, 0.0) + jnp.log1p(jnp.exp(-jnp.abs(raw)))
    z = (mean - truth_eo) / noise
    per_cell = noise * CELLS
    g_head = jnp.concatenate(
        [z / per_cell, (1.0 - z * z) / per_cell * sigmoid(raw)], axis=0
    ).astype(BF16)

    def taps_of(target_ref, row, even, odd):
        target_ref[row, 0:32] = later(odd, 1)
        target_ref[row, 32:64] = even
        target_ref[row, 64:96] = odd
        target_ref[row, 96:128] = earlier(even, 1)

    back = dot(db_head, g_head)
    for i in (0, 3, 1, 2):
        rows = slice(64 * i, 64 * i + 64)
        g_four[i] = (back[rows] * slope(pre_four[rows, :])).astype(BF16)
        if i == 0:
            send(g_four.at[0], far_four.at[1], s_4.at[0], r_4.at[1], (g, band_peer(-1)))
        if i == 3:
            send(g_four.at[3], far_four.at[0], s_4.at[1], r_4.at[0], (g, band_peer(1)))

    mean_pad = jnp.concatenate([mean, jnp.zeros((8, 48), F32)], axis=1)
    cuts = thirds(mean_pad)
    lines = []
    for j in range(6):
        for cut in cuts:
            block = cut[:, LANES * j : LANES * j + LANES]
            swapped = jnp.concatenate([block[4:], block[:4]], axis=0)
            lines.append(jnp.concatenate([block, swapped], axis=1))
    woven = dot(jnp.concatenate(lines, axis=0).astype(BF16), weave)
    joined = []
    for j in range(6):
        one = woven[24 * j : 24 * j + 8] + woven[24 * j + 8 : 24 * j + 16]
        joined.append(one + woven[24 * j + 16 : 24 * j + 24])
    mean_out[0] = jnp.concatenate(joined, axis=1)[:ROWS, :LON]

    g_all = g_four[...].reshape(256, HALF)
    cross = dot_t(g_head, h_four[...])
    head_grad = []
    for k in range(2):
        line = jnp.sum(jnp.where(matches, cross[8 * k : 8 * k + 8], 0.0), axis=0, keepdims=True)
        total = line[:, 0:32]
        for n in range(1, 8):
            total = total + line[:, 32 * n : 32 * n + 32]
        head_grad.append(total)
    head_grad = jnp.concatenate(head_grad, axis=0)
    up_grads = []
    for ref, source in ((big_a, x_three[...]), (big_b, x_one[6:12])):
        ref[...] = dot_t(g_all, source.reshape(768, HALF))
        for a in range(3):
            total = None
            for i in range(4):
                for p in range(2):
                    row, col = (2 * i + p) * 32, (i + a) * 128 + p * 32
                    piece = ref[row : row + 32, col : col + 96]
                    total = piece if total is None else total + piece
            up_grads.append(total)

    for i in range(4):
        taps_of(x_gfour, i + 1, g_four[i, 0:32], g_four[i, 32:64])
    above = as_scale(b > 0)
    below = as_scale(b < n_band - 1)
    for n, (k, row, there) in enumerate(((-1, 0, above), (1, 5, below))):
        arrive(far_four.at[n], s_4.at[n], r_4.at[n], (g, band_peer(k)))
        value = (far_four[n].astype(F32) * there).astype(BF16)
        taps_of(x_gfour, row, value[:32], value[32:])

    for it in range(2):
        value = dot(db_up[...], x_gfour[2 * it : 2 * it + 4].reshape(512, HALF))
        pooled = None
        for s in range(2):
            for p in range(2):
                at = 128 * s + 64 * p
                rounded = value[at : at + 64].astype(BF16)
                gj_one[2 * it + s, 32 * p : 32 * p + 32] = rounded[32:]
                upper = rounded[:32].astype(F32)
                pooled = upper if pooled is None else pooled + upper
        g_three[it] = (pooled * slope(pre_three[it + 1])).astype(BF16)
    send(g_three, far_three.at[1], s_3.at[0], r_3.at[1], (g, band_peer(-1)))
    send(g_three, far_three.at[0], s_3.at[1], r_3.at[0], (g, band_peer(1)))

    def spread_taps(target_ref, row, value, count):
        target_ref[row, 0:32] = later(value, count)
        target_ref[row, 32:64] = value
        target_ref[row, 64:96] = earlier(value, count)

    cross = dot_t(g_three[...].reshape(64, HALF), x_two[1:7].reshape(576, HALF))
    mid_grads = [
        cross[0:32, 192 * a : 192 * a + 96] + cross[32:64, 192 * a + 96 : 192 * a + 192]
        for a in range(3)
    ]
    for m in range(2):
        spread_taps(x_gthree, 2 + m, g_three[m], 2)
    for n, (k, row, there) in enumerate(((-1, 0, above), (1, 4, below))):
        arrive(far_three.at[n], s_3.at[n], r_3.at[n], (g, band_peer(k)))
        for m in range(2):
            value = (far_three[n, m].astype(F32) * there).astype(BF16)
            spread_taps(x_gthree, row + m, value, 2)
    value = dot(db_mid[...], x_gthree[...].reshape(576, HALF))
    for m in range(2):
        g_two[m] = (value[32 * m : 32 * m + 32] * slope(pre_two[3 + m])).astype(BF16)
    send(g_two.at[0], far_two.at[1], s_2.at[0], r_2.at[1], (g, band_peer(-1)))
    send(g_two.at[1], far_two.at[0], s_2.at[1], r_2.at[0], (g, band_peer(1)))

    cross = dot_t(g_two[...].reshape(64, HALF), x_one[6:12].reshape(768, HALF))
    down_grads = [
        cross[0:32, 128 * a : 128 * a + 128] + cross[32:64, 128 * a + 256 : 128 * a + 384]
        for a in range(4)
    ]
    for m in range(2):
        spread_taps(x_gtwo, 1 + m, g_two[m], 1)
    for n, (k, row, there) in enumerate(((-1, 0, above), (1, 3, below))):
        arrive(far_two.at[n], s_2.at[n], r_2.at[n], (g, band_peer(k)))
        value = (far_two[n].astype(F32) * there).astype(BF16)
        spread_taps(x_gtwo, row, value, 1)
    value = dot(db_down[...], x_gtwo[...].reshape(384, HALF))
    for i in range(4):
        total = value[64 * i : 64 * i + 64] + gj_one[i].astype(F32)
        g_one[i] = (total * slope(pre_one[7 + i])).astype(BF16)
    cross = dot_t(g_one[...].reshape(256, HALF), x_f[7:13].reshape(192, HALF))
    in_grads = []
    for a in range(3):
        total = None
        for i in range(4):
            for p in range(2):
                row, col = (2 * i + p) * 32, (i + a) * 32 + p * 8
                piece = cross[row : row + 32, col : col + 24]
                total = piece if total is None else total + piece
        in_grads.append(total)

    blocks = list(down_grads)
    pieces = [grad[:, 32 * t : 32 * t + 32] for grad in mid_grads for t in range(3)]
    for n in range(6):
        blocks.append(jnp.concatenate([up_grads[n], pieces[n]], axis=1))
    blank = jnp.zeros((32, 8), F32)
    blocks.append(jnp.concatenate(pieces[6:9] + [in_grads[0], blank], axis=1))
    head_block = jnp.concatenate([head_grad, jnp.zeros((30, 32), F32)], axis=0)
    blocks.append(
        jnp.concatenate(
            [in_grads[1], blank, in_grads[2], blank, head_block, jnp.zeros((32, 32), F32)], axis=1
        )
    )
    for n, block in enumerate(blocks):
        grads[4 * n : 4 * n + 4] = block.reshape(4, 8, LANES)

    for k in range(1, n_group):
        peer = group_peer(k)
        send(grads.at[pl.ds(chunk * peer, chunk)], got.at[g], s_g1.at[k], r_g1.at[g], (peer, b))
    got[g] = grads[pl.ds(chunk * g, chunk)]
    for k in range(1, n_group):
        peer = group_peer(-k)
        arrive(got.at[peer], s_g1.at[k], r_g1.at[peer], (peer, b))
    total = got[0]
    for n in range(1, n_group):
        total = total + got[n]
    part[b] = total
    for k in range(1, n_band):
        peer = band_peer(k)
        send(part.at[b], part.at[b], s_b.at[k], r_b.at[b], (g, peer))
    for k in range(1, n_band):
        peer = band_peer(-k)
        arrive(part.at[peer], s_b.at[k], r_b.at[peer], (g, peer))
    total = part[0]
    for n in range(1, n_band):
        total = total + part[n]
    full[pl.ds(chunk * g, chunk)] = total
    for k in range(1, n_group):
        peer = group_peer(k)
        mine = full.at[pl.ds(chunk * g, chunk)]
        send(mine, mine, s_g2.at[k], r_g2.at[g], (peer, b))
    for k in range(1, n_group):
        peer = group_peer(-k)
        arrive(full.at[pl.ds(chunk * peer, chunk)], s_g2.at[k], r_g2.at[peer], (peer, b))

    def final(n):
        return full[4 * n : 4 * n + 4].reshape(32, LANES)

    last = [final(n) for n in range(12)]
    for a in range(4):
        for t in range(4):
            down_out[a, t] = last[a][:, 32 * t : 32 * t + 32]
    pieces = [last[4 + n][:, 96:128] for n in range(6)]
    pieces += [last[10][:, 32 * t : 32 * t + 32] for t in range(3)]
    wholes = (last[10][:, 96:120], last[11][:, 0:24], last[11][:, 32:56])
    for a in range(3):
        for t in range(3):
            up_out[a, t] = jnp.concatenate(
                [last[4 + a][:, 32 * t : 32 * t + 32], last[7 + a][:, 32 * t : 32 * t + 32]], axis=1
            )
            mid_out[a, t] = pieces[3 * a + t]
            in_out[a, t] = wholes[a][:, 8 * t : 8 * t + 8]
    head_out[...] = last[11][0:2, 64:96]
    for copy in sent:
        copy.wait_send()


def local(
    station_rows,
    station_lons,
    station_obs,
    station_live,
    block_band,
    truth_field,
    length_scales,
    w_in,
    w_down,
    w_mid,
    w_up,
    w_head,
):
    n_group, n_band = lax.axis_size("group"), lax.axis_size("band")
    vmem = pl.BlockSpec(memory_space=pltpu.VMEM)
    smem = pl.BlockSpec(memory_space=pltpu.SMEM)
    dma = pltpu.SemaphoreType.DMA

    def space(dtype, *shape):
        return pltpu.VMEM(shape, dtype)

    outs = (truth_field, w_in, w_down, w_mid, w_up, w_head)
    return pl.pallas_call(
        functools.partial(step_kernel, n_group, n_band),
        out_shape=[jax.ShapeDtypeStruct(out.shape, F32) for out in outs],
        in_specs=[vmem] * 10 + [smem] * 2,
        out_specs=[vmem] * 6,
        scratch_shapes=[
            space(F32, 4, n_band * CAP, LANES),
            space(F32, n_band, 4 * CAP, LANES),
            space(F32, n_band, 4 * CAP, LANES),
            space(F32, 32 * SLABS, LANES),
            space(BF16, 4, 2 * LANES, 6 * 2 * LANES),
            space(F32, ROWS, 16, HALF),
            space(BF16, ROWS, 16, HALF),
            space(BF16, 4, ROWS, 16, HALF),
            space(BF16, 20, 32, HALF),
            space(BF16, 18, 128, HALF),
            space(F32, 18, 64, HALF),
            space(BF16, 8, 96, HALF),
            space(F32, 8, 32, HALF),
            space(F32, 4, 32, HALF),
            space(BF16, 6, 128, HALF),
            space(F32, 256, HALF),
            space(BF16, 256, HALF),
            space(BF16, 4, 64, HALF),
            space(BF16, 2, 64, HALF),
            space(BF16, 6, 128, HALF),
            space(F32, 256, 768),
            space(F32, 256, 768),
            space(BF16, 4, 64, HALF),
            space(BF16, 2, 32, HALF),
            space(BF16, 2, 2, 32, HALF),
            space(BF16, 6, 96, HALF),
            space(BF16, 2, 32, HALF),
            space(BF16, 2, 32, HALF),
            space(BF16, 4, 96, HALF),
            space(BF16, 4, 64, HALF),
            space(BF16, 192, 160),
            space(BF16, 64, 768),
            space(BF16, 64, 576),
            space(BF16, 128, 512),
            space(BF16, 128, 512),
            space(BF16, 256, 512),
            space(BF16, 64, 576),
            space(BF16, 256, 384),
            space(F32, 48, 8, LANES),
            space(F32, n_group, 48 // n_group, 8, LANES),
            space(F32, n_band, 48 // n_group, 8, LANES),
            space(F32, 48, 8, LANES),
            dma((n_band,)),
            dma((n_band,)),
            dma((4,)),
            dma((4,)),
            dma((2,)),
            dma((2,)),
            dma((2,)),
            dma((2,)),
            dma((2,)),
            dma((2,)),
            dma((n_group,)),
            dma((n_group,)),
            dma((n_band,)),
            dma((n_band,)),
            dma((n_group,)),
            dma((n_group,)),
        ],
        compiler_params=pltpu.CompilerParams(
            collective_id=0, has_side_effects=True, vmem_limit_bytes=VMEM_LIMIT
        ),
    )(
        station_rows,
        station_lons,
        station_obs,
        station_live,
        truth_field,
        w_in,
        w_down,
        w_mid,
        w_up,
        w_head,
        block_band,
        length_scales,
    )


def solution(mesh):
    spread = P("group", "band", None)
    return jax.shard_map(
        local,
        mesh=mesh,
        in_specs=(spread,) * 6 + (P(),) * 6,
        out_specs=(spread,) + (P(),) * 5,
        check_vma=False,
    )
```

```python
import functools

import jax
import jax.numpy as jnp
from jax import lax
from jax.experimental import pallas as pl
from jax.experimental.pallas import tpu as pltpu
from jax.sharding import PartitionSpec as P

MESH = pl.DeviceIdType.MESH
F32 = jnp.float32
BF16 = jnp.bfloat16
PHASES = (((1, 0), (3, -1)), ((0, 1), (2, 0)))
ROWS = 4
LON = 1440
HALF = 720
NBLK = 24
CAP = 3
LANES = 128
CELL = 120
SLABS = 12
CELLS = 92160.0
VMEM_LIMIT = 56 * 1024 * 1024


def dot(first, second):
    return lax.dot_general(first, second, (((1,), (0,)), ((), ())), preferred_element_type=F32)


def dot_t(first, second):
    return lax.dot_general(first, second, (((1,), (1,)), ((), ())), preferred_element_type=F32)


def iota(shape, dim):
    return lax.broadcasted_iota(jnp.int32, shape, dim)


def eye(size):
    return (iota((size, size), 0) == iota((size, size), 1)).astype(F32).astype(BF16)


def later(values, count):
    width = values.shape[-1]
    return jnp.concatenate([values[:, width - count :], values[:, : width - count]], axis=1)


def earlier(values, count):
    return jnp.concatenate([values[:, count:], values[:, :count]], axis=1)


def thirds(values):
    high = values.astype(BF16).astype(F32)
    rest = values - high
    middle = rest.astype(BF16).astype(F32)
    return high, middle, rest - middle


def sigmoid(values):
    return 1.0 / (1.0 + jnp.exp(-values))


def slope(values):
    squash = sigmoid(values)
    return squash * (1.0 + values * (1.0 - squash))


def as_scale(flag):
    return flag.astype(jnp.int32).astype(F32)


def step_kernel(
    n_group,
    n_band,
    rows_ref,
    lons_ref,
    obs_ref,
    live_ref,
    truth_ref,
    w_in,
    w_down,
    w_mid,
    w_up,
    w_head,
    band_ref,
    ell_ref,
    mean_out,
    early_out,
    late_out,
    in_out,
    picked,
    outbox,
    inbox,
    hist,
    gauss,
    feats32,
    own_f,
    far_f,
    x_f,
    x_one,
    pre_one,
    x_two,
    pre_two,
    pre_three,
    x_three,
    pre_four,
    h_four,
    g_four,
    edge_out,
    edge_in,
    x_gfour,
    big_a,
    big_b,
    gj_one,
    g_three,
    far_three,
    x_gthree,
    g_two,
    x_gtwo,
    g_one,
    wb_in,
    wb_down,
    wb_mid,
    wb_up3,
    wb_up1,
    db_up,
    db_mid,
    db_down,
    early,
    early_got,
    early_part,
    early_full,
    late,
    late_got,
    late_part,
    late_full,
    in_got,
    in_part,
    s_a,
    r_a,
    s_f,
    r_f,
    s_t,
    r_t,
    s_3,
    r_3,
    s_e1,
    r_e1,
    s_e2,
    r_e2,
    s_e3,
    r_e3,
    s_l1,
    r_l1,
    s_l2,
    r_l2,
    s_l3,
    r_l3,
    s_i1,
    r_i1,
    s_i2,
    r_i2,
):
    g = lax.axis_index("group")
    b = lax.axis_index("band")
    barrier = pltpu.get_barrier_semaphore()
    for k in range(1, n_group):
        pl.semaphore_signal(
            barrier, inc=1, device_id=(lax.rem(g + k, n_group), b), device_id_type=MESH
        )
    for k in range(1, n_band):
        pl.semaphore_signal(
            barrier, inc=1, device_id=(g, lax.rem(b + k, n_band)), device_id_type=MESH
        )

    def band_peer(k):
        return lax.rem(b + n_band + k, n_band)

    def group_peer(k):
        return lax.rem(g + n_group + k, n_group)

    sent = []

    def send(source, target, send_sem, recv_sem, device):
        copy = pltpu.make_async_remote_copy(
            src_ref=source,
            dst_ref=target,
            send_sem=send_sem,
            recv_sem=recv_sem,
            device_id=device,
            device_id_type=MESH,
        )
        copy.start()
        sent.append(copy)

    def arrive(target, send_sem, recv_sem, device):
        pltpu.make_async_remote_copy(
            src_ref=target,
            dst_ref=target,
            send_sem=send_sem,
            recv_sem=recv_sem,
            device_id=device,
            device_id_type=MESH,
        ).wait_recv()

    slot_rows = iota((n_band * CAP, LANES), 0)
    slot_band, slot_place = slot_rows // CAP, slot_rows % CAP
    seen = jnp.zeros((n_band * CAP, LANES), jnp.int32)
    chosen = [jnp.zeros((n_band * CAP, LANES), F32) for _ in range(4)]
    for block in range(NBLK):
        mine = slot_band == band_ref[0, 0, block]
        here = jnp.logical_and(mine, seen == slot_place)
        fields = (
            rows_ref[0, block : block + 1, :].astype(F32),
            lons_ref[0, block : block + 1, :].astype(F32),
            obs_ref[0, block : block + 1, :],
            live_ref[0, block : block + 1, :].astype(F32),
        )
        chosen = [jnp.where(here, new, old) for new, old in zip(fields, chosen)]
        seen = seen + mine.astype(jnp.int32)
    for field in range(4):
        picked[field] = chosen[field]
    for q in range(n_band):
        for field in range(4):
            outbox[q, CAP * field : CAP * field + CAP, :] = picked[
                field, CAP * q : CAP * q + CAP, :
            ]

    edge_out[0] = truth_ref[0, 0:1, :]
    edge_out[1] = truth_ref[0, ROWS - 1 : ROWS, :]
    pl.semaphore_wait(barrier, n_group + n_band - 2)
    for k in range(1, n_band):
        peer = band_peer(k)
        send(outbox.at[peer], inbox.at[b], s_a.at[k], r_a.at[b], (g, peer))
    send(edge_out.at[0], edge_in.at[1], s_t.at[0], r_t.at[1], (g, band_peer(-1)))
    send(edge_out.at[1], edge_in.at[0], s_t.at[1], r_t.at[0], (g, band_peer(1)))
    inbox[b] = outbox[b]

    wide = (2 * LANES, 2 * LANES)
    row_id, col_id = iota(wide, 0), iota(wide, 1)
    base = (
        2 * (col_id % LANES) + col_id // LANES - row_id % LANES + CELL * (row_id // LANES)
    ).astype(F32)
    coefs = []
    for scale in range(4):
        ell = jnp.full((1, 2 * LANES), ell_ref[scale], F32)
        coefs.append(-0.5 / (ell * ell))

    def gauss_step(e, carry):
        gap = jnp.abs(base + (2 * CELL * e).astype(F32))
        gap = jnp.minimum(gap, LON - gap)
        square = gap * gap
        cols = pl.ds(pl.multiple_of(e * 2 * LANES, 2 * LANES), 2 * LANES)
        for scale in range(4):
            gauss[scale, :, cols] = jnp.exp(square * coefs[scale]).astype(BF16)
        return carry

    lax.fori_loop(0, SLABS // 2, gauss_step, 0)

    for ref in (wb_in, wb_down, wb_mid, wb_up3, wb_up1, db_up, db_mid, db_down):
        ref[...] = jnp.zeros_like(ref)
    turned_in = dot_t(eye(32), w_in[...].astype(F32).reshape(72, 32).astype(BF16)).astype(BF16)
    turned_up = dot_t(eye(64), w_up[...].reshape(288, 64)).astype(BF16)
    turned_mid = dot_t(eye(32), w_mid[...].reshape(288, 32)).astype(BF16)
    turned_down = dot_t(eye(32), w_down[...].reshape(512, 32)).astype(BF16)
    for a in range(3):
        for t in range(3):
            at = (a * 3 + t) * 8
            block = turned_in[:, at : at + 8]
            for i in range(3):
                for p in range(2):
                    row, col = (2 * i + p) * 32, (i + a) * 32 + (t + p) * 8
                    wb_in[row : row + 32, col : col + 8] = block
            upper, lower = w_up[a, t, :, :32], w_up[a, t, :, 32:]
            at = ((2 - a) * 3 + 2 - t) * 32
            for i in range(2):
                for p in range(2):
                    row, col = (2 * i + p) * 32, (i + a) * 128 + (t + p) * 32
                    wb_up3[row : row + 32, col : col + 32] = upper
                    wb_up1[row : row + 32, col : col + 32] = lower
                    db_up[2 * row : 2 * row + 64, col : col + 32] = turned_up[:, at : at + 32]
                row, col = i * 32, (i + 2 * a) * 96 + t * 32
                wb_mid[row : row + 32, col : col + 32] = w_mid[a, t]
                db_mid[row : row + 32, col : col + 32] = turned_mid[:, at : at + 32]
    for a in range(4):
        for t in range(4):
            for m in range(2):
                col = (2 * m + a) * 128 + t * 32
                wb_down[m * 32 : m * 32 + 32, col : col + 32] = w_down[a, t]
    for m in range(2):
        for s in range(2):
            for p in range(2):
                row = ((2 * m + s) * 2 + p) * 32
                for a, up_down in PHASES[s]:
                    for t, left_right in PHASES[p]:
                        col = (m + up_down + 1) * 96 + (left_right + 1) * 32
                        at = (a * 4 + t) * 32
                        db_down[row : row + 32, col : col + 32] = turned_down[:, at : at + 32]
    head_row, head_col = iota((16, 384), 0), iota((16, 384), 1)
    matches = (head_col // 32) == (head_row % 8) * 2 + head_row // 8
    own_match = jnp.logical_and(matches, jnp.logical_and(head_col >= 64, head_col < 320))
    parts = []
    for k in range(2):
        line = jnp.concatenate([w_head[k : k + 1, :].astype(F32)] * 12, axis=1)
        parts.append(jnp.where(matches, line, 0.0))
    wb_head = jnp.concatenate(parts, axis=0).astype(BF16)
    db_head = dot_t(eye(384), wb_head).astype(BF16)

    weave = (col_id == 2 * (row_id % LANES) + row_id // LANES).astype(F32).astype(BF16)

    for k in range(1, n_band):
        peer = band_peer(-k)
        arrive(inbox.at[peer], s_a.at[k], r_a.at[peer], (g, peer))

    left_id = iota((32, LANES), 0)
    left_row = (left_id % 4).astype(F32)
    with_obs = (left_id // 4) % 2 == 1
    left_coef = jnp.zeros((32, LANES), F32)
    for scale in range(4):
        left_coef = jnp.where(left_id // 8 == scale, coefs[scale][:, :LANES], left_coef)
    lane_cell = iota((LANES, LANES), 0).astype(F32)
    hist[...] = jnp.zeros_like(hist)

    def hist_step(it, carry):
        lefts, rights = [], []
        for u in range(2):
            fields = inbox[2 * it + u]
            for slot in range(CAP):
                row = fields[slot : slot + 1]
                lon = fields[CAP + slot : CAP + slot + 1]
                seen_value = fields[2 * CAP + slot : 2 * CAP + slot + 1]
                alive = fields[3 * CAP + slot : 3 * CAP + slot + 1]
                slab = jnp.floor((lon + 0.5) * (1.0 / CELL))
                cell = lon - CELL * slab
                gap = left_row - row
                factor = jnp.where(with_obs, alive * seen_value, alive)
                left = factor * jnp.exp(gap * gap * left_coef)
                lefts.append(
                    jnp.concatenate(
                        [jnp.where(slab == float(h), left, 0.0) for h in range(SLABS)], axis=0
                    ).astype(BF16)
                )
                rights.append(jnp.where(lane_cell == cell, 1.0, 0.0).astype(BF16))
        hist[...] += dot_t(jnp.concatenate(lefts, axis=1), jnp.concatenate(rights, axis=1))
        return carry

    lax.fori_loop(0, n_band // 2, hist_step, 0)

    cuts = thirds(hist[...])
    for scale in range(4):
        lines = []
        for j in range(6):
            now, before = (2 * j) * 32 + 8 * scale, ((2 * j - 1) % SLABS) * 32 + 8 * scale
            for cut in cuts:
                lines.append(jnp.concatenate([cut[now : now + 8], cut[before : before + 8]], axis=1))
        spread = dot(jnp.concatenate(lines, axis=0).astype(BF16), gauss[scale])
        even, odd = [], []
        for j in range(6):
            total = None
            for e in range(6):
                at = 24 * ((j - e) % 6)
                for third in range(3):
                    piece = spread[at + 8 * third : at + 8 * third + 8, 256 * e : 256 * e + 256]
                    total = piece if total is None else total + piece
            even.append(total[:, :CELL])
            odd.append(total[:, LANES : LANES + CELL])
        for p, pieces in enumerate((even, odd)):
            sums = jnp.concatenate(pieces, axis=1)
            density, signal = sums[:4], sums[4:]
            base_p = 1.0 + density
            first, second = density / base_p, signal / base_p
            for r in range(ROWS):
                at = 8 * p + 2 * scale
                feats32[r, at : at + 1, :] = first[r : r + 1]
                feats32[r, at + 1 : at + 2, :] = second[r : r + 1]
    for r in range(ROWS):
        own_f[r] = feats32[r].astype(BF16)

    reach = (-2, -1, 1, 2)
    for n, k in enumerate(reach):
        send(own_f, far_f.at[3 - n], s_f.at[n], r_f.at[3 - n], (g, band_peer(k)))

    def feature_taps(source, scale):
        values = source.astype(F32) if scale is None else source.astype(F32) * scale
        even, odd = values[:8], values[8:]
        return jnp.concatenate([later(odd, 1), even, odd, earlier(even, 1)], axis=0).astype(BF16)

    for r in range(ROWS):
        x_f[8 + r] = feature_taps(own_f[r], None)
    for n, k in enumerate((-1, 1)):
        arrive(edge_in.at[n], s_t.at[n], r_t.at[n], (g, band_peer(k)))
    truth = jnp.concatenate(
        [edge_in[0], truth_ref[0], edge_in[1], jnp.zeros((2, LON), F32)], axis=0
    )
    truth = jnp.concatenate([truth, jnp.zeros((8, 96), F32)], axis=1)
    cuts = thirds(truth)
    lines = [cut[:, 256 * j : 256 * j + 256] for j in range(6) for cut in cuts]
    split = dot_t(jnp.concatenate(lines, axis=0).astype(BF16), weave)
    even, odd = [], []
    for j in range(6):
        one = split[24 * j : 24 * j + 8] + split[24 * j + 8 : 24 * j + 16]
        one = one + split[24 * j + 16 : 24 * j + 24]
        even.append(one[:, :LANES])
        odd.append(one[:, LANES:])
    truth_eo = jnp.concatenate(
        [jnp.concatenate(even, axis=1), jnp.concatenate(odd, axis=1)], axis=0
    )[:, :HALF]

    for n, k in enumerate(reach):
        arrive(far_f.at[n], s_f.at[n], r_f.at[n], (g, band_peer(k)))
    for n, k in enumerate(reach):
        there = as_scale(jnp.logical_and(b + k >= 0, b + k < n_band))
        start = (0, 4, 12, 16)[n]
        for r in range(ROWS):
            x_f[start + r] = feature_taps(far_f[n, r], there)

    def one_step(it, carry):
        window = x_f[pl.ds(3 * it, 5)].reshape(160, HALF)
        value = dot(wb_in[...], window)
        for i in range(3):
            row = 3 * it + i
            place = ROWS * b + row - 7
            inside = as_scale(jnp.logical_and(place >= 0, place < ROWS * n_band))
            here = value[64 * i : 64 * i + 64]
            pre_one[row] = here
            hidden = (here * sigmoid(here) * inside).astype(BF16)
            even, odd = hidden[:32], hidden[32:]
            x_one[row, 0:32] = later(odd, 1)
            x_one[row, 32:64] = even
            x_one[row, 64:96] = odd
            x_one[row, 96:128] = earlier(even, 1)
        return carry

    lax.fori_loop(0, 6, one_step, 0)

    def two_step(it, carry):
        value = dot(wb_down[...], x_one[pl.ds(4 * it, 6)].reshape(768, HALF))
        for m in range(2):
            row = 2 * it + m
            place = 2 * b + row - 3
            inside = as_scale(jnp.logical_and(place >= 0, place < 2 * n_band))
            here = value[32 * m : 32 * m + 32]
            pre_two[row] = here
            hidden = (here * sigmoid(here) * inside).astype(BF16)
            x_two[row, 0:32] = later(hidden, 2)
            x_two[row, 32:64] = hidden
            x_two[row, 64:96] = earlier(hidden, 2)
        return carry

    lax.fori_loop(0, 4, two_step, 0)

    for it in range(2):
        value = dot(wb_mid[...], x_two[2 * it : 2 * it + 6].reshape(576, HALF))
        for m in range(2):
            row = 2 * it + m
            place = 2 * b + row - 1
            inside = as_scale(jnp.logical_and(place >= 0, place < 2 * n_band))
            here = value[32 * m : 32 * m + 32]
            pre_three[row] = here
            hidden = (here * sigmoid(here) * inside).astype(BF16)
            before, after = later(hidden, 1), earlier(hidden, 1)
            for target in (2 * row, 2 * row + 1):
                x_three[target, 0:32] = before
                x_three[target, 32:64] = hidden
                x_three[target, 64:96] = hidden
                x_three[target, 96:128] = after

    def four_step(it, carry):
        value = dot(wb_up3[...], x_three[pl.ds(2 * it, 4)].reshape(512, HALF))
        value = value + dot(wb_up1[...], x_one[pl.ds(2 * it + 5, 4)].reshape(512, HALF))
        rows = pl.ds(pl.multiple_of(128 * it, 128), 128)
        pre_four[rows, :] = value
        h_four[rows, :] = (value * sigmoid(value)).astype(BF16)
        return carry

    lax.fori_loop(0, 3, four_step, 0)

    head = dot(wb_head, h_four[...])
    mean, raw = head[:16], head[16:]
    noise = 0.1 + jnp.maximum(raw, 0.0) + jnp.log1p(jnp.exp(-jnp.abs(raw)))
    z = (mean - truth_eo) / noise
    per_cell = noise * CELLS
    head_place = iota((16, HALF), 0) % 8 + ROWS * b - 1
    on_grid = jnp.logical_and(head_place >= 0, head_place < ROWS * n_band)
    on_grid = jnp.logical_and(on_grid, iota((16, HALF), 0) % 8 < 6)
    g_mean = jnp.where(on_grid, z / per_cell, 0.0)
    g_raw = jnp.where(on_grid, (1.0 - z * z) / per_cell * sigmoid(raw), 0.0)
    g_head = jnp.concatenate([g_mean, g_raw], axis=0).astype(BF16)

    def taps_of(target_ref, row, even, odd):
        target_ref[row, 0:32] = later(odd, 1)
        target_ref[row, 32:64] = even
        target_ref[row, 64:96] = odd
        target_ref[row, 96:128] = earlier(even, 1)

    back = dot(db_head, g_head)
    for i in range(6):
        rows = slice(64 * i, 64 * i + 64)
        value = (back[rows] * slope(pre_four[rows, :])).astype(BF16)
        g_four[i] = value
        taps_of(x_gfour, i, value[:32], value[32:])

    for it in range(2):
        value = dot(db_up[...], x_gfour[2 * it : 2 * it + 4].reshape(512, HALF))
        pooled = None
        for s in range(2):
            for p in range(2):
                at = 128 * s + 64 * p
                rounded = value[at : at + 64].astype(BF16)
                gj_one[2 * it + s, 32 * p : 32 * p + 32] = rounded[32:]
                upper = rounded[:32].astype(F32)
                pooled = upper if pooled is None else pooled + upper
        g_three[it] = (pooled * slope(pre_three[it + 1])).astype(BF16)
    send(g_three, far_three.at[2], s_3.at[0], r_3.at[2], (g, band_peer(-1)))
    send(g_three, far_three.at[1], s_3.at[1], r_3.at[1], (g, band_peer(1)))
    send(g_three.at[0], far_three.at[3, 0], s_3.at[2], r_3.at[3], (g, band_peer(-2)))
    send(g_three.at[1], far_three.at[0, 1], s_3.at[3], r_3.at[0], (g, band_peer(2)))

    cuts = thirds(jnp.concatenate([mean, jnp.zeros((16, 48), F32)], axis=1))
    lines = []
    for j in range(6):
        for cut in cuts:
            block = cut[:, LANES * j : LANES * j + LANES]
            lines.append(jnp.concatenate([block[:8], block[8:]], axis=1))
    woven = dot(jnp.concatenate(lines, axis=0).astype(BF16), weave)
    joined = []
    for j in range(6):
        one = woven[24 * j : 24 * j + 8] + woven[24 * j + 8 : 24 * j + 16]
        joined.append(one + woven[24 * j + 16 : 24 * j + 24])
    mean_out[0] = jnp.concatenate(joined, axis=1)[1 : 1 + ROWS, :LON]

    g_all = g_four[1:5].reshape(256, HALF)
    cross = dot_t(g_head, h_four[...])
    head_grad = []
    for k in range(2):
        line = jnp.sum(
            jnp.where(own_match, cross[16 * k : 16 * k + 16], 0.0), axis=0, keepdims=True
        )
        total = line[:, 0:32]
        for n in range(1, 12):
            total = total + line[:, 32 * n : 32 * n + 32]
        head_grad.append(total)
    head_grad = jnp.concatenate(head_grad + [jnp.zeros((30, 32), F32)], axis=0)
    up_grads = []
    for ref, source in ((big_a, x_three[1:7]), (big_b, x_one[6:12])):
        ref[...] = dot_t(g_all, source.reshape(768, HALF))
        for a in range(3):
            total = None
            for i in range(4):
                for p in range(2):
                    row, col = (2 * i + p) * 32, (i + a) * 128 + p * 32
                    piece = ref[row : row + 32, col : col + 96]
                    total = piece if total is None else total + piece
            up_grads.append(total)
    cross = dot_t(g_three[...].reshape(64, HALF), x_two[1:7].reshape(576, HALF))
    mid_grads = [
        cross[0:32, 192 * a : 192 * a + 96] + cross[32:64, 192 * a + 96 : 192 * a + 192]
        for a in range(3)
    ]
    pieces = [grad[:, 32 * t : 32 * t + 32] for grad in mid_grads for t in range(3)]
    for n in range(6):
        block = jnp.concatenate([up_grads[n], pieces[n]], axis=1)
        early[4 * n : 4 * n + 4] = block.reshape(4, 8, LANES)
    early[24:28] = jnp.concatenate(pieces[6:9] + [head_grad], axis=1).reshape(4, 8, LANES)
    early[28:32] = jnp.zeros((4, 8, LANES), F32)

    def scatter_group(source, size, target, send_sems, recv_sems):
        for k in range(1, n_group):
            peer = group_peer(k)
            send(
                source.at[pl.ds(size * peer, size)],
                target.at[g],
                send_sems.at[k],
                recv_sems.at[g],
                (peer, b),
            )
        target[g] = source[pl.ds(size * g, size)]

    def spread_group(target, send_sems, recv_sems):
        for k in range(1, n_group):
            send(target.at[g], target.at[g], send_sems.at[k], recv_sems.at[g], (group_peer(k), b))

    def spread_band(target, send_sems, recv_sems):
        for k in range(1, n_band):
            send(target.at[b], target.at[b], send_sems.at[k], recv_sems.at[b], (g, band_peer(k)))

    def await_group(target, send_sems, recv_sems):
        for k in range(1, n_group):
            peer = group_peer(-k)
            arrive(target.at[peer], send_sems.at[k], recv_sems.at[peer], (peer, b))

    def await_band(target, send_sems, recv_sems):
        for k in range(1, n_band):
            peer = band_peer(-k)
            arrive(target.at[peer], send_sems.at[k], recv_sems.at[peer], (g, peer))

    def added(ref, count):
        total = ref[0]
        for n in range(1, count):
            total = total + ref[n]
        return total

    early_size, late_size = 32 // n_group, 16 // n_group
    scatter_group(early, early_size, early_got, s_e1, r_e1)

    def spread_taps(target_ref, row, value, count):
        target_ref[row, 0:32] = later(value, count)
        target_ref[row, 32:64] = value
        target_ref[row, 64:96] = earlier(value, count)

    for m in range(2):
        spread_taps(x_gthree, 3 + m, g_three[m], 2)
    for n, k in ((1, -1), (2, 1), (0, -2), (3, 2)):
        target = (far_three.at[0, 1], far_three.at[1], far_three.at[2], far_three.at[3, 0])[n]
        arrive(target, s_3.at[n], r_3.at[n], (g, band_peer(k)))
        there = as_scale(jnp.logical_and(b + k >= 0, b + k < n_band))
        for m in ((1,), (0, 1), (0, 1), (0,))[n]:
            value = (far_three[n, m].astype(F32) * there).astype(BF16)
            spread_taps(x_gthree, 3 + 2 * k + m, value, 2)
    for it in range(2):
        value = dot(db_mid[...], x_gthree[2 * it : 2 * it + 6].reshape(576, HALF))
        for m in range(2):
            row = 2 * it + m
            place = 2 * b + row - 1
            inside = as_scale(jnp.logical_and(place >= 0, place < 2 * n_band))
            here = value[32 * m : 32 * m + 32] * slope(pre_two[2 + row]) * inside
            g_two[row] = here.astype(BF16)
    cross = dot_t(g_two[1:3].reshape(64, HALF), x_one[6:12].reshape(768, HALF))
    for a in range(4):
        block = (
            cross[0:32, 128 * a : 128 * a + 128] + cross[32:64, 128 * a + 256 : 128 * a + 384]
        )
        late[4 * a : 4 * a + 4] = block.reshape(4, 8, LANES)
    scatter_group(late, late_size, late_got, s_l1, r_l1)
    for m in range(4):
        spread_taps(x_gtwo, m, g_two[m], 1)
    value = dot(db_down[...], x_gtwo[...].reshape(384, HALF))
    for i in range(4):
        total = value[64 * i : 64 * i + 64] + gj_one[i].astype(F32)
        g_one[i] = (total * slope(pre_one[7 + i])).astype(BF16)
    cross = dot_t(x_f[7:13].reshape(192, HALF), g_one[...].reshape(256, HALF))
    in_grads = []
    for a in range(3):
        total = None
        for i in range(4):
            for p in range(2):
                row, col = (i + a) * 32 + p * 8, (2 * i + p) * 32
                piece = cross[row : row + 24, col : col + 32]
                total = piece if total is None else total + piece
        in_grads.append(total)
    in_got[g] = jnp.concatenate(in_grads + [jnp.zeros((24, 32), F32)], axis=1)
    spread_group(in_got, s_i1, r_i1)
    await_group(early_got, s_e1, r_e1)
    early_part[b] = added(early_got, n_group)
    spread_band(early_part, s_e2, r_e2)
    await_group(late_got, s_l1, r_l1)
    late_part[b] = added(late_got, n_group)
    spread_band(late_part, s_l2, r_l2)
    await_group(in_got, s_i1, r_i1)
    in_part[b] = added(in_got, n_group)
    spread_band(in_part, s_i2, r_i2)
    await_band(early_part, s_e2, r_e2)
    early_full[g] = added(early_part, n_band)
    spread_group(early_full, s_e3, r_e3)
    await_band(late_part, s_l2, r_l2)
    late_full[g] = added(late_part, n_band)
    spread_group(late_full, s_l3, r_l3)
    await_band(in_part, s_i2, r_i2)
    in_out[...] = added(in_part, n_band)
    await_group(early_full, s_e3, r_e3)
    early_out[...] = early_full[...].reshape(32, 8, LANES)
    await_group(late_full, s_l3, r_l3)
    late_out[...] = late_full[...].reshape(16, 8, LANES)
    for copy in sent:
        copy.wait_send()


def outputs_kernel(
    mean_ref, early_ref, late_ref, in_ref, mean_out, in_out, down_out, mid_out, up_out, head_out
):
    mean_out[...] = mean_ref[...]
    early = [early_ref[4 * n : 4 * n + 4].reshape(32, LANES) for n in range(7)]
    pieces = [early[n][:, 96:128] for n in range(6)]
    pieces += [early[6][:, 32 * t : 32 * t + 32] for t in range(3)]
    for a in range(4):
        block = late_ref[4 * a : 4 * a + 4].reshape(32, LANES)
        for t in range(4):
            down_out[a, t] = block[:, 32 * t : 32 * t + 32]
    for a in range(3):
        for t in range(3):
            up_out[a, t] = jnp.concatenate(
                [early[a][:, 32 * t : 32 * t + 32], early[3 + a][:, 32 * t : 32 * t + 32]], axis=1
            )
            mid_out[a, t] = pieces[3 * a + t]
            in_out[a, t] = in_ref[8 * t : 8 * t + 8, 32 * a : 32 * a + 32]
    head_out[...] = early[6][0:2, 96:128]


def local(
    station_rows,
    station_lons,
    station_obs,
    station_live,
    block_band,
    truth_field,
    length_scales,
    w_in,
    w_down,
    w_mid,
    w_up,
    w_head,
):
    n_group, n_band = lax.axis_size("group"), lax.axis_size("band")
    vmem = pl.BlockSpec(memory_space=pltpu.VMEM)
    smem = pl.BlockSpec(memory_space=pltpu.SMEM)
    dma = pltpu.SemaphoreType.DMA

    def space(dtype, *shape):
        return pltpu.VMEM(shape, dtype)

    w_in = jnp.transpose(w_in, (0, 1, 3, 2))
    early_size, late_size = 32 // n_group, 16 // n_group
    raw = (truth_field.shape, (32, 8, LANES), (16, 8, LANES), (24, LANES))
    summed = pl.pallas_call(
        functools.partial(step_kernel, n_group, n_band),
        out_shape=[jax.ShapeDtypeStruct(shape, F32) for shape in raw],
        in_specs=[vmem] * 10 + [smem] * 2,
        out_specs=[vmem] * 4,
        scratch_shapes=[
            space(F32, 4, n_band * CAP, LANES),
            space(F32, n_band, 4 * CAP, LANES),
            space(F32, n_band, 4 * CAP, LANES),
            space(F32, 32 * SLABS, LANES),
            space(BF16, 4, 2 * LANES, 6 * 2 * LANES),
            space(F32, ROWS, 16, HALF),
            space(BF16, ROWS, 16, HALF),
            space(BF16, 4, ROWS, 16, HALF),
            space(BF16, 20, 32, HALF),
            space(BF16, 18, 128, HALF),
            space(F32, 18, 64, HALF),
            space(BF16, 8, 96, HALF),
            space(F32, 8, 32, HALF),
            space(F32, 4, 32, HALF),
            space(BF16, 8, 128, HALF),
            space(F32, 384, HALF),
            space(BF16, 384, HALF),
            space(BF16, 6, 64, HALF),
            space(F32, 2, 1, LON),
            space(F32, 2, 1, LON),
            space(BF16, 6, 128, HALF),
            space(F32, 256, 768),
            space(F32, 256, 768),
            space(BF16, 4, 64, HALF),
            space(BF16, 2, 32, HALF),
            space(BF16, 4, 2, 32, HALF),
            space(BF16, 8, 96, HALF),
            space(BF16, 4, 32, HALF),
            space(BF16, 4, 96, HALF),
            space(BF16, 4, 64, HALF),
            space(BF16, 192, 160),
            space(BF16, 64, 768),
            space(BF16, 64, 576),
            space(BF16, 128, 512),
            space(BF16, 128, 512),
            space(BF16, 256, 512),
            space(BF16, 64, 576),
            space(BF16, 256, 384),
            space(F32, 32, 8, LANES),
            space(F32, n_group, early_size, 8, LANES),
            space(F32, n_band, early_size, 8, LANES),
            space(F32, n_group, early_size, 8, LANES),
            space(F32, 16, 8, LANES),
            space(F32, n_group, late_size, 8, LANES),
            space(F32, n_band, late_size, 8, LANES),
            space(F32, n_group, late_size, 8, LANES),
            space(F32, n_group, 24, LANES),
            space(F32, n_band, 24, LANES),
            dma((n_band,)),
            dma((n_band,)),
            dma((4,)),
            dma((4,)),
            dma((2,)),
            dma((2,)),
            dma((4,)),
            dma((4,)),
        ]
        + [dma((count,)) for count in (n_group, n_band, n_group) * 2 for _ in range(2)]
        + [dma((count,)) for count in (n_group, n_band) for _ in range(2)],
        compiler_params=pltpu.CompilerParams(
            collective_id=0, has_side_effects=True, vmem_limit_bytes=VMEM_LIMIT
        ),
    )(
        station_rows,
        station_lons,
        station_obs,
        station_live,
        truth_field,
        w_in,
        w_down,
        w_mid,
        w_up,
        w_head,
        jnp.transpose(block_band, (0, 2, 1)),
        length_scales,
    )
    outs = (truth_field, w_in, w_down, w_mid, w_up, w_head)
    mean, grad_in, grad_down, grad_mid, grad_up, grad_head = pl.pallas_call(
        outputs_kernel,
        out_shape=[jax.ShapeDtypeStruct(out.shape, F32) for out in outs],
        in_specs=[vmem] * 4,
        out_specs=[vmem] * 6,
    )(*summed)
    return mean, jnp.transpose(grad_in, (0, 1, 3, 2)), grad_down, grad_mid, grad_up, grad_head


def solution(mesh):
    spread = P("group", "band", None)
    return jax.shard_map(
        local,
        mesh=mesh,
        in_specs=(spread,) * 6 + (P(),) * 6,
        out_specs=(spread,) + (P(),) * 5,
        check_vma=False,
    )
```

```python
import functools

import jax
import jax.numpy as jnp
from jax import lax
from jax.experimental import pallas as pl
from jax.experimental.pallas import tpu as pltpu
from jax.sharding import PartitionSpec as P

MESH = pl.DeviceIdType.MESH
F32 = jnp.float32
BF16 = jnp.bfloat16
PHASES = (((1, 0), (3, -1)), ((0, 1), (2, 0)))
ROWS = 4
LON = 1440
HALF = 720
NBLK = 24
CAP = 3
LANES = 128
CELL = 120
SLABS = 12
CELLS = 92160.0
VMEM_LIMIT = 56 * 1024 * 1024


def dot(first, second):
    return lax.dot_general(first, second, (((1,), (0,)), ((), ())), preferred_element_type=F32)


def dot_t(first, second):
    return lax.dot_general(first, second, (((1,), (1,)), ((), ())), preferred_element_type=F32)


def iota(shape, dim):
    return lax.broadcasted_iota(jnp.int32, shape, dim)


def eye(size):
    return (iota((size, size), 0) == iota((size, size), 1)).astype(F32).astype(BF16)


def later(values, count):
    width = values.shape[-1]
    return jnp.concatenate([values[:, width - count :], values[:, : width - count]], axis=1)


def earlier(values, count):
    return jnp.concatenate([values[:, count:], values[:, :count]], axis=1)


def thirds(values):
    high = values.astype(BF16).astype(F32)
    rest = values - high
    middle = rest.astype(BF16).astype(F32)
    return high, middle, rest - middle


def sigmoid(values):
    return 0.5 * jnp.tanh(0.5 * values) + 0.5


def slope(values):
    squash = sigmoid(values)
    return squash * (1.0 + values * (1.0 - squash))


def as_scale(flag):
    return flag.astype(jnp.int32).astype(F32)


def step_kernel(
    n_group,
    n_band,
    rows_far,
    lons_far,
    obs_far,
    live_far,
    truth_far,
    w_in_far,
    w_down_far,
    w_mid_far,
    w_up_far,
    w_head_far,
    band_ref,
    ell_ref,
    mean_out,
    early_out,
    late_out,
    in_out,
    rows_ref,
    lons_ref,
    obs_ref,
    live_ref,
    truth_ref,
    w_in,
    w_down,
    w_mid,
    w_up,
    w_head,
    s_in,
    picked,
    outbox,
    inbox,
    gauss,
    feats32,
    own_f,
    far_f,
    x_f,
    x_one,
    pre_one,
    x_two,
    pre_two,
    pre_three,
    x_three,
    pre_four,
    h_four,
    g_four,
    edge_out,
    edge_in,
    x_gfour,
    big_a,
    big_b,
    gj_one,
    g_three,
    far_three,
    x_gthree,
    g_two,
    x_gtwo,
    g_one,
    wb_in,
    wb_down,
    wb_mid,
    wb_up3,
    wb_up1,
    db_up,
    db_mid,
    db_down,
    early,
    early_got,
    early_part,
    early_full,
    late,
    late_got,
    late_part,
    late_full,
    in_got,
    in_part,
    s_a,
    r_a,
    s_f,
    r_f,
    s_t,
    r_t,
    s_3,
    r_3,
    s_e1,
    r_e1,
    s_e2,
    r_e2,
    s_e3,
    r_e3,
    s_l1,
    r_l1,
    s_l2,
    r_l2,
    s_l3,
    r_l3,
    s_i1,
    r_i1,
    s_i2,
    r_i2,
):
    g = lax.axis_index("group")
    b = lax.axis_index("band")
    barrier = pltpu.get_barrier_semaphore()
    for k in range(1, n_group):
        pl.semaphore_signal(
            barrier, inc=1, device_id=(lax.rem(g + k, n_group), b), device_id_type=MESH
        )
    for k in range(1, n_band):
        pl.semaphore_signal(
            barrier, inc=1, device_id=(g, lax.rem(b + k, n_band)), device_id_type=MESH
        )

    def band_peer(k):
        return lax.rem(b + n_band + k, n_band)

    def group_peer(k):
        return lax.rem(g + n_group + k, n_group)

    sent = []

    def send(source, target, send_sem, recv_sem, device):
        copy = pltpu.make_async_remote_copy(
            src_ref=source,
            dst_ref=target,
            send_sem=send_sem,
            recv_sem=recv_sem,
            device_id=device,
            device_id_type=MESH,
        )
        copy.start()
        sent.append(copy)

    def arrive(target, send_sem, recv_sem, device):
        pltpu.make_async_remote_copy(
            src_ref=target,
            dst_ref=target,
            send_sem=send_sem,
            recv_sem=recv_sem,
            device_id=device,
            device_id_type=MESH,
        ).wait_recv()

    fetches = []
    pairs = (
        (rows_far, rows_ref),
        (lons_far, lons_ref),
        (obs_far, obs_ref),
        (live_far, live_ref),
        (truth_far, truth_ref),
        (w_in_far, w_in),
        (w_down_far, w_down),
        (w_mid_far, w_mid),
        (w_up_far, w_up),
        (w_head_far, w_head),
    )
    for n, (source, target) in enumerate(pairs):
        fetch = pltpu.make_async_copy(source, target, s_in.at[n])
        fetch.start()
        fetches.append(fetch)
    for fetch in fetches[:5]:
        fetch.wait()
    slot_rows = iota((n_band * CAP, LANES), 0)
    slot_band, slot_place = slot_rows // CAP, slot_rows % CAP
    seen = jnp.zeros((n_band * CAP, LANES), jnp.int32)
    chosen = [jnp.zeros((n_band * CAP, LANES), F32) for _ in range(4)]
    for block in range(NBLK):
        mine = slot_band == band_ref[0, 0, block]
        here = jnp.logical_and(mine, seen == slot_place)
        fields = (
            rows_ref[0, block : block + 1, :].astype(F32),
            lons_ref[0, block : block + 1, :].astype(F32),
            obs_ref[0, block : block + 1, :],
            live_ref[0, block : block + 1, :].astype(F32),
        )
        chosen = [jnp.where(here, new, old) for new, old in zip(fields, chosen)]
        seen = seen + mine.astype(jnp.int32)
    for field in range(4):
        picked[field] = chosen[field]
    for q in range(n_band):
        for field in range(4):
            outbox[q, CAP * field : CAP * field + CAP, :] = picked[
                field, CAP * q : CAP * q + CAP, :
            ]

    edge_out[0] = truth_ref[0, 0:1, :]
    edge_out[1] = truth_ref[0, ROWS - 1 : ROWS, :]
    pl.semaphore_wait(barrier, n_group + n_band - 2)
    for k in range(1, n_band):
        peer = band_peer(k)
        send(outbox.at[peer], inbox.at[b], s_a.at[k], r_a.at[b], (g, peer))
    send(edge_out.at[0], edge_in.at[1], s_t.at[0], r_t.at[1], (g, band_peer(-1)))
    send(edge_out.at[1], edge_in.at[0], s_t.at[1], r_t.at[0], (g, band_peer(1)))
    inbox[b] = outbox[b]

    wide = (2 * LANES, 2 * LANES)
    row_id, col_id = iota(wide, 0), iota(wide, 1)
    base = (
        2 * (col_id % LANES) + col_id // LANES - row_id % LANES + CELL * (row_id // LANES)
    ).astype(F32)
    coefs = []
    for scale in range(4):
        ell = jnp.full((1, 2 * LANES), ell_ref[scale], F32)
        coefs.append(-0.5 / (ell * ell))

    def gauss_step(e, carry):
        gap = jnp.abs(base + (2 * CELL * e).astype(F32))
        gap = jnp.minimum(gap, LON - gap)
        square = gap * gap
        cols = pl.ds(pl.multiple_of(e * 2 * LANES, 2 * LANES), 2 * LANES)
        for scale in range(4):
            gauss[scale, :, cols] = jnp.exp(square * coefs[scale]).astype(BF16)
        return carry

    lax.fori_loop(0, SLABS // 2, gauss_step, 0)

    weave = (col_id == 2 * (row_id % LANES) + row_id // LANES).astype(F32).astype(BF16)

    left_id = iota((32, LANES), 0)
    left_row = (left_id % 4).astype(F32)
    with_obs = (left_id // 4) % 2 == 1
    left_coef = jnp.zeros((32, LANES), F32)
    for scale in range(4):
        left_coef = jnp.where(left_id // 8 == scale, coefs[scale][:, :LANES], left_coef)
    lane_cell = iota((LANES, LANES), 0).astype(F32)
    counted = None
    order = [0]
    for k in range(1, n_band // 2):
        order += [k, -k]
    order.append(n_band // 2)
    for quarter in range(4):
        lefts, rights = [], []
        for k in order[4 * quarter : 4 * quarter + 4]:
            peer = band_peer(-k)
            if k:
                arrive(inbox.at[peer], s_a.at[k % n_band], r_a.at[peer], (g, peer))
            fields = inbox[peer]
            for slot in range(CAP):
                row = fields[slot : slot + 1]
                lon = fields[CAP + slot : CAP + slot + 1]
                seen_value = fields[2 * CAP + slot : 2 * CAP + slot + 1]
                alive = fields[3 * CAP + slot : 3 * CAP + slot + 1]
                slab = jnp.floor((lon + 0.5) * (1.0 / CELL))
                cell = lon - CELL * slab
                gap = left_row - row
                factor = jnp.where(with_obs, alive * seen_value, alive)
                left = factor * jnp.exp(gap * gap * left_coef)
                lefts.append(
                    jnp.concatenate(
                        [jnp.where(slab == float(h), left, 0.0) for h in range(SLABS)], axis=0
                    ).astype(BF16)
                )
                rights.append(jnp.where(lane_cell == cell, 1.0, 0.0).astype(BF16))
        more = dot_t(jnp.concatenate(lefts, axis=1), jnp.concatenate(rights, axis=1))
        counted = more if counted is None else counted + more

    cuts = thirds(counted)
    for scale in range(4):
        lines = []
        for j in range(6):
            now, before = (2 * j) * 32 + 8 * scale, ((2 * j - 1) % SLABS) * 32 + 8 * scale
            for cut in cuts:
                lines.append(jnp.concatenate([cut[now : now + 8], cut[before : before + 8]], axis=1))
        spread = dot(jnp.concatenate(lines, axis=0).astype(BF16), gauss[scale])
        even, odd = [], []
        for j in range(6):
            total = None
            for e in range(6):
                at = 24 * ((j - e) % 6)
                for third in range(3):
                    piece = spread[at + 8 * third : at + 8 * third + 8, 256 * e : 256 * e + 256]
                    total = piece if total is None else total + piece
            even.append(total[:, :CELL])
            odd.append(total[:, LANES : LANES + CELL])
        for p, pieces in enumerate((even, odd)):
            sums = jnp.concatenate(pieces, axis=1)
            density, signal = sums[:4], sums[4:]
            base_p = 1.0 + density
            first, second = density / base_p, signal / base_p
            for r in range(ROWS):
                at = 8 * p + 2 * scale
                feats32[r, at : at + 1, :] = first[r : r + 1]
                feats32[r, at + 1 : at + 2, :] = second[r : r + 1]
    for r in range(ROWS):
        own_f[r] = feats32[r].astype(BF16)

    reach = (-2, -1, 1, 2)
    for n, k in enumerate(reach):
        send(own_f, far_f.at[3 - n], s_f.at[n], r_f.at[3 - n], (g, band_peer(k)))

    def feature_taps(source, scale):
        values = source.astype(F32) if scale is None else source.astype(F32) * scale
        even, odd = values[:8], values[8:]
        return jnp.concatenate([later(odd, 1), even, odd, earlier(even, 1)], axis=0).astype(BF16)

    for r in range(ROWS):
        x_f[8 + r] = feature_taps(own_f[r], None)
    for fetch in fetches[5:]:
        fetch.wait()
    for ref in (wb_in, wb_down, wb_mid, wb_up3, wb_up1, db_up, db_mid, db_down):
        ref[...] = jnp.zeros_like(ref)
    turned_in = dot_t(eye(32), w_in[...].astype(F32).reshape(72, 32).astype(BF16)).astype(BF16)
    turned_up = dot_t(eye(64), w_up[...].reshape(288, 64)).astype(BF16)
    turned_mid = dot_t(eye(32), w_mid[...].reshape(288, 32)).astype(BF16)
    turned_down = dot_t(eye(32), w_down[...].reshape(512, 32)).astype(BF16)
    for a in range(3):
        for t in range(3):
            at = (a * 3 + t) * 8
            block = turned_in[:, at : at + 8]
            for i in range(3):
                for p in range(2):
                    row, col = (2 * i + p) * 32, (i + a) * 32 + (t + p) * 8
                    wb_in[row : row + 32, col : col + 8] = block
            upper, lower = w_up[a, t, :, :32], w_up[a, t, :, 32:]
            at = ((2 - a) * 3 + 2 - t) * 32
            for i in range(2):
                for p in range(2):
                    row, col = (2 * i + p) * 32, (i + a) * 128 + (t + p) * 32
                    wb_up3[row : row + 32, col : col + 32] = upper
                    wb_up1[row : row + 32, col : col + 32] = lower
                    db_up[2 * row : 2 * row + 64, col : col + 32] = turned_up[:, at : at + 32]
                row, col = i * 32, (i + 2 * a) * 96 + t * 32
                wb_mid[row : row + 32, col : col + 32] = w_mid[a, t]
                db_mid[row : row + 32, col : col + 32] = turned_mid[:, at : at + 32]
    for a in range(4):
        for t in range(4):
            for m in range(2):
                col = (2 * m + a) * 128 + t * 32
                wb_down[m * 32 : m * 32 + 32, col : col + 32] = w_down[a, t]
    for m in range(2):
        for s in range(2):
            for p in range(2):
                row = ((2 * m + s) * 2 + p) * 32
                for a, up_down in PHASES[s]:
                    for t, left_right in PHASES[p]:
                        col = (m + up_down + 1) * 96 + (left_right + 1) * 32
                        at = (a * 4 + t) * 32
                        db_down[row : row + 32, col : col + 32] = turned_down[:, at : at + 32]
    head_row, head_col = iota((16, 384), 0), iota((16, 384), 1)
    matches = (head_col // 32) == (head_row % 8) * 2 + head_row // 8
    own_match = jnp.logical_and(matches, jnp.logical_and(head_col >= 64, head_col < 320))
    parts = []
    for k in range(2):
        line = jnp.concatenate([w_head[k : k + 1, :].astype(F32)] * 12, axis=1)
        parts.append(jnp.where(matches, line, 0.0))
    wb_head = jnp.concatenate(parts, axis=0).astype(BF16)
    db_head = dot_t(eye(384), wb_head).astype(BF16)

    for n, k in enumerate((-1, 1)):
        arrive(edge_in.at[n], s_t.at[n], r_t.at[n], (g, band_peer(k)))
    truth = jnp.concatenate(
        [edge_in[0], truth_ref[0], edge_in[1], jnp.zeros((2, LON), F32)], axis=0
    )
    truth = jnp.concatenate([truth, jnp.zeros((8, 96), F32)], axis=1)
    cuts = thirds(truth)
    lines = [cut[:, 256 * j : 256 * j + 256] for j in range(6) for cut in cuts]
    split = dot_t(jnp.concatenate(lines, axis=0).astype(BF16), weave)
    even, odd = [], []
    for j in range(6):
        one = split[24 * j : 24 * j + 8] + split[24 * j + 8 : 24 * j + 16]
        one = one + split[24 * j + 16 : 24 * j + 24]
        even.append(one[:, :LANES])
        odd.append(one[:, LANES:])
    truth_eo = jnp.concatenate(
        [jnp.concatenate(even, axis=1), jnp.concatenate(odd, axis=1)], axis=0
    )[:, :HALF]

    for n, k in enumerate(reach):
        arrive(far_f.at[n], s_f.at[n], r_f.at[n], (g, band_peer(k)))
    for n, k in enumerate(reach):
        there = as_scale(jnp.logical_and(b + k >= 0, b + k < n_band))
        start = (0, 4, 12, 16)[n]
        for r in range(ROWS):
            x_f[start + r] = feature_taps(far_f[n, r], there)

    def one_step(it, carry):
        window = x_f[pl.ds(3 * it, 5)].reshape(160, HALF)
        value = dot(wb_in[...], window)
        for i in range(3):
            row = 3 * it + i
            place = ROWS * b + row - 7
            inside = as_scale(jnp.logical_and(place >= 0, place < ROWS * n_band))
            here = value[64 * i : 64 * i + 64]
            pre_one[row] = here
            hidden = (here * sigmoid(here) * inside).astype(BF16)
            even, odd = hidden[:32], hidden[32:]
            x_one[row, 0:32] = later(odd, 1)
            x_one[row, 32:64] = even
            x_one[row, 64:96] = odd
            x_one[row, 96:128] = earlier(even, 1)
        return carry

    lax.fori_loop(0, 6, one_step, 0, unroll=3)

    def two_step(it, carry):
        value = dot(wb_down[...], x_one[pl.ds(4 * it, 6)].reshape(768, HALF))
        for m in range(2):
            row = 2 * it + m
            place = 2 * b + row - 3
            inside = as_scale(jnp.logical_and(place >= 0, place < 2 * n_band))
            here = value[32 * m : 32 * m + 32]
            pre_two[row] = here
            hidden = (here * sigmoid(here) * inside).astype(BF16)
            x_two[row, 0:32] = later(hidden, 2)
            x_two[row, 32:64] = hidden
            x_two[row, 64:96] = earlier(hidden, 2)
        return carry

    lax.fori_loop(0, 4, two_step, 0, unroll=True)

    for it in range(2):
        value = dot(wb_mid[...], x_two[2 * it : 2 * it + 6].reshape(576, HALF))
        for m in range(2):
            row = 2 * it + m
            place = 2 * b + row - 1
            inside = as_scale(jnp.logical_and(place >= 0, place < 2 * n_band))
            here = value[32 * m : 32 * m + 32]
            pre_three[row] = here
            hidden = (here * sigmoid(here) * inside).astype(BF16)
            before, after = later(hidden, 1), earlier(hidden, 1)
            for target in (2 * row, 2 * row + 1):
                x_three[target, 0:32] = before
                x_three[target, 32:64] = hidden
                x_three[target, 64:96] = hidden
                x_three[target, 96:128] = after

    def four_step(it, carry):
        value = dot(wb_up3[...], x_three[pl.ds(2 * it, 4)].reshape(512, HALF))
        value = value + dot(wb_up1[...], x_one[pl.ds(2 * it + 5, 4)].reshape(512, HALF))
        rows = pl.ds(pl.multiple_of(128 * it, 128), 128)
        pre_four[rows, :] = value
        h_four[rows, :] = (value * sigmoid(value)).astype(BF16)
        return carry

    lax.fori_loop(0, 3, four_step, 0, unroll=True)

    head = dot(wb_head, h_four[...])
    mean, raw = head[:16], head[16:]
    noise = 0.1 + jnp.maximum(raw, 0.0) + jnp.log1p(jnp.exp(-jnp.abs(raw)))
    z = (mean - truth_eo) / noise
    per_cell = noise * CELLS
    head_place = iota((16, HALF), 0) % 8 + ROWS * b - 1
    on_grid = jnp.logical_and(head_place >= 0, head_place < ROWS * n_band)
    on_grid = jnp.logical_and(on_grid, iota((16, HALF), 0) % 8 < 6)
    g_mean = jnp.where(on_grid, z / per_cell, 0.0)
    g_raw = jnp.where(on_grid, (1.0 - z * z) / per_cell * sigmoid(raw), 0.0)
    g_head = jnp.concatenate([g_mean, g_raw], axis=0).astype(BF16)

    def taps_of(target_ref, row, even, odd):
        target_ref[row, 0:32] = later(odd, 1)
        target_ref[row, 32:64] = even
        target_ref[row, 64:96] = odd
        target_ref[row, 96:128] = earlier(even, 1)

    back = dot(db_head, g_head)
    for i in range(6):
        rows = slice(64 * i, 64 * i + 64)
        value = (back[rows] * slope(pre_four[rows, :])).astype(BF16)
        g_four[i] = value
        taps_of(x_gfour, i, value[:32], value[32:])

    for it in range(2):
        value = dot(db_up[...], x_gfour[2 * it : 2 * it + 4].reshape(512, HALF))
        pooled = None
        for s in range(2):
            for p in range(2):
                at = 128 * s + 64 * p
                rounded = value[at : at + 64].astype(BF16)
                gj_one[2 * it + s, 32 * p : 32 * p + 32] = rounded[32:]
                upper = rounded[:32].astype(F32)
                pooled = upper if pooled is None else pooled + upper
        g_three[it] = (pooled * slope(pre_three[it + 1])).astype(BF16)
    send(g_three, far_three.at[2], s_3.at[0], r_3.at[2], (g, band_peer(-1)))
    send(g_three, far_three.at[1], s_3.at[1], r_3.at[1], (g, band_peer(1)))
    send(g_three.at[0], far_three.at[3, 0], s_3.at[2], r_3.at[3], (g, band_peer(-2)))
    send(g_three.at[1], far_three.at[0, 1], s_3.at[3], r_3.at[0], (g, band_peer(2)))

    cuts = thirds(jnp.concatenate([mean, jnp.zeros((16, 48), F32)], axis=1))
    lines = []
    for j in range(6):
        for cut in cuts:
            block = cut[:, LANES * j : LANES * j + LANES]
            lines.append(jnp.concatenate([block[:8], block[8:]], axis=1))
    woven = dot(jnp.concatenate(lines, axis=0).astype(BF16), weave)
    joined = []
    for j in range(6):
        one = woven[24 * j : 24 * j + 8] + woven[24 * j + 8 : 24 * j + 16]
        joined.append(one + woven[24 * j + 16 : 24 * j + 24])
    mean_out[0] = jnp.concatenate(joined, axis=1)[1 : 1 + ROWS, :LON]

    g_all = g_four[1:5].reshape(256, HALF)
    cross = dot_t(g_head, h_four[...])
    head_grad = []
    for k in range(2):
        line = jnp.sum(
            jnp.where(own_match, cross[16 * k : 16 * k + 16], 0.0), axis=0, keepdims=True
        )
        total = line[:, 0:32]
        for n in range(1, 12):
            total = total + line[:, 32 * n : 32 * n + 32]
        head_grad.append(total)
    head_grad = jnp.concatenate(head_grad + [jnp.zeros((30, 32), F32)], axis=0)
    up_grads = []
    for ref, source in ((big_a, x_three[1:7]), (big_b, x_one[6:12])):
        ref[...] = dot_t(g_all, source.reshape(768, HALF))
        for a in range(3):
            total = None
            for i in range(4):
                for p in range(2):
                    row, col = (2 * i + p) * 32, (i + a) * 128 + p * 32
                    piece = ref[row : row + 32, col : col + 96]
                    total = piece if total is None else total + piece
            up_grads.append(total)
    cross = dot_t(g_three[...].reshape(64, HALF), x_two[1:7].reshape(576, HALF))
    mid_grads = [
        cross[0:32, 192 * a : 192 * a + 96] + cross[32:64, 192 * a + 96 : 192 * a + 192]
        for a in range(3)
    ]
    pieces = [grad[:, 32 * t : 32 * t + 32] for grad in mid_grads for t in range(3)]
    for n in range(6):
        block = jnp.concatenate([up_grads[n], pieces[n]], axis=1)
        early[4 * n : 4 * n + 4] = block.reshape(4, 8, LANES)
    early[24:28] = jnp.concatenate(pieces[6:9] + [head_grad], axis=1).reshape(4, 8, LANES)
    early[28:32] = jnp.zeros((4, 8, LANES), F32)

    def scatter_group(source, size, target, send_sems, recv_sems):
        for k in range(1, n_group):
            peer = group_peer(k)
            send(
                source.at[pl.ds(size * peer, size)],
                target.at[g],
                send_sems.at[k],
                recv_sems.at[g],
                (peer, b),
            )
        target[g] = source[pl.ds(size * g, size)]

    def spread_group(target, send_sems, recv_sems):
        for k in range(1, n_group):
            send(target.at[g], target.at[g], send_sems.at[k], recv_sems.at[g], (group_peer(k), b))

    def spread_band(target, send_sems, recv_sems):
        for k in range(1, n_band):
            send(target.at[b], target.at[b], send_sems.at[k], recv_sems.at[b], (g, band_peer(k)))

    def await_group(target, send_sems, recv_sems):
        for k in range(1, n_group):
            peer = group_peer(-k)
            arrive(target.at[peer], send_sems.at[k], recv_sems.at[peer], (peer, b))

    def await_band(target, send_sems, recv_sems):
        for k in range(1, n_band):
            peer = band_peer(-k)
            arrive(target.at[peer], send_sems.at[k], recv_sems.at[peer], (g, peer))

    def added(ref, count):
        total = ref[0]
        for n in range(1, count):
            total = total + ref[n]
        return total

    early_size, late_size = 32 // n_group, 16 // n_group
    scatter_group(early, early_size, early_got, s_e1, r_e1)

    def spread_taps(target_ref, row, value, count):
        target_ref[row, 0:32] = later(value, count)
        target_ref[row, 32:64] = value
        target_ref[row, 64:96] = earlier(value, count)

    for m in range(2):
        spread_taps(x_gthree, 3 + m, g_three[m], 2)
    for n, k in ((1, -1), (2, 1), (0, -2), (3, 2)):
        target = (far_three.at[0, 1], far_three.at[1], far_three.at[2], far_three.at[3, 0])[n]
        arrive(target, s_3.at[n], r_3.at[n], (g, band_peer(k)))
        there = as_scale(jnp.logical_and(b + k >= 0, b + k < n_band))
        for m in ((1,), (0, 1), (0, 1), (0,))[n]:
            value = (far_three[n, m].astype(F32) * there).astype(BF16)
            spread_taps(x_gthree, 3 + 2 * k + m, value, 2)
    for it in range(2):
        value = dot(db_mid[...], x_gthree[2 * it : 2 * it + 6].reshape(576, HALF))
        for m in range(2):
            row = 2 * it + m
            place = 2 * b + row - 1
            inside = as_scale(jnp.logical_and(place >= 0, place < 2 * n_band))
            here = value[32 * m : 32 * m + 32] * slope(pre_two[2 + row]) * inside
            g_two[row] = here.astype(BF16)
    cross = dot_t(g_two[1:3].reshape(64, HALF), x_one[6:12].reshape(768, HALF))
    for a in range(4):
        block = (
            cross[0:32, 128 * a : 128 * a + 128] + cross[32:64, 128 * a + 256 : 128 * a + 384]
        )
        late[4 * a : 4 * a + 4] = block.reshape(4, 8, LANES)
    scatter_group(late, late_size, late_got, s_l1, r_l1)
    for m in range(4):
        spread_taps(x_gtwo, m, g_two[m], 1)
    value = dot(db_down[...], x_gtwo[...].reshape(384, HALF))
    for i in range(4):
        total = value[64 * i : 64 * i + 64] + gj_one[i].astype(F32)
        g_one[i] = (total * slope(pre_one[7 + i])).astype(BF16)
    cross = dot_t(x_f[7:13].reshape(192, HALF), g_one[...].reshape(256, HALF))
    in_grads = []
    for a in range(3):
        total = None
        for i in range(4):
            for p in range(2):
                row, col = (i + a) * 32 + p * 8, (2 * i + p) * 32
                piece = cross[row : row + 24, col : col + 32]
                total = piece if total is None else total + piece
        in_grads.append(total)
    in_got[g] = jnp.concatenate(in_grads + [jnp.zeros((24, 32), F32)], axis=1)
    spread_group(in_got, s_i1, r_i1)
    await_group(early_got, s_e1, r_e1)
    early_part[b] = added(early_got, n_group)
    spread_band(early_part, s_e2, r_e2)
    await_group(late_got, s_l1, r_l1)
    late_part[b] = added(late_got, n_group)
    spread_band(late_part, s_l2, r_l2)
    await_group(in_got, s_i1, r_i1)
    in_part[b] = added(in_got, n_group)
    spread_band(in_part, s_i2, r_i2)
    await_band(early_part, s_e2, r_e2)
    early_full[g] = added(early_part, n_band)
    spread_group(early_full, s_e3, r_e3)
    await_band(late_part, s_l2, r_l2)
    late_full[g] = added(late_part, n_band)
    spread_group(late_full, s_l3, r_l3)
    await_band(in_part, s_i2, r_i2)
    in_out[...] = added(in_part, n_band)
    await_group(early_full, s_e3, r_e3)
    early_out[...] = early_full[...].reshape(32, 8, LANES)
    await_group(late_full, s_l3, r_l3)
    late_out[...] = late_full[...].reshape(16, 8, LANES)
    for copy in sent:
        copy.wait_send()


def outputs_kernel(
    mean_ref, early_ref, late_ref, in_ref, mean_out, in_out, down_out, mid_out, up_out, head_out
):
    mean_out[...] = mean_ref[...]
    early = [early_ref[4 * n : 4 * n + 4].reshape(32, LANES) for n in range(7)]
    pieces = [early[n][:, 96:128] for n in range(6)]
    pieces += [early[6][:, 32 * t : 32 * t + 32] for t in range(3)]
    for a in range(4):
        block = late_ref[4 * a : 4 * a + 4].reshape(32, LANES)
        for t in range(4):
            down_out[a, t] = block[:, 32 * t : 32 * t + 32]
    for a in range(3):
        for t in range(3):
            up_out[a, t] = jnp.concatenate(
                [early[a][:, 32 * t : 32 * t + 32], early[3 + a][:, 32 * t : 32 * t + 32]], axis=1
            )
            mid_out[a, t] = pieces[3 * a + t]
            in_out[a, t] = in_ref[8 * t : 8 * t + 8, 32 * a : 32 * a + 32]
    head_out[...] = early[6][0:2, 96:128]


def local(
    station_rows,
    station_lons,
    station_obs,
    station_live,
    block_band,
    truth_field,
    length_scales,
    w_in,
    w_down,
    w_mid,
    w_up,
    w_head,
):
    n_group, n_band = lax.axis_size("group"), lax.axis_size("band")
    vmem = pl.BlockSpec(memory_space=pltpu.VMEM)
    smem = pl.BlockSpec(memory_space=pltpu.SMEM)
    dma = pltpu.SemaphoreType.DMA

    def space(dtype, *shape):
        return pltpu.VMEM(shape, dtype)

    w_in = jnp.transpose(w_in, (0, 1, 3, 2))
    early_size, late_size = 32 // n_group, 16 // n_group
    raw = (truth_field.shape, (32, 8, LANES), (16, 8, LANES), (24, LANES))
    summed = pl.pallas_call(
        functools.partial(step_kernel, n_group, n_band),
        out_shape=[pltpu.VMEM(shape, F32) for shape in raw],
        in_specs=[pl.BlockSpec(memory_space=pl.ANY)] * 10 + [smem] * 2,
        out_specs=[vmem] * 4,
        scratch_shapes=[
            pltpu.VMEM(part.shape, part.dtype)
            for part in (
                station_rows,
                station_lons,
                station_obs,
                station_live,
                truth_field,
                w_in,
                w_down,
                w_mid,
                w_up,
                w_head,
            )
        ]
        + [
            dma((10,)),
            space(F32, 4, n_band * CAP, LANES),
            space(F32, n_band, 4 * CAP, LANES),
            space(F32, n_band, 4 * CAP, LANES),
            space(BF16, 4, 2 * LANES, 6 * 2 * LANES),
            space(F32, ROWS, 16, HALF),
            space(BF16, ROWS, 16, HALF),
            space(BF16, 4, ROWS, 16, HALF),
            space(BF16, 20, 32, HALF),
            space(BF16, 18, 128, HALF),
            space(F32, 18, 64, HALF),
            space(BF16, 8, 96, HALF),
            space(F32, 8, 32, HALF),
            space(F32, 4, 32, HALF),
            space(BF16, 8, 128, HALF),
            space(F32, 384, HALF),
            space(BF16, 384, HALF),
            space(BF16, 6, 64, HALF),
            space(F32, 2, 1, LON),
            space(F32, 2, 1, LON),
            space(BF16, 6, 128, HALF),
            space(F32, 256, 768),
            space(F32, 256, 768),
            space(BF16, 4, 64, HALF),
            space(BF16, 2, 32, HALF),
            space(BF16, 4, 2, 32, HALF),
            space(BF16, 8, 96, HALF),
            space(BF16, 4, 32, HALF),
            space(BF16, 4, 96, HALF),
            space(BF16, 4, 64, HALF),
            space(BF16, 192, 160),
            space(BF16, 64, 768),
            space(BF16, 64, 576),
            space(BF16, 128, 512),
            space(BF16, 128, 512),
            space(BF16, 256, 512),
            space(BF16, 64, 576),
            space(BF16, 256, 384),
            space(F32, 32, 8, LANES),
            space(F32, n_group, early_size, 8, LANES),
            space(F32, n_band, early_size, 8, LANES),
            space(F32, n_group, early_size, 8, LANES),
            space(F32, 16, 8, LANES),
            space(F32, n_group, late_size, 8, LANES),
            space(F32, n_band, late_size, 8, LANES),
            space(F32, n_group, late_size, 8, LANES),
            space(F32, n_group, 24, LANES),
            space(F32, n_band, 24, LANES),
            dma((n_band,)),
            dma((n_band,)),
            dma((4,)),
            dma((4,)),
            dma((2,)),
            dma((2,)),
            dma((4,)),
            dma((4,)),
        ]
        + [dma((count,)) for count in (n_group, n_band, n_group) * 2 for _ in range(2)]
        + [dma((count,)) for count in (n_group, n_band) for _ in range(2)],
        compiler_params=pltpu.CompilerParams(
            collective_id=0, has_side_effects=True, vmem_limit_bytes=VMEM_LIMIT
        ),
    )(
        station_rows,
        station_lons,
        station_obs,
        station_live,
        truth_field,
        w_in,
        w_down,
        w_mid,
        w_up,
        w_head,
        jnp.transpose(block_band, (0, 2, 1)),
        length_scales,
    )
    outs = (truth_field, w_in, w_down, w_mid, w_up, w_head)
    mean, grad_in, grad_down, grad_mid, grad_up, grad_head = pl.pallas_call(
        outputs_kernel,
        out_shape=[jax.ShapeDtypeStruct(out.shape, F32) for out in outs],
        in_specs=[vmem] * 4,
        out_specs=[vmem] * 6,
    )(*[pltpu.with_memory_space_constraint(part, pltpu.VMEM) for part in summed])
    return mean, jnp.transpose(grad_in, (0, 1, 3, 2)), grad_down, grad_mid, grad_up, grad_head


def solution(mesh):
    spread = P("group", "band", None)
    return jax.shard_map(
        local,
        mesh=mesh,
        in_specs=(spread,) * 6 + (P(),) * 6,
        out_specs=(spread,) + (P(),) * 5,
        check_vma=False,
    )
```

```python
import functools

import jax
import jax.numpy as jnp
from jax import lax
from jax.experimental import pallas as pl
from jax.experimental.pallas import tpu as pltpu
from jax.sharding import PartitionSpec as P

MESH = pl.DeviceIdType.MESH
F32 = jnp.float32
BF16 = jnp.bfloat16
PHASES = (((1, 0), (3, -1)), ((0, 1), (2, 0)))
ROWS = 4
LON = 1440
HALF = 720
NBLK = 24
CAP = 3
LANES = 128
CELL = 120
SLABS = 12
CELLS = 92160.0
VMEM_LIMIT = 56 * 1024 * 1024


def dot(first, second):
    return lax.dot_general(first, second, (((1,), (0,)), ((), ())), preferred_element_type=F32)


def dot_t(first, second):
    return lax.dot_general(first, second, (((1,), (1,)), ((), ())), preferred_element_type=F32)


def iota(shape, dim):
    return lax.broadcasted_iota(jnp.int32, shape, dim)


def eye(size):
    return (iota((size, size), 0) == iota((size, size), 1)).astype(F32).astype(BF16)


def later(values, count):
    width = values.shape[-1]
    return jnp.concatenate([values[:, width - count :], values[:, : width - count]], axis=1)


def earlier(values, count):
    return jnp.concatenate([values[:, count:], values[:, :count]], axis=1)


def thirds(values):
    high = values.astype(BF16).astype(F32)
    rest = values - high
    middle = rest.astype(BF16).astype(F32)
    return high, middle, rest - middle


def sigmoid(values):
    return 0.5 * jnp.tanh(0.5 * values) + 0.5


def slope(values):
    squash = sigmoid(values)
    return squash * (1.0 + values * (1.0 - squash))


def as_scale(flag):
    return flag.astype(jnp.int32).astype(F32)


def step_kernel(
    n_group,
    n_band,
    rows_far,
    lons_far,
    obs_far,
    live_far,
    truth_far,
    w_in_far,
    w_down_far,
    w_mid_far,
    w_up_far,
    w_head_far,
    band_ref,
    ell_ref,
    mean_out,
    early_out,
    late_out,
    in_out,
    rows_ref,
    lons_ref,
    obs_ref,
    live_ref,
    truth_ref,
    w_in,
    w_down,
    w_mid,
    w_up,
    w_head,
    s_in,
    picked,
    outbox,
    inbox,
    gauss,
    feats32,
    own_f,
    far_f,
    x_f,
    x_one,
    pre_one,
    x_two,
    pre_two,
    pre_three,
    x_three,
    pre_four,
    h_four,
    g_four,
    edge_out,
    edge_in,
    x_gfour,
    big_a,
    big_b,
    gj_one,
    g_three,
    far_three,
    x_gthree,
    g_two,
    x_gtwo,
    g_one,
    wb_in,
    wb_down,
    wb_mid,
    wb_up3,
    wb_up1,
    db_up,
    db_mid,
    db_down,
    early,
    early_got,
    early_part,
    early_full,
    late,
    late_got,
    late_part,
    late_full,
    in_got,
    in_part,
    s_a,
    r_a,
    s_f,
    r_f,
    s_t,
    r_t,
    s_3,
    r_3,
    s_e1,
    r_e1,
    s_e2,
    r_e2,
    s_e3,
    r_e3,
    s_l1,
    r_l1,
    s_l2,
    r_l2,
    s_l3,
    r_l3,
    s_i1,
    r_i1,
    s_i2,
    r_i2,
):
    g = lax.axis_index("group")
    b = lax.axis_index("band")
    barrier = pltpu.get_barrier_semaphore()
    for k in range(1, n_group):
        pl.semaphore_signal(
            barrier, inc=1, device_id=(lax.rem(g + k, n_group), b), device_id_type=MESH
        )
    for k in range(1, n_band):
        pl.semaphore_signal(
            barrier, inc=1, device_id=(g, lax.rem(b + k, n_band)), device_id_type=MESH
        )

    def band_peer(k):
        return lax.rem(b + n_band + k, n_band)

    def group_peer(k):
        return lax.rem(g + n_group + k, n_group)

    sent = []

    def send(source, target, send_sem, recv_sem, device):
        copy = pltpu.make_async_remote_copy(
            src_ref=source,
            dst_ref=target,
            send_sem=send_sem,
            recv_sem=recv_sem,
            device_id=device,
            device_id_type=MESH,
        )
        copy.start()
        sent.append(copy)

    def arrive(target, send_sem, recv_sem, device):
        pltpu.make_async_remote_copy(
            src_ref=target,
            dst_ref=target,
            send_sem=send_sem,
            recv_sem=recv_sem,
            device_id=device,
            device_id_type=MESH,
        ).wait_recv()

    fetches = []
    pairs = (
        (rows_far, rows_ref),
        (lons_far, lons_ref),
        (obs_far, obs_ref),
        (live_far, live_ref),
        (truth_far, truth_ref),
        (w_in_far, w_in),
        (w_down_far, w_down),
        (w_mid_far, w_mid),
        (w_up_far, w_up),
        (w_head_far, w_head),
    )
    for n, (source, target) in enumerate(pairs):
        fetch = pltpu.make_async_copy(source, target, s_in.at[n])
        fetch.start()
        fetches.append(fetch)
    for fetch in fetches[:5]:
        fetch.wait()
    slot_rows = iota((n_band * CAP, LANES), 0)
    slot_band, slot_place = slot_rows // CAP, slot_rows % CAP
    seen = jnp.zeros((n_band * CAP, LANES), jnp.int32)
    chosen = [jnp.zeros((n_band * CAP, LANES), F32) for _ in range(4)]
    for block in range(NBLK):
        mine = slot_band == band_ref[0, 0, block]
        here = jnp.logical_and(mine, seen == slot_place)
        fields = (
            rows_ref[0, block : block + 1, :].astype(F32),
            lons_ref[0, block : block + 1, :].astype(F32),
            obs_ref[0, block : block + 1, :],
            live_ref[0, block : block + 1, :].astype(F32),
        )
        chosen = [jnp.where(here, new, old) for new, old in zip(fields, chosen)]
        seen = seen + mine.astype(jnp.int32)
    for field in range(4):
        picked[field] = chosen[field]
    for q in range(n_band):
        for field in range(4):
            outbox[q, CAP * field : CAP * field + CAP, :] = picked[
                field, CAP * q : CAP * q + CAP, :
            ]

    edge_out[0] = truth_ref[0, 0:1, :]
    edge_out[1] = truth_ref[0, ROWS - 1 : ROWS, :]
    pl.semaphore_wait(barrier, n_group + n_band - 2)
    for k in range(1, n_band):
        peer = band_peer(k)
        send(outbox.at[peer], inbox.at[b], s_a.at[k], r_a.at[b], (g, peer))
    send(edge_out.at[0], edge_in.at[1], s_t.at[0], r_t.at[1], (g, band_peer(-1)))
    send(edge_out.at[1], edge_in.at[0], s_t.at[1], r_t.at[0], (g, band_peer(1)))
    inbox[b] = outbox[b]

    wide = (2 * LANES, 2 * LANES)
    row_id, col_id = iota(wide, 0), iota(wide, 1)
    base = (
        2 * (col_id % LANES) + col_id // LANES - row_id % LANES + CELL * (row_id // LANES)
    ).astype(F32)
    coefs = []
    for scale in range(4):
        ell = jnp.full((1, 2 * LANES), ell_ref[scale], F32)
        coefs.append(-0.5 / (ell * ell))

    def gauss_step(e, carry):
        gap = jnp.abs(base + (2 * CELL * e).astype(F32))
        gap = jnp.minimum(gap, LON - gap)
        square = gap * gap
        cols = pl.ds(pl.multiple_of(e * 2 * LANES, 2 * LANES), 2 * LANES)
        for scale in range(4):
            gauss[scale, :, cols] = jnp.exp(square * coefs[scale]).astype(BF16)
        return carry

    lax.fori_loop(0, SLABS // 2, gauss_step, 0)

    weave = (col_id == 2 * (row_id % LANES) + row_id // LANES).astype(F32).astype(BF16)

    left_id = iota((32, LANES), 0)
    left_row = (left_id % 4).astype(F32)
    with_obs = (left_id // 4) % 2 == 1
    left_coef = jnp.zeros((32, LANES), F32)
    for scale in range(4):
        left_coef = jnp.where(left_id // 8 == scale, coefs[scale][:, :LANES], left_coef)
    lane_cell = iota((LANES, LANES), 0).astype(F32)
    counted = None
    order = [0]
    for k in range(1, n_band // 2):
        order += [k, -k]
    order.append(n_band // 2)
    for quarter in range(4):
        lefts, rights = [], []
        for k in order[4 * quarter : 4 * quarter + 4]:
            peer = band_peer(-k)
            if k:
                arrive(inbox.at[peer], s_a.at[k % n_band], r_a.at[peer], (g, peer))
            fields = inbox[peer]
            for slot in range(CAP):
                row = fields[slot : slot + 1]
                lon = fields[CAP + slot : CAP + slot + 1]
                seen_value = fields[2 * CAP + slot : 2 * CAP + slot + 1]
                alive = fields[3 * CAP + slot : 3 * CAP + slot + 1]
                slab = jnp.floor((lon + 0.5) * (1.0 / CELL))
                cell = lon - CELL * slab
                gap = left_row - row
                factor = jnp.where(with_obs, alive * seen_value, alive)
                left = factor * jnp.exp(gap * gap * left_coef)
                lefts.append(
                    jnp.concatenate(
                        [jnp.where(slab == float(h), left, 0.0) for h in range(SLABS)], axis=0
                    ).astype(BF16)
                )
                rights.append(jnp.where(lane_cell == cell, 1.0, 0.0).astype(BF16))
        more = dot_t(jnp.concatenate(lefts, axis=1), jnp.concatenate(rights, axis=1))
        counted = more if counted is None else counted + more

    cuts = thirds(counted)
    for scale in range(4):
        lines = []
        for j in range(6):
            now, before = (2 * j) * 32 + 8 * scale, ((2 * j - 1) % SLABS) * 32 + 8 * scale
            for cut in cuts:
                lines.append(jnp.concatenate([cut[now : now + 8], cut[before : before + 8]], axis=1))
        spread = dot(jnp.concatenate(lines, axis=0).astype(BF16), gauss[scale])
        even, odd = [], []
        for j in range(6):
            total = None
            for e in range(6):
                at = 24 * ((j - e) % 6)
                for third in range(3):
                    piece = spread[at + 8 * third : at + 8 * third + 8, 256 * e : 256 * e + 256]
                    total = piece if total is None else total + piece
            even.append(total[:, :CELL])
            odd.append(total[:, LANES : LANES + CELL])
        for p, pieces in enumerate((even, odd)):
            sums = jnp.concatenate(pieces, axis=1)
            density, signal = sums[:4], sums[4:]
            base_p = 1.0 + density
            first, second = density / base_p, signal / base_p
            for r in range(ROWS):
                at = 8 * p + 2 * scale
                feats32[r, at : at + 1, :] = first[r : r + 1]
                feats32[r, at + 1 : at + 2, :] = second[r : r + 1]
    for r in range(ROWS):
        own_f[r] = feats32[r].astype(BF16)

    reach = (-2, -1, 1, 2)
    for n, k in enumerate(reach):
        send(own_f, far_f.at[3 - n], s_f.at[n], r_f.at[3 - n], (g, band_peer(k)))

    def feature_taps(source, scale):
        values = source.astype(F32) if scale is None else source.astype(F32) * scale
        even, odd = values[:8], values[8:]
        return jnp.concatenate([later(odd, 1), even, odd, earlier(even, 1)], axis=0).astype(BF16)

    for r in range(ROWS):
        x_f[8 + r] = feature_taps(own_f[r], None)
    for fetch in fetches[5:]:
        fetch.wait()
    for ref in (wb_in, wb_down, wb_mid, wb_up3, wb_up1, db_up, db_mid, db_down):
        ref[...] = jnp.zeros_like(ref)
    turned_in = dot_t(eye(32), w_in[...].astype(F32).reshape(72, 32).astype(BF16)).astype(BF16)
    turned_up = dot_t(eye(64), w_up[...].reshape(288, 64)).astype(BF16)
    turned_mid = dot_t(eye(32), w_mid[...].reshape(288, 32)).astype(BF16)
    turned_down = dot_t(eye(32), w_down[...].reshape(512, 32)).astype(BF16)
    for a in range(3):
        for t in range(3):
            at = (a * 3 + t) * 8
            block = turned_in[:, at : at + 8]
            for i in range(3):
                for p in range(2):
                    row, col = (2 * i + p) * 32, (i + a) * 32 + (t + p) * 8
                    wb_in[row : row + 32, col : col + 8] = block
            upper, lower = w_up[a, t, :, :32], w_up[a, t, :, 32:]
            at = ((2 - a) * 3 + 2 - t) * 32
            for i in range(2):
                for p in range(2):
                    row, col = (2 * i + p) * 32, (i + a) * 128 + (t + p) * 32
                    wb_up3[row : row + 32, col : col + 32] = upper
                    wb_up1[row : row + 32, col : col + 32] = lower
                    db_up[2 * row : 2 * row + 64, col : col + 32] = turned_up[:, at : at + 32]
                row, col = i * 32, (i + 2 * a) * 96 + t * 32
                wb_mid[row : row + 32, col : col + 32] = w_mid[a, t]
                db_mid[row : row + 32, col : col + 32] = turned_mid[:, at : at + 32]
    for a in range(4):
        for t in range(4):
            for m in range(2):
                col = (2 * m + a) * 128 + t * 32
                wb_down[m * 32 : m * 32 + 32, col : col + 32] = w_down[a, t]
    for m in range(2):
        for s in range(2):
            for p in range(2):
                row = ((2 * m + s) * 2 + p) * 32
                for a, up_down in PHASES[s]:
                    for t, left_right in PHASES[p]:
                        col = (m + up_down + 1) * 96 + (left_right + 1) * 32
                        at = (a * 4 + t) * 32
                        db_down[row : row + 32, col : col + 32] = turned_down[:, at : at + 32]
    head_row, head_col = iota((16, 384), 0), iota((16, 384), 1)
    matches = (head_col // 32) == (head_row % 8) * 2 + head_row // 8
    own_match = jnp.logical_and(matches, jnp.logical_and(head_col >= 64, head_col < 320))
    parts = []
    for k in range(2):
        line = jnp.concatenate([w_head[k : k + 1, :].astype(F32)] * 12, axis=1)
        parts.append(jnp.where(matches, line, 0.0))
    wb_head = jnp.concatenate(parts, axis=0).astype(BF16)
    db_head = dot_t(eye(384), wb_head).astype(BF16)

    for n, k in enumerate((-1, 1)):
        arrive(edge_in.at[n], s_t.at[n], r_t.at[n], (g, band_peer(k)))
    truth = jnp.concatenate(
        [edge_in[0], truth_ref[0], edge_in[1], jnp.zeros((2, LON), F32)], axis=0
    )
    truth = jnp.concatenate([truth, jnp.zeros((8, 96), F32)], axis=1)
    cuts = thirds(truth)
    lines = [cut[:, 256 * j : 256 * j + 256] for j in range(6) for cut in cuts]
    split = dot_t(jnp.concatenate(lines, axis=0).astype(BF16), weave)
    even, odd = [], []
    for j in range(6):
        one = split[24 * j : 24 * j + 8] + split[24 * j + 8 : 24 * j + 16]
        one = one + split[24 * j + 16 : 24 * j + 24]
        even.append(one[:, :LANES])
        odd.append(one[:, LANES:])
    truth_eo = jnp.concatenate(
        [jnp.concatenate(even, axis=1), jnp.concatenate(odd, axis=1)], axis=0
    )[:, :HALF]

    for n, k in enumerate(reach):
        arrive(far_f.at[n], s_f.at[n], r_f.at[n], (g, band_peer(k)))
    for n, k in enumerate(reach):
        there = as_scale(jnp.logical_and(b + k >= 0, b + k < n_band))
        start = (0, 4, 12, 16)[n]
        for r in range(ROWS):
            x_f[start + r] = feature_taps(far_f[n, r], there)

    def one_step(it, carry):
        window = x_f[pl.ds(3 * it, 5)].reshape(160, HALF)
        value = dot(wb_in[...], window)
        for i in range(3):
            row = 3 * it + i
            place = ROWS * b + row - 7
            inside = as_scale(jnp.logical_and(place >= 0, place < ROWS * n_band))
            here = value[64 * i : 64 * i + 64]
            pre_one[row] = here
            hidden = (here * sigmoid(here) * inside).astype(BF16)
            even, odd = hidden[:32], hidden[32:]
            x_one[row, 0:32] = later(odd, 1)
            x_one[row, 32:64] = even
            x_one[row, 64:96] = odd
            x_one[row, 96:128] = earlier(even, 1)
        return carry

    lax.fori_loop(0, 6, one_step, 0, unroll=3)

    def two_step(it, carry):
        value = dot(wb_down[...], x_one[pl.ds(4 * it, 6)].reshape(768, HALF))
        for m in range(2):
            row = 2 * it + m
            place = 2 * b + row - 3
            inside = as_scale(jnp.logical_and(place >= 0, place < 2 * n_band))
            here = value[32 * m : 32 * m + 32]
            pre_two[row] = here
            hidden = (here * sigmoid(here) * inside).astype(BF16)
            x_two[row, 0:32] = later(hidden, 2)
            x_two[row, 32:64] = hidden
            x_two[row, 64:96] = earlier(hidden, 2)
        return carry

    lax.fori_loop(0, 4, two_step, 0, unroll=True)

    for it in range(2):
        value = dot(wb_mid[...], x_two[2 * it : 2 * it + 6].reshape(576, HALF))
        for m in range(2):
            row = 2 * it + m
            place = 2 * b + row - 1
            inside = as_scale(jnp.logical_and(place >= 0, place < 2 * n_band))
            here = value[32 * m : 32 * m + 32]
            pre_three[row] = here
            hidden = (here * sigmoid(here) * inside).astype(BF16)
            before, after = later(hidden, 1), earlier(hidden, 1)
            for target in (2 * row, 2 * row + 1):
                x_three[target, 0:32] = before
                x_three[target, 32:64] = hidden
                x_three[target, 64:96] = hidden
                x_three[target, 96:128] = after

    def four_step(it, carry):
        value = dot(wb_up3[...], x_three[pl.ds(2 * it, 4)].reshape(512, HALF))
        value = value + dot(wb_up1[...], x_one[pl.ds(2 * it + 5, 4)].reshape(512, HALF))
        rows = pl.ds(pl.multiple_of(128 * it, 128), 128)
        pre_four[rows, :] = value
        h_four[rows, :] = (value * sigmoid(value)).astype(BF16)
        return carry

    lax.fori_loop(0, 3, four_step, 0, unroll=True)

    head = dot(wb_head, h_four[...])
    mean, raw = head[:16], head[16:]
    noise = 0.1 + jnp.maximum(raw, 0.0) + jnp.log1p(jnp.exp(-jnp.abs(raw)))
    z = (mean - truth_eo) / noise
    per_cell = noise * CELLS
    head_place = iota((16, HALF), 0) % 8 + ROWS * b - 1
    on_grid = jnp.logical_and(head_place >= 0, head_place < ROWS * n_band)
    on_grid = jnp.logical_and(on_grid, iota((16, HALF), 0) % 8 < 6)
    g_mean = jnp.where(on_grid, z / per_cell, 0.0)
    g_raw = jnp.where(on_grid, (1.0 - z * z) / per_cell * sigmoid(raw), 0.0)
    g_head = jnp.concatenate([g_mean, g_raw], axis=0).astype(BF16)

    def taps_of(target_ref, row, even, odd):
        target_ref[row, 0:32] = later(odd, 1)
        target_ref[row, 32:64] = even
        target_ref[row, 64:96] = odd
        target_ref[row, 96:128] = earlier(even, 1)

    back = dot(db_head, g_head)
    for i in range(6):
        rows = slice(64 * i, 64 * i + 64)
        value = (back[rows] * slope(pre_four[rows, :])).astype(BF16)
        g_four[i] = value
        taps_of(x_gfour, i, value[:32], value[32:])

    for it in range(2):
        value = dot(db_up[...], x_gfour[2 * it : 2 * it + 4].reshape(512, HALF))
        pooled = None
        for s in range(2):
            for p in range(2):
                at = 128 * s + 64 * p
                rounded = value[at : at + 64].astype(BF16)
                gj_one[2 * it + s, 32 * p : 32 * p + 32] = rounded[32:]
                upper = rounded[:32].astype(F32)
                pooled = upper if pooled is None else pooled + upper
        g_three[it] = (pooled * slope(pre_three[it + 1])).astype(BF16)
        for slot, k in ((2, -1), (1, 1), (3, -2) if it == 0 else (0, 2)):
            send(
                g_three.at[it],
                far_three.at[slot, it],
                s_3.at[slot, it],
                r_3.at[slot, it],
                (g, band_peer(k)),
            )

    g_all = g_four[1:5].reshape(256, HALF)
    cross = dot_t(g_head, h_four[...])
    head_grad = []
    for k in range(2):
        line = jnp.sum(
            jnp.where(own_match, cross[16 * k : 16 * k + 16], 0.0), axis=0, keepdims=True
        )
        total = line[:, 0:32]
        for n in range(1, 12):
            total = total + line[:, 32 * n : 32 * n + 32]
        head_grad.append(total)
    head_grad = jnp.concatenate(head_grad + [jnp.zeros((30, 32), F32)], axis=0)
    up_grads = []
    for ref, source in ((big_a, x_three[1:7]), (big_b, x_one[6:12])):
        ref[...] = dot_t(g_all, source.reshape(768, HALF))
        for a in range(3):
            total = None
            for i in range(4):
                for p in range(2):
                    row, col = (2 * i + p) * 32, (i + a) * 128 + p * 32
                    piece = ref[row : row + 32, col : col + 96]
                    total = piece if total is None else total + piece
            up_grads.append(total)
    cross = dot_t(g_three[...].reshape(64, HALF), x_two[1:7].reshape(576, HALF))
    mid_grads = [
        cross[0:32, 192 * a : 192 * a + 96] + cross[32:64, 192 * a + 96 : 192 * a + 192]
        for a in range(3)
    ]
    pieces = [grad[:, 32 * t : 32 * t + 32] for grad in mid_grads for t in range(3)]
    for n in range(6):
        block = jnp.concatenate([up_grads[n], pieces[n]], axis=1)
        early[4 * n : 4 * n + 4] = block.reshape(4, 8, LANES)
    early[24:28] = jnp.concatenate(pieces[6:9] + [head_grad], axis=1).reshape(4, 8, LANES)
    early[28:32] = jnp.zeros((4, 8, LANES), F32)

    def scatter_group(source, size, target, send_sems, recv_sems):
        for k in range(1, n_group):
            peer = group_peer(k)
            send(
                source.at[pl.ds(size * peer, size)],
                target.at[g],
                send_sems.at[k],
                recv_sems.at[g],
                (peer, b),
            )
        target[g] = source[pl.ds(size * g, size)]

    def spread_group(target, send_sems, recv_sems):
        for k in range(1, n_group):
            send(target.at[g], target.at[g], send_sems.at[k], recv_sems.at[g], (group_peer(k), b))

    def spread_band(target, send_sems, recv_sems):
        for k in range(1, n_band):
            send(target.at[b], target.at[b], send_sems.at[k], recv_sems.at[b], (g, band_peer(k)))

    def await_group(target, send_sems, recv_sems):
        for k in range(1, n_group):
            peer = group_peer(-k)
            arrive(target.at[peer], send_sems.at[k], recv_sems.at[peer], (peer, b))

    def await_band(target, send_sems, recv_sems):
        for k in range(1, n_band):
            peer = band_peer(-k)
            arrive(target.at[peer], send_sems.at[k], recv_sems.at[peer], (g, peer))

    def added(ref, count):
        total = ref[0]
        for n in range(1, count):
            total = total + ref[n]
        return total

    early_size, late_size = 32 // n_group, 16 // n_group
    scatter_group(early, early_size, early_got, s_e1, r_e1)

    cuts = thirds(jnp.concatenate([mean, jnp.zeros((16, 48), F32)], axis=1))
    lines = []
    for j in range(6):
        for cut in cuts:
            block = cut[:, LANES * j : LANES * j + LANES]
            lines.append(jnp.concatenate([block[:8], block[8:]], axis=1))
    woven = dot(jnp.concatenate(lines, axis=0).astype(BF16), weave)
    joined = []
    for j in range(6):
        one = woven[24 * j : 24 * j + 8] + woven[24 * j + 8 : 24 * j + 16]
        joined.append(one + woven[24 * j + 16 : 24 * j + 24])
    mean_out[0] = jnp.concatenate(joined, axis=1)[1 : 1 + ROWS, :LON]

    def spread_taps(target_ref, row, value, count):
        target_ref[row, 0:32] = later(value, count)
        target_ref[row, 32:64] = value
        target_ref[row, 64:96] = earlier(value, count)

    for m in range(2):
        spread_taps(x_gthree, 3 + m, g_three[m], 2)
    for n, k, m in ((1, -1, 0), (2, 1, 0), (3, 2, 0), (0, -2, 1), (1, -1, 1), (2, 1, 1)):
        arrive(far_three.at[n, m], s_3.at[n, m], r_3.at[n, m], (g, band_peer(k)))
        there = as_scale(jnp.logical_and(b + k >= 0, b + k < n_band))
        value = (far_three[n, m].astype(F32) * there).astype(BF16)
        spread_taps(x_gthree, 3 + 2 * k + m, value, 2)
    for it in range(2):
        value = dot(db_mid[...], x_gthree[2 * it : 2 * it + 6].reshape(576, HALF))
        for m in range(2):
            row = 2 * it + m
            place = 2 * b + row - 1
            inside = as_scale(jnp.logical_and(place >= 0, place < 2 * n_band))
            here = value[32 * m : 32 * m + 32] * slope(pre_two[2 + row]) * inside
            g_two[row] = here.astype(BF16)
    cross = dot_t(g_two[1:3].reshape(64, HALF), x_one[6:12].reshape(768, HALF))
    for a in range(4):
        block = (
            cross[0:32, 128 * a : 128 * a + 128] + cross[32:64, 128 * a + 256 : 128 * a + 384]
        )
        late[4 * a : 4 * a + 4] = block.reshape(4, 8, LANES)
    scatter_group(late, late_size, late_got, s_l1, r_l1)
    await_group(early_got, s_e1, r_e1)
    early_part[b] = added(early_got, n_group)
    spread_band(early_part, s_e2, r_e2)
    for m in range(4):
        spread_taps(x_gtwo, m, g_two[m], 1)
    value = dot(db_down[...], x_gtwo[...].reshape(384, HALF))
    for i in range(4):
        total = value[64 * i : 64 * i + 64] + gj_one[i].astype(F32)
        g_one[i] = (total * slope(pre_one[7 + i])).astype(BF16)
    cross = dot_t(x_f[7:13].reshape(192, HALF), g_one[...].reshape(256, HALF))
    in_grads = []
    for a in range(3):
        total = None
        for i in range(4):
            for p in range(2):
                row, col = (i + a) * 32 + p * 8, (2 * i + p) * 32
                piece = cross[row : row + 24, col : col + 32]
                total = piece if total is None else total + piece
        in_grads.append(total)
    in_got[b] = jnp.concatenate(
        [
            jnp.concatenate([grad[:18] for grad in in_grads], axis=1),
            jnp.concatenate([grad[18:] for grad in in_grads], axis=0),
        ],
        axis=1,
    )
    spread_band(in_got, s_i1, r_i1)
    await_group(late_got, s_l1, r_l1)
    late_part[b] = added(late_got, n_group)
    spread_band(late_part, s_l2, r_l2)
    await_band(in_got, s_i1, r_i1)
    in_part[g] = added(in_got, n_band)
    spread_group(in_part, s_i2, r_i2)
    await_band(early_part, s_e2, r_e2)
    early_full[g] = added(early_part, n_band)
    spread_group(early_full, s_e3, r_e3)
    await_band(late_part, s_l2, r_l2)
    late_full[g] = added(late_part, n_band)
    spread_group(late_full, s_l3, r_l3)
    await_group(in_part, s_i2, r_i2)
    in_out[...] = added(in_part, n_group)
    await_group(early_full, s_e3, r_e3)
    early_out[...] = early_full[...].reshape(32, 8, LANES)
    await_group(late_full, s_l3, r_l3)
    late_out[...] = late_full[...].reshape(16, 8, LANES)
    for copy in sent:
        copy.wait_send()


def outputs_kernel(
    mean_ref, early_ref, late_ref, in_ref, mean_out, in_out, down_out, mid_out, up_out, head_out
):
    mean_out[...] = mean_ref[...]
    early = [early_ref[4 * n : 4 * n + 4].reshape(32, LANES) for n in range(7)]
    pieces = [early[n][:, 96:128] for n in range(6)]
    pieces += [early[6][:, 32 * t : 32 * t + 32] for t in range(3)]
    for a in range(4):
        block = late_ref[4 * a : 4 * a + 4].reshape(32, LANES)
        for t in range(4):
            down_out[a, t] = block[:, 32 * t : 32 * t + 32]
    for a in range(3):
        for t in range(3):
            up_out[a, t] = jnp.concatenate(
                [early[a][:, 32 * t : 32 * t + 32], early[3 + a][:, 32 * t : 32 * t + 32]], axis=1
            )
            mid_out[a, t] = pieces[3 * a + t]
    head_out[...] = early[6][0:2, 96:128]
    packed = in_ref[...]
    for a in range(3):
        whole = jnp.concatenate(
            [packed[:, 32 * a : 32 * a + 32], packed[6 * a : 6 * a + 6, 96:128]], axis=0
        )
        for t in range(3):
            in_out[a, t] = whole[8 * t : 8 * t + 8]


def local(
    station_rows,
    station_lons,
    station_obs,
    station_live,
    block_band,
    truth_field,
    length_scales,
    w_in,
    w_down,
    w_mid,
    w_up,
    w_head,
):
    n_group, n_band = lax.axis_size("group"), lax.axis_size("band")
    vmem = pl.BlockSpec(memory_space=pltpu.VMEM)
    smem = pl.BlockSpec(memory_space=pltpu.SMEM)
    dma = pltpu.SemaphoreType.DMA

    def space(dtype, *shape):
        return pltpu.VMEM(shape, dtype)

    w_in = jnp.transpose(w_in, (0, 1, 3, 2))
    early_size, late_size = 32 // n_group, 16 // n_group
    raw = (truth_field.shape, (32, 8, LANES), (16, 8, LANES), (18, LANES))
    summed = pl.pallas_call(
        functools.partial(step_kernel, n_group, n_band),
        out_shape=[pltpu.VMEM(shape, F32) for shape in raw],
        in_specs=[pl.BlockSpec(memory_space=pl.ANY)] * 10 + [smem] * 2,
        out_specs=[vmem] * 4,
        scratch_shapes=[
            pltpu.VMEM(part.shape, part.dtype)
            for part in (
                station_rows,
                station_lons,
                station_obs,
                station_live,
                truth_field,
                w_in,
                w_down,
                w_mid,
                w_up,
                w_head,
            )
        ]
        + [
            dma((10,)),
            space(F32, 4, n_band * CAP, LANES),
            space(F32, n_band, 4 * CAP, LANES),
            space(F32, n_band, 4 * CAP, LANES),
            space(BF16, 4, 2 * LANES, 6 * 2 * LANES),
            space(F32, ROWS, 16, HALF),
            space(BF16, ROWS, 16, HALF),
            space(BF16, 4, ROWS, 16, HALF),
            space(BF16, 20, 32, HALF),
            space(BF16, 18, 128, HALF),
            space(F32, 18, 64, HALF),
            space(BF16, 8, 96, HALF),
            space(F32, 8, 32, HALF),
            space(F32, 4, 32, HALF),
            space(BF16, 8, 128, HALF),
            space(F32, 384, HALF),
            space(BF16, 384, HALF),
            space(BF16, 6, 64, HALF),
            space(F32, 2, 1, LON),
            space(F32, 2, 1, LON),
            space(BF16, 6, 128, HALF),
            space(F32, 256, 768),
            space(F32, 256, 768),
            space(BF16, 4, 64, HALF),
            space(BF16, 2, 32, HALF),
            space(BF16, 4, 2, 32, HALF),
            space(BF16, 8, 96, HALF),
            space(BF16, 4, 32, HALF),
            space(BF16, 4, 96, HALF),
            space(BF16, 4, 64, HALF),
            space(BF16, 192, 160),
            space(BF16, 64, 768),
            space(BF16, 64, 576),
            space(BF16, 128, 512),
            space(BF16, 128, 512),
            space(BF16, 256, 512),
            space(BF16, 64, 576),
            space(BF16, 256, 384),
            space(F32, 32, 8, LANES),
            space(F32, n_group, early_size, 8, LANES),
            space(F32, n_band, early_size, 8, LANES),
            space(F32, n_group, early_size, 8, LANES),
            space(F32, 16, 8, LANES),
            space(F32, n_group, late_size, 8, LANES),
            space(F32, n_band, late_size, 8, LANES),
            space(F32, n_group, late_size, 8, LANES),
            space(F32, n_band, 18, LANES),
            space(F32, n_group, 18, LANES),
            dma((n_band,)),
            dma((n_band,)),
            dma((4,)),
            dma((4,)),
            dma((2,)),
            dma((2,)),
            dma((4, 2)),
            dma((4, 2)),
        ]
        + [dma((count,)) for count in (n_group, n_band, n_group) * 2 for _ in range(2)]
        + [dma((count,)) for count in (n_band, n_group) for _ in range(2)],
        compiler_params=pltpu.CompilerParams(
            collective_id=0, has_side_effects=True, vmem_limit_bytes=VMEM_LIMIT
        ),
    )(
        station_rows,
        station_lons,
        station_obs,
        station_live,
        truth_field,
        w_in,
        w_down,
        w_mid,
        w_up,
        w_head,
        jnp.transpose(block_band, (0, 2, 1)),
        length_scales,
    )
    outs = (truth_field, w_in, w_down, w_mid, w_up, w_head)
    mean, grad_in, grad_down, grad_mid, grad_up, grad_head = pl.pallas_call(
        outputs_kernel,
        out_shape=[jax.ShapeDtypeStruct(out.shape, F32) for out in outs],
        in_specs=[vmem] * 4,
        out_specs=[vmem] * 6,
    )(*[pltpu.with_memory_space_constraint(part, pltpu.VMEM) for part in summed])
    return mean, jnp.transpose(grad_in, (0, 1, 3, 2)), grad_down, grad_mid, grad_up, grad_head


def solution(mesh):
    spread = P("group", "band", None)
    return jax.shard_map(
        local,
        mesh=mesh,
        in_specs=(spread,) * 6 + (P(),) * 6,
        out_specs=(spread,) + (P(),) * 5,
        check_vma=False,
    )
```

```python
import functools

import jax
import jax.numpy as jnp
from jax import lax
from jax.experimental import pallas as pl
from jax.experimental.pallas import tpu as pltpu
from jax.sharding import PartitionSpec as P

MESH = pl.DeviceIdType.MESH
F32 = jnp.float32
BF16 = jnp.bfloat16
PHASES = (((1, 0), (3, -1)), ((0, 1), (2, 0)))
ROWS = 4
LON = 1440
HALF = 720
NBLK = 24
CAP = 3
LANES = 128
CELL = 120
SLABS = 12
CELLS = 92160.0
FAR_GROUP = (6, 10, 7, 9, 5, 11, 2, 14, 3, 13, 8, 1, 15, 4, 12)
FAR_BAND = (7, 9, 8, 5, 11, 6, 10, 3, 13, 4, 12, 1, 15, 2, 14)
VMEM_LIMIT = 56 * 1024 * 1024


def dot(first, second):
    return lax.dot_general(first, second, (((1,), (0,)), ((), ())), preferred_element_type=F32)


def dot_t(first, second):
    return lax.dot_general(first, second, (((1,), (1,)), ((), ())), preferred_element_type=F32)


def iota(shape, dim):
    return lax.broadcasted_iota(jnp.int32, shape, dim)


def eye(size):
    return (iota((size, size), 0) == iota((size, size), 1)).astype(F32).astype(BF16)


def later(values, count):
    width = values.shape[-1]
    return jnp.concatenate([values[:, width - count :], values[:, : width - count]], axis=1)


def earlier(values, count):
    return jnp.concatenate([values[:, count:], values[:, :count]], axis=1)


def thirds(values):
    high = values.astype(BF16).astype(F32)
    rest = values - high
    middle = rest.astype(BF16).astype(F32)
    return high, middle, rest - middle


def sigmoid(values):
    return 0.5 * jnp.tanh(0.5 * values) + 0.5


def slope(values):
    squash = sigmoid(values)
    return squash * (1.0 + values * (1.0 - squash))


def as_scale(flag):
    return flag.astype(jnp.int32).astype(F32)


def step_kernel(
    n_group,
    n_band,
    rows_far,
    lons_far,
    obs_far,
    live_far,
    truth_far,
    w_in_far,
    w_down_far,
    w_mid_far,
    w_up_far,
    w_head_far,
    band_ref,
    ell_ref,
    mean_out,
    early_out,
    late_out,
    in_out,
    rows_ref,
    lons_ref,
    obs_ref,
    live_ref,
    truth_ref,
    w_in,
    w_down,
    w_mid,
    w_up,
    w_head,
    s_in,
    picked,
    outbox,
    inbox,
    gauss,
    feats32,
    own_f,
    far_f,
    x_f,
    x_one,
    pre_one,
    x_two,
    pre_two,
    pre_three,
    x_three,
    pre_four,
    h_four,
    g_four,
    edge_out,
    edge_in,
    x_gfour,
    big_a,
    big_b,
    gj_one,
    g_three,
    far_three,
    x_gthree,
    g_two,
    x_gtwo,
    g_one,
    wb_in,
    wb_down,
    wb_mid,
    wb_up3,
    wb_up1,
    db_up,
    db_mid,
    db_down,
    early,
    early_got,
    early_part,
    early_full,
    late,
    late_got,
    late_part,
    late_full,
    in_got,
    in_part,
    s_a,
    r_a,
    s_f,
    r_f,
    s_t,
    r_t,
    s_3,
    r_3,
    s_e1,
    r_e1,
    s_e2,
    r_e2,
    s_e3,
    r_e3,
    s_l1,
    r_l1,
    s_l2,
    r_l2,
    s_l3,
    r_l3,
    s_i1,
    r_i1,
    s_i2,
    r_i2,
):
    g = lax.axis_index("group")
    b = lax.axis_index("band")
    barrier = pltpu.get_barrier_semaphore()
    for k in FAR_BAND:
        pl.semaphore_signal(
            barrier, inc=1, device_id=(g, lax.rem(b + k, n_band)), device_id_type=MESH
        )
    for k in FAR_GROUP[: n_group - 1]:
        pl.semaphore_signal(
            barrier, inc=1, device_id=(lax.rem(g + k, n_group), b), device_id_type=MESH
        )

    def band_peer(k):
        return lax.rem(b + n_band + k, n_band)

    def group_peer(k):
        return lax.rem(g + n_group + k, n_group)

    sent = []

    def send(source, target, send_sem, recv_sem, device):
        copy = pltpu.make_async_remote_copy(
            src_ref=source,
            dst_ref=target,
            send_sem=send_sem,
            recv_sem=recv_sem,
            device_id=device,
            device_id_type=MESH,
        )
        copy.start()
        sent.append(copy)

    def arrive(target, send_sem, recv_sem, device):
        pltpu.make_async_remote_copy(
            src_ref=target,
            dst_ref=target,
            send_sem=send_sem,
            recv_sem=recv_sem,
            device_id=device,
            device_id_type=MESH,
        ).wait_recv()

    fetches = []
    pairs = (
        (rows_far, rows_ref),
        (lons_far, lons_ref),
        (obs_far, obs_ref),
        (live_far, live_ref),
        (truth_far, truth_ref),
        (w_in_far, w_in),
        (w_down_far, w_down),
        (w_mid_far, w_mid),
        (w_up_far, w_up),
        (w_head_far, w_head),
    )
    for n, (source, target) in enumerate(pairs):
        fetch = pltpu.make_async_copy(source, target, s_in.at[n])
        fetch.start()
        fetches.append(fetch)
    for fetch in fetches[:5]:
        fetch.wait()
    slot_rows = iota((n_band * CAP, LANES), 0)
    slot_band, slot_place = slot_rows // CAP, slot_rows % CAP
    seen = jnp.zeros((n_band * CAP, LANES), jnp.int32)
    chosen = [jnp.zeros((n_band * CAP, LANES), F32) for _ in range(4)]
    for block in range(NBLK):
        mine = slot_band == band_ref[0, 0, block]
        here = jnp.logical_and(mine, seen == slot_place)
        fields = (
            rows_ref[0, block : block + 1, :].astype(F32),
            lons_ref[0, block : block + 1, :].astype(F32),
            obs_ref[0, block : block + 1, :],
            live_ref[0, block : block + 1, :].astype(F32),
        )
        chosen = [jnp.where(here, new, old) for new, old in zip(fields, chosen)]
        seen = seen + mine.astype(jnp.int32)
    for field in range(4):
        picked[field] = chosen[field]
    for q in range(n_band):
        for field in range(4):
            outbox[q, CAP * field : CAP * field + CAP, :] = picked[
                field, CAP * q : CAP * q + CAP, :
            ]

    edge_out[0] = truth_ref[0, 0:1, :]
    edge_out[1] = truth_ref[0, ROWS - 1 : ROWS, :]
    pl.semaphore_wait(barrier, n_group + n_band - 2)
    for k in FAR_BAND:
        peer = band_peer(k)
        send(outbox.at[peer], inbox.at[b], s_a.at[k], r_a.at[b], (g, peer))
    send(edge_out.at[0], edge_in.at[1], s_t.at[0], r_t.at[1], (g, band_peer(-1)))
    send(edge_out.at[1], edge_in.at[0], s_t.at[1], r_t.at[0], (g, band_peer(1)))
    inbox[b] = outbox[b]

    wide = (2 * LANES, 2 * LANES)
    row_id, col_id = iota(wide, 0), iota(wide, 1)
    base = (
        2 * (col_id % LANES) + col_id // LANES - row_id % LANES + CELL * (row_id // LANES)
    ).astype(F32)
    coefs = []
    for scale in range(4):
        ell = jnp.full((1, 2 * LANES), ell_ref[scale], F32)
        coefs.append(-0.5 / (ell * ell))

    def gauss_step(e, carry):
        gap = jnp.abs(base + (2 * CELL * e).astype(F32))
        gap = jnp.minimum(gap, LON - gap)
        square = gap * gap
        cols = pl.ds(pl.multiple_of(e * 2 * LANES, 2 * LANES), 2 * LANES)
        for scale in range(4):
            gauss[scale, :, cols] = jnp.exp(square * coefs[scale]).astype(BF16)
        return carry

    lax.fori_loop(0, SLABS // 2, gauss_step, 0)

    weave = (col_id == 2 * (row_id % LANES) + row_id // LANES).astype(F32).astype(BF16)

    left_id = iota((32, LANES), 0)
    left_row = (left_id % 4).astype(F32)
    with_obs = (left_id // 4) % 2 == 1
    left_coef = jnp.zeros((32, LANES), F32)
    for scale in range(4):
        left_coef = jnp.where(left_id // 8 == scale, coefs[scale][:, :LANES], left_coef)
    lane_cell = iota((LANES, LANES), 0).astype(F32)
    counted = None
    order = [0]
    for k in range(1, n_band // 2):
        order += [k, -k]
    order.append(n_band // 2)
    for first, last in ((0, 5), (5, 10), (10, 14), (14, 16)):
        lefts, rights = [], []
        for k in order[first:last]:
            peer = band_peer(-k)
            if k:
                arrive(inbox.at[peer], s_a.at[k % n_band], r_a.at[peer], (g, peer))
            fields = inbox[peer]
            for slot in range(CAP):
                row = fields[slot : slot + 1]
                lon = fields[CAP + slot : CAP + slot + 1]
                seen_value = fields[2 * CAP + slot : 2 * CAP + slot + 1]
                alive = fields[3 * CAP + slot : 3 * CAP + slot + 1]
                slab = jnp.floor((lon + 0.5) * (1.0 / CELL))
                cell = lon - CELL * slab
                gap = left_row - row
                factor = jnp.where(with_obs, alive * seen_value, alive)
                left = factor * jnp.exp(gap * gap * left_coef)
                lefts.append(
                    jnp.concatenate(
                        [jnp.where(slab == float(h), left, 0.0) for h in range(SLABS)], axis=0
                    ).astype(BF16)
                )
                rights.append(jnp.where(lane_cell == cell, 1.0, 0.0).astype(BF16))
        more = dot_t(jnp.concatenate(lefts, axis=1), jnp.concatenate(rights, axis=1))
        counted = more if counted is None else counted + more

    cuts = thirds(counted)
    for scale in range(4):
        lines = []
        for j in range(6):
            now, before = (2 * j) * 32 + 8 * scale, ((2 * j - 1) % SLABS) * 32 + 8 * scale
            for cut in cuts:
                lines.append(jnp.concatenate([cut[now : now + 8], cut[before : before + 8]], axis=1))
        spread = dot(jnp.concatenate(lines, axis=0).astype(BF16), gauss[scale])
        even, odd = [], []
        for j in range(6):
            total = None
            for e in range(6):
                at = 24 * ((j - e) % 6)
                for third in range(3):
                    piece = spread[at + 8 * third : at + 8 * third + 8, 256 * e : 256 * e + 256]
                    total = piece if total is None else total + piece
            even.append(total[:, :CELL])
            odd.append(total[:, LANES : LANES + CELL])
        for p, pieces in enumerate((even, odd)):
            sums = jnp.concatenate(pieces, axis=1)
            density, signal = sums[:4], sums[4:]
            base_p = 1.0 + density
            first, second = density / base_p, signal / base_p
            for r in range(ROWS):
                at = 8 * p + 2 * scale
                feats32[r, at : at + 1, :] = first[r : r + 1]
                feats32[r, at + 1 : at + 2, :] = second[r : r + 1]
    for r in range(ROWS):
        own_f[r] = feats32[r].astype(BF16)

    reach = (-2, -1, 1, 2)
    for n, k in enumerate(reach):
        send(own_f, far_f.at[3 - n], s_f.at[n], r_f.at[3 - n], (g, band_peer(k)))

    def feature_taps(source, scale):
        values = source.astype(F32) if scale is None else source.astype(F32) * scale
        even, odd = values[:8], values[8:]
        return jnp.concatenate([later(odd, 1), even, odd, earlier(even, 1)], axis=0).astype(BF16)

    for r in range(ROWS):
        x_f[8 + r] = feature_taps(own_f[r], None)
    for fetch in fetches[5:]:
        fetch.wait()
    for ref in (wb_in, wb_down, wb_mid, wb_up3, wb_up1, db_up, db_mid, db_down):
        ref[...] = jnp.zeros_like(ref)
    turned_in = dot_t(eye(32), w_in[...].astype(F32).reshape(72, 32).astype(BF16)).astype(BF16)
    turned_up = dot_t(eye(64), w_up[...].reshape(288, 64)).astype(BF16)
    turned_mid = dot_t(eye(32), w_mid[...].reshape(288, 32)).astype(BF16)
    turned_down = dot_t(eye(32), w_down[...].reshape(512, 32)).astype(BF16)
    for a in range(3):
        for t in range(3):
            at = (a * 3 + t) * 8
            block = turned_in[:, at : at + 8]
            for i in range(3):
                for p in range(2):
                    row, col = (2 * i + p) * 32, (i + a) * 32 + (t + p) * 8
                    wb_in[row : row + 32, col : col + 8] = block
            upper, lower = w_up[a, t, :, :32], w_up[a, t, :, 32:]
            at = ((2 - a) * 3 + 2 - t) * 32
            for i in range(2):
                for p in range(2):
                    row, col = (2 * i + p) * 32, (i + a) * 128 + (t + p) * 32
                    wb_up3[row : row + 32, col : col + 32] = upper
                    wb_up1[row : row + 32, col : col + 32] = lower
                    db_up[2 * row : 2 * row + 64, col : col + 32] = turned_up[:, at : at + 32]
                row, col = i * 32, (i + 2 * a) * 96 + t * 32
                wb_mid[row : row + 32, col : col + 32] = w_mid[a, t]
                db_mid[row : row + 32, col : col + 32] = turned_mid[:, at : at + 32]
    for a in range(4):
        for t in range(4):
            for m in range(2):
                col = (2 * m + a) * 128 + t * 32
                wb_down[m * 32 : m * 32 + 32, col : col + 32] = w_down[a, t]
    for m in range(2):
        for s in range(2):
            for p in range(2):
                row = ((2 * m + s) * 2 + p) * 32
                for a, up_down in PHASES[s]:
                    for t, left_right in PHASES[p]:
                        col = (m + up_down + 1) * 96 + (left_right + 1) * 32
                        at = (a * 4 + t) * 32
                        db_down[row : row + 32, col : col + 32] = turned_down[:, at : at + 32]
    head_row, head_col = iota((16, 384), 0), iota((16, 384), 1)
    matches = (head_col // 32) == (head_row % 8) * 2 + head_row // 8
    own_match = jnp.logical_and(matches, jnp.logical_and(head_col >= 64, head_col < 320))
    parts = []
    for k in range(2):
        line = jnp.concatenate([w_head[k : k + 1, :].astype(F32)] * 12, axis=1)
        parts.append(jnp.where(matches, line, 0.0))
    wb_head = jnp.concatenate(parts, axis=0).astype(BF16)
    db_head = dot_t(eye(384), wb_head).astype(BF16)

    for n, k in enumerate((-1, 1)):
        arrive(edge_in.at[n], s_t.at[n], r_t.at[n], (g, band_peer(k)))
    truth = jnp.concatenate(
        [edge_in[0], truth_ref[0], edge_in[1], jnp.zeros((2, LON), F32)], axis=0
    )
    truth = jnp.concatenate([truth, jnp.zeros((8, 96), F32)], axis=1)
    cuts = thirds(truth)
    lines = [cut[:, 256 * j : 256 * j + 256] for j in range(6) for cut in cuts]
    split = dot_t(jnp.concatenate(lines, axis=0).astype(BF16), weave)
    even, odd = [], []
    for j in range(6):
        one = split[24 * j : 24 * j + 8] + split[24 * j + 8 : 24 * j + 16]
        one = one + split[24 * j + 16 : 24 * j + 24]
        even.append(one[:, :LANES])
        odd.append(one[:, LANES:])
    truth_eo = jnp.concatenate(
        [jnp.concatenate(even, axis=1), jnp.concatenate(odd, axis=1)], axis=0
    )[:, :HALF]

    for n, k in enumerate(reach):
        arrive(far_f.at[n], s_f.at[n], r_f.at[n], (g, band_peer(k)))
    for n, k in enumerate(reach):
        there = as_scale(jnp.logical_and(b + k >= 0, b + k < n_band))
        start = (0, 4, 12, 16)[n]
        for r in range(ROWS):
            x_f[start + r] = feature_taps(far_f[n, r], there)

    def one_step(it, carry):
        window = x_f[pl.ds(3 * it, 5)].reshape(160, HALF)
        value = dot(wb_in[...], window)
        for i in range(3):
            row = 3 * it + i
            place = ROWS * b + row - 7
            inside = as_scale(jnp.logical_and(place >= 0, place < ROWS * n_band))
            here = value[64 * i : 64 * i + 64]
            pre_one[row] = here
            hidden = (here * sigmoid(here) * inside).astype(BF16)
            even, odd = hidden[:32], hidden[32:]
            x_one[row, 0:32] = later(odd, 1)
            x_one[row, 32:64] = even
            x_one[row, 64:96] = odd
            x_one[row, 96:128] = earlier(even, 1)
        return carry

    lax.fori_loop(0, 6, one_step, 0, unroll=3)

    def two_step(it, carry):
        value = dot(wb_down[...], x_one[pl.ds(4 * it, 6)].reshape(768, HALF))
        for m in range(2):
            row = 2 * it + m
            place = 2 * b + row - 3
            inside = as_scale(jnp.logical_and(place >= 0, place < 2 * n_band))
            here = value[32 * m : 32 * m + 32]
            pre_two[row] = here
            hidden = (here * sigmoid(here) * inside).astype(BF16)
            x_two[row, 0:32] = later(hidden, 2)
            x_two[row, 32:64] = hidden
            x_two[row, 64:96] = earlier(hidden, 2)
        return carry

    lax.fori_loop(0, 4, two_step, 0, unroll=True)

    for it in range(2):
        value = dot(wb_mid[...], x_two[2 * it : 2 * it + 6].reshape(576, HALF))
        for m in range(2):
            row = 2 * it + m
            place = 2 * b + row - 1
            inside = as_scale(jnp.logical_and(place >= 0, place < 2 * n_band))
            here = value[32 * m : 32 * m + 32]
            pre_three[row] = here
            hidden = (here * sigmoid(here) * inside).astype(BF16)
            before, after = later(hidden, 1), earlier(hidden, 1)
            for target in (2 * row, 2 * row + 1):
                x_three[target, 0:32] = before
                x_three[target, 32:64] = hidden
                x_three[target, 64:96] = hidden
                x_three[target, 96:128] = after

    def four_step(it, carry):
        value = dot(wb_up3[...], x_three[pl.ds(2 * it, 4)].reshape(512, HALF))
        value = value + dot(wb_up1[...], x_one[pl.ds(2 * it + 5, 4)].reshape(512, HALF))
        rows = pl.ds(pl.multiple_of(128 * it, 128), 128)
        pre_four[rows, :] = value
        h_four[rows, :] = (value * sigmoid(value)).astype(BF16)
        return carry

    lax.fori_loop(0, 3, four_step, 0, unroll=True)

    head = dot(wb_head, h_four[...])
    mean, raw = head[:16], head[16:]
    noise = 0.1 + jnp.maximum(raw, 0.0) + jnp.log1p(jnp.exp(-jnp.abs(raw)))
    z = (mean - truth_eo) / noise
    per_cell = noise * CELLS
    head_place = iota((16, HALF), 0) % 8 + ROWS * b - 1
    on_grid = jnp.logical_and(head_place >= 0, head_place < ROWS * n_band)
    on_grid = jnp.logical_and(on_grid, iota((16, HALF), 0) % 8 < 6)
    g_mean = jnp.where(on_grid, z / per_cell, 0.0)
    g_raw = jnp.where(on_grid, (1.0 - z * z) / per_cell * sigmoid(raw), 0.0)
    g_head = jnp.concatenate([g_mean, g_raw], axis=0).astype(BF16)

    def taps_of(target_ref, row, even, odd):
        target_ref[row, 0:32] = later(odd, 1)
        target_ref[row, 32:64] = even
        target_ref[row, 64:96] = odd
        target_ref[row, 96:128] = earlier(even, 1)

    back = dot(db_head, g_head)
    for i in range(6):
        rows = slice(64 * i, 64 * i + 64)
        value = (back[rows] * slope(pre_four[rows, :])).astype(BF16)
        g_four[i] = value
        taps_of(x_gfour, i, value[:32], value[32:])

    for it in range(2):
        value = dot(db_up[...], x_gfour[2 * it : 2 * it + 4].reshape(512, HALF))
        pooled = None
        for s in range(2):
            for p in range(2):
                at = 128 * s + 64 * p
                rounded = value[at : at + 64].astype(BF16)
                gj_one[2 * it + s, 32 * p : 32 * p + 32] = rounded[32:]
                upper = rounded[:32].astype(F32)
                pooled = upper if pooled is None else pooled + upper
        g_three[it] = (pooled * slope(pre_three[it + 1])).astype(BF16)
        for slot, k in ((2, -1), (1, 1), (3, -2) if it == 0 else (0, 2)):
            send(
                g_three.at[it],
                far_three.at[slot, it],
                s_3.at[slot, it],
                r_3.at[slot, it],
                (g, band_peer(k)),
            )

    g_all = g_four[1:5].reshape(256, HALF)
    cross = dot_t(g_head, h_four[...])
    head_grad = []
    for k in range(2):
        line = jnp.sum(
            jnp.where(own_match, cross[16 * k : 16 * k + 16], 0.0), axis=0, keepdims=True
        )
        total = line[:, 0:32]
        for n in range(1, 12):
            total = total + line[:, 32 * n : 32 * n + 32]
        head_grad.append(total)
    head_grad = jnp.concatenate(head_grad + [jnp.zeros((30, 32), F32)], axis=0)
    up_grads = []
    for ref, source in ((big_a, x_three[1:7]), (big_b, x_one[6:12])):
        ref[...] = dot_t(g_all, source.reshape(768, HALF))
        for a in range(3):
            total = None
            for i in range(4):
                for p in range(2):
                    row, col = (2 * i + p) * 32, (i + a) * 128 + p * 32
                    piece = ref[row : row + 32, col : col + 96]
                    total = piece if total is None else total + piece
            up_grads.append(total)
    cross = dot_t(g_three[...].reshape(64, HALF), x_two[1:7].reshape(576, HALF))
    mid_grads = [
        cross[0:32, 192 * a : 192 * a + 96] + cross[32:64, 192 * a + 96 : 192 * a + 192]
        for a in range(3)
    ]
    pieces = [grad[:, 32 * t : 32 * t + 32] for grad in mid_grads for t in range(3)]
    for n in range(6):
        block = jnp.concatenate([up_grads[n], pieces[n]], axis=1)
        early[4 * n : 4 * n + 4] = block.reshape(4, 8, LANES)
    early[24:28] = jnp.concatenate(pieces[6:9] + [head_grad], axis=1).reshape(4, 8, LANES)
    early[28:32] = jnp.zeros((4, 8, LANES), F32)

    def scatter_group(source, size, target, send_sems, recv_sems):
        for k in FAR_GROUP[: n_group - 1]:
            peer = group_peer(k)
            send(
                source.at[pl.ds(size * peer, size)],
                target.at[g],
                send_sems.at[k],
                recv_sems.at[g],
                (peer, b),
            )
        target[g] = source[pl.ds(size * g, size)]

    def spread_group(target, send_sems, recv_sems):
        for k in FAR_GROUP[: n_group - 1]:
            send(target.at[g], target.at[g], send_sems.at[k], recv_sems.at[g], (group_peer(k), b))

    def spread_band(target, send_sems, recv_sems):
        for k in FAR_BAND:
            send(target.at[b], target.at[b], send_sems.at[k], recv_sems.at[b], (g, band_peer(k)))

    def await_group(target, send_sems, recv_sems):
        for k in range(1, n_group):
            peer = group_peer(-k)
            arrive(target.at[peer], send_sems.at[k], recv_sems.at[peer], (peer, b))

    def await_band(target, send_sems, recv_sems):
        for k in range(1, n_band):
            peer = band_peer(-k)
            arrive(target.at[peer], send_sems.at[k], recv_sems.at[peer], (g, peer))

    def added(ref, count):
        total = ref[0]
        for n in range(1, count):
            total = total + ref[n]
        return total

    early_size, late_size = 32 // n_group, 16 // n_group
    scatter_group(early, early_size, early_got, s_e1, r_e1)

    cuts = thirds(jnp.concatenate([mean, jnp.zeros((16, 48), F32)], axis=1))
    lines = []
    for j in range(6):
        for cut in cuts:
            block = cut[:, LANES * j : LANES * j + LANES]
            lines.append(jnp.concatenate([block[:8], block[8:]], axis=1))
    woven = dot(jnp.concatenate(lines, axis=0).astype(BF16), weave)
    joined = []
    for j in range(6):
        one = woven[24 * j : 24 * j + 8] + woven[24 * j + 8 : 24 * j + 16]
        joined.append(one + woven[24 * j + 16 : 24 * j + 24])
    mean_out[0] = jnp.concatenate(joined, axis=1)[1 : 1 + ROWS, :LON]

    def spread_taps(target_ref, row, value, count):
        target_ref[row, 0:32] = later(value, count)
        target_ref[row, 32:64] = value
        target_ref[row, 64:96] = earlier(value, count)

    for m in range(2):
        spread_taps(x_gthree, 3 + m, g_three[m], 2)
    for n, k, m in ((1, -1, 0), (2, 1, 0), (3, 2, 0), (0, -2, 1), (1, -1, 1), (2, 1, 1)):
        arrive(far_three.at[n, m], s_3.at[n, m], r_3.at[n, m], (g, band_peer(k)))
        there = as_scale(jnp.logical_and(b + k >= 0, b + k < n_band))
        value = (far_three[n, m].astype(F32) * there).astype(BF16)
        spread_taps(x_gthree, 3 + 2 * k + m, value, 2)
    for it in range(2):
        value = dot(db_mid[...], x_gthree[2 * it : 2 * it + 6].reshape(576, HALF))
        for m in range(2):
            row = 2 * it + m
            place = 2 * b + row - 1
            inside = as_scale(jnp.logical_and(place >= 0, place < 2 * n_band))
            here = value[32 * m : 32 * m + 32] * slope(pre_two[2 + row]) * inside
            g_two[row] = here.astype(BF16)
    cross = dot_t(g_two[1:3].reshape(64, HALF), x_one[6:12].reshape(768, HALF))
    for a in range(4):
        block = (
            cross[0:32, 128 * a : 128 * a + 128] + cross[32:64, 128 * a + 256 : 128 * a + 384]
        )
        late[4 * a : 4 * a + 4] = block.reshape(4, 8, LANES)
    scatter_group(late, late_size, late_got, s_l1, r_l1)
    for m in range(4):
        spread_taps(x_gtwo, m, g_two[m], 1)
    value = dot(db_down[...], x_gtwo[...].reshape(384, HALF))
    for i in range(4):
        total = value[64 * i : 64 * i + 64] + gj_one[i].astype(F32)
        g_one[i] = (total * slope(pre_one[7 + i])).astype(BF16)
    cross = dot_t(x_f[7:13].reshape(192, HALF), g_one[...].reshape(256, HALF))
    in_grads = []
    for a in range(3):
        total = None
        for i in range(4):
            for p in range(2):
                row, col = (i + a) * 32 + p * 8, (2 * i + p) * 32
                piece = cross[row : row + 24, col : col + 32]
                total = piece if total is None else total + piece
        in_grads.append(total)
    in_got[g] = jnp.concatenate(
        [
            jnp.concatenate([grad[:18] for grad in in_grads], axis=1),
            jnp.concatenate([grad[18:] for grad in in_grads], axis=0),
        ],
        axis=1,
    )
    spread_group(in_got, s_i1, r_i1)
    await_group(early_got, s_e1, r_e1)
    early_part[b] = added(early_got, n_group)
    spread_band(early_part, s_e2, r_e2)
    await_group(late_got, s_l1, r_l1)
    late_part[b] = added(late_got, n_group)
    spread_band(late_part, s_l2, r_l2)
    await_group(in_got, s_i1, r_i1)
    in_part[b] = added(in_got, n_group)
    spread_band(in_part, s_i2, r_i2)
    await_band(early_part, s_e2, r_e2)
    early_full[g] = added(early_part, n_band)
    spread_group(early_full, s_e3, r_e3)
    await_band(late_part, s_l2, r_l2)
    late_full[g] = added(late_part, n_band)
    spread_group(late_full, s_l3, r_l3)
    await_band(in_part, s_i2, r_i2)
    in_out[...] = added(in_part, n_band)
    await_group(early_full, s_e3, r_e3)
    early_out[...] = early_full[...].reshape(32, 8, LANES)
    await_group(late_full, s_l3, r_l3)
    late_out[...] = late_full[...].reshape(16, 8, LANES)
    for copy in sent:
        copy.wait_send()


def outputs_kernel(
    mean_ref, early_ref, late_ref, in_ref, mean_out, in_out, down_out, mid_out, up_out, head_out
):
    mean_out[...] = mean_ref[...]
    early = [early_ref[4 * n : 4 * n + 4].reshape(32, LANES) for n in range(7)]
    pieces = [early[n][:, 96:128] for n in range(6)]
    pieces += [early[6][:, 32 * t : 32 * t + 32] for t in range(3)]
    for a in range(4):
        block = late_ref[4 * a : 4 * a + 4].reshape(32, LANES)
        for t in range(4):
            down_out[a, t] = block[:, 32 * t : 32 * t + 32]
    for a in range(3):
        for t in range(3):
            up_out[a, t] = jnp.concatenate(
                [early[a][:, 32 * t : 32 * t + 32], early[3 + a][:, 32 * t : 32 * t + 32]], axis=1
            )
            mid_out[a, t] = pieces[3 * a + t]
    head_out[...] = early[6][0:2, 96:128]
    packed = in_ref[...]
    for a in range(3):
        whole = jnp.concatenate(
            [packed[:, 32 * a : 32 * a + 32], packed[6 * a : 6 * a + 6, 96:128]], axis=0
        )
        for t in range(3):
            in_out[a, t] = whole[8 * t : 8 * t + 8]


def local(
    station_rows,
    station_lons,
    station_obs,
    station_live,
    block_band,
    truth_field,
    length_scales,
    w_in,
    w_down,
    w_mid,
    w_up,
    w_head,
):
    n_group, n_band = lax.axis_size("group"), lax.axis_size("band")
    vmem = pl.BlockSpec(memory_space=pltpu.VMEM)
    smem = pl.BlockSpec(memory_space=pltpu.SMEM)
    dma = pltpu.SemaphoreType.DMA

    def space(dtype, *shape):
        return pltpu.VMEM(shape, dtype)

    w_in = jnp.transpose(w_in, (0, 1, 3, 2))
    early_size, late_size = 32 // n_group, 16 // n_group
    raw = (truth_field.shape, (32, 8, LANES), (16, 8, LANES), (18, LANES))
    summed = pl.pallas_call(
        functools.partial(step_kernel, n_group, n_band),
        out_shape=[pltpu.VMEM(shape, F32) for shape in raw],
        in_specs=[pl.BlockSpec(memory_space=pl.ANY)] * 10 + [smem] * 2,
        out_specs=[vmem] * 4,
        scratch_shapes=[
            pltpu.VMEM(part.shape, part.dtype)
            for part in (
                station_rows,
                station_lons,
                station_obs,
                station_live,
                truth_field,
                w_in,
                w_down,
                w_mid,
                w_up,
                w_head,
            )
        ]
        + [
            dma((10,)),
            space(F32, 4, n_band * CAP, LANES),
            space(F32, n_band, 4 * CAP, LANES),
            space(F32, n_band, 4 * CAP, LANES),
            space(BF16, 4, 2 * LANES, 6 * 2 * LANES),
            space(F32, ROWS, 16, HALF),
            space(BF16, ROWS, 16, HALF),
            space(BF16, 4, ROWS, 16, HALF),
            space(BF16, 20, 32, HALF),
            space(BF16, 18, 128, HALF),
            space(F32, 18, 64, HALF),
            space(BF16, 8, 96, HALF),
            space(F32, 8, 32, HALF),
            space(F32, 4, 32, HALF),
            space(BF16, 8, 128, HALF),
            space(F32, 384, HALF),
            space(BF16, 384, HALF),
            space(BF16, 6, 64, HALF),
            space(F32, 2, 1, LON),
            space(F32, 2, 1, LON),
            space(BF16, 6, 128, HALF),
            space(F32, 256, 768),
            space(F32, 256, 768),
            space(BF16, 4, 64, HALF),
            space(BF16, 2, 32, HALF),
            space(BF16, 4, 2, 32, HALF),
            space(BF16, 8, 96, HALF),
            space(BF16, 4, 32, HALF),
            space(BF16, 4, 96, HALF),
            space(BF16, 4, 64, HALF),
            space(BF16, 192, 160),
            space(BF16, 64, 768),
            space(BF16, 64, 576),
            space(BF16, 128, 512),
            space(BF16, 128, 512),
            space(BF16, 256, 512),
            space(BF16, 64, 576),
            space(BF16, 256, 384),
            space(F32, 32, 8, LANES),
            space(F32, n_group, early_size, 8, LANES),
            space(F32, n_band, early_size, 8, LANES),
            space(F32, n_group, early_size, 8, LANES),
            space(F32, 16, 8, LANES),
            space(F32, n_group, late_size, 8, LANES),
            space(F32, n_band, late_size, 8, LANES),
            space(F32, n_group, late_size, 8, LANES),
            space(F32, n_group, 18, LANES),
            space(F32, n_band, 18, LANES),
            dma((n_band,)),
            dma((n_band,)),
            dma((4,)),
            dma((4,)),
            dma((2,)),
            dma((2,)),
            dma((4, 2)),
            dma((4, 2)),
        ]
        + [dma((count,)) for count in (n_group, n_band, n_group) * 2 for _ in range(2)]
        + [dma((count,)) for count in (n_group, n_band) for _ in range(2)],
        compiler_params=pltpu.CompilerParams(
            collective_id=0, has_side_effects=True, vmem_limit_bytes=VMEM_LIMIT
        ),
    )(
        station_rows,
        station_lons,
        station_obs,
        station_live,
        truth_field,
        w_in,
        w_down,
        w_mid,
        w_up,
        w_head,
        jnp.transpose(block_band, (0, 2, 1)),
        length_scales,
    )
    outs = (truth_field, w_in, w_down, w_mid, w_up, w_head)
    mean, grad_in, grad_down, grad_mid, grad_up, grad_head = pl.pallas_call(
        outputs_kernel,
        out_shape=[jax.ShapeDtypeStruct(out.shape, F32) for out in outs],
        in_specs=[vmem] * 4,
        out_specs=[vmem] * 6,
    )(*[pltpu.with_memory_space_constraint(part, pltpu.VMEM) for part in summed])
    return mean, jnp.transpose(grad_in, (0, 1, 3, 2)), grad_down, grad_mid, grad_up, grad_head


def solution(mesh):
    spread = P("group", "band", None)
    return jax.shard_map(
        local,
        mesh=mesh,
        in_specs=(spread,) * 6 + (P(),) * 6,
        out_specs=(spread,) + (P(),) * 5,
        check_vma=False,
    )
```

```python
import functools

import jax
import jax.numpy as jnp
from jax import lax
from jax.experimental import pallas as pl
from jax.experimental.pallas import tpu as pltpu
from jax.sharding import PartitionSpec as P

MESH = pl.DeviceIdType.MESH
F32 = jnp.float32
BF16 = jnp.bfloat16
PHASES = (((1, 0), (3, -1)), ((0, 1), (2, 0)))
ROWS = 4
LON = 1440
HALF = 720
NBLK = 24
CAP = 3
LANES = 128
CELL = 120
SLABS = 12
CELLS = 92160.0
FAR_GROUP = (6, 10, 7, 9, 5, 11, 2, 14, 3, 13, 8, 1, 15, 4, 12)
FAR_BAND = (7, 9, 8, 5, 11, 6, 10, 3, 13, 4, 12, 1, 15, 2, 14)
VMEM_LIMIT = 56 * 1024 * 1024


def dot(first, second):
    return lax.dot_general(first, second, (((1,), (0,)), ((), ())), preferred_element_type=F32)


def dot_t(first, second):
    return lax.dot_general(first, second, (((1,), (1,)), ((), ())), preferred_element_type=F32)


def iota(shape, dim):
    return lax.broadcasted_iota(jnp.int32, shape, dim)


def eye(size):
    return (iota((size, size), 0) == iota((size, size), 1)).astype(F32).astype(BF16)


def later(values, count):
    width = values.shape[-1]
    return jnp.concatenate([values[:, width - count :], values[:, : width - count]], axis=1)


def earlier(values, count):
    return jnp.concatenate([values[:, count:], values[:, :count]], axis=1)


def thirds(values):
    high = values.astype(BF16).astype(F32)
    rest = values - high
    middle = rest.astype(BF16).astype(F32)
    return high, middle, rest - middle


def sigmoid(values):
    return 0.5 * jnp.tanh(0.5 * values) + 0.5


def slope(values):
    squash = sigmoid(values)
    return squash * (1.0 + values * (1.0 - squash))


def as_scale(flag):
    return flag.astype(jnp.int32).astype(F32)


def step_kernel(
    n_group,
    n_band,
    rows_far,
    lons_far,
    obs_far,
    live_far,
    truth_far,
    w_in_far,
    w_down_far,
    w_mid_far,
    w_up_far,
    w_head_far,
    band_ref,
    ell_ref,
    mean_out,
    early_out,
    late_out,
    rows_ref,
    lons_ref,
    obs_ref,
    live_ref,
    truth_ref,
    w_in,
    w_down,
    w_mid,
    w_up,
    w_head,
    s_in,
    picked,
    outbox,
    inbox,
    gauss,
    feats32,
    own_f,
    far_f,
    x_f,
    x_one,
    pre_one,
    x_two,
    pre_two,
    pre_three,
    x_three,
    pre_four,
    h_four,
    g_four,
    edge_out,
    edge_in,
    x_gfour,
    big_a,
    big_b,
    gj_one,
    g_three,
    far_three,
    x_gthree,
    g_two,
    x_gtwo,
    g_one,
    wb_in,
    wb_down,
    wb_mid,
    wb_up3,
    wb_up1,
    db_up,
    db_mid,
    db_down,
    early,
    early_got,
    early_part,
    early_full,
    late,
    late_got,
    late_part,
    late_full,
    s_a,
    r_a,
    s_f,
    r_f,
    s_t,
    r_t,
    s_3,
    r_3,
    s_e1,
    r_e1,
    s_e2,
    r_e2,
    s_e3,
    r_e3,
    s_l1,
    r_l1,
    s_l2,
    r_l2,
    s_l3,
    r_l3,
):
    g = lax.axis_index("group")
    b = lax.axis_index("band")
    barrier = pltpu.get_barrier_semaphore()
    for k in FAR_BAND:
        pl.semaphore_signal(
            barrier, inc=1, device_id=(g, lax.rem(b + k, n_band)), device_id_type=MESH
        )
    for k in FAR_GROUP[: n_group - 1]:
        pl.semaphore_signal(
            barrier, inc=1, device_id=(lax.rem(g + k, n_group), b), device_id_type=MESH
        )

    def band_peer(k):
        return lax.rem(b + n_band + k, n_band)

    def group_peer(k):
        return lax.rem(g + n_group + k, n_group)

    sent = []

    def send(source, target, send_sem, recv_sem, device):
        copy = pltpu.make_async_remote_copy(
            src_ref=source,
            dst_ref=target,
            send_sem=send_sem,
            recv_sem=recv_sem,
            device_id=device,
            device_id_type=MESH,
        )
        copy.start()
        sent.append(copy)

    def arrive(target, send_sem, recv_sem, device):
        pltpu.make_async_remote_copy(
            src_ref=target,
            dst_ref=target,
            send_sem=send_sem,
            recv_sem=recv_sem,
            device_id=device,
            device_id_type=MESH,
        ).wait_recv()

    fetches = []
    pairs = (
        (rows_far, rows_ref),
        (lons_far, lons_ref),
        (obs_far, obs_ref),
        (live_far, live_ref),
        (truth_far, truth_ref),
        (w_in_far, w_in),
        (w_down_far, w_down),
        (w_mid_far, w_mid),
        (w_up_far, w_up),
        (w_head_far, w_head),
    )
    for n, (source, target) in enumerate(pairs):
        fetch = pltpu.make_async_copy(source, target, s_in.at[n])
        fetch.start()
        fetches.append(fetch)
    for fetch in fetches[:5]:
        fetch.wait()
    slot_rows = iota((n_band * CAP, LANES), 0)
    slot_band, slot_place = slot_rows // CAP, slot_rows % CAP
    seen = jnp.zeros((n_band * CAP, LANES), jnp.int32)
    chosen = [jnp.zeros((n_band * CAP, LANES), F32) for _ in range(4)]
    for block in range(NBLK):
        mine = slot_band == band_ref[0, 0, block]
        here = jnp.logical_and(mine, seen == slot_place)
        fields = (
            rows_ref[0, block : block + 1, :].astype(F32),
            lons_ref[0, block : block + 1, :].astype(F32),
            obs_ref[0, block : block + 1, :],
            live_ref[0, block : block + 1, :].astype(F32),
        )
        chosen = [jnp.where(here, new, old) for new, old in zip(fields, chosen)]
        seen = seen + mine.astype(jnp.int32)
    for field in range(4):
        picked[field] = chosen[field]
    for q in range(n_band):
        for field in range(4):
            outbox[q, CAP * field : CAP * field + CAP, :] = picked[
                field, CAP * q : CAP * q + CAP, :
            ]

    edge_out[0] = truth_ref[0, 0:1, :]
    edge_out[1] = truth_ref[0, ROWS - 1 : ROWS, :]
    pl.semaphore_wait(barrier, n_group + n_band - 2)
    for k in FAR_BAND:
        peer = band_peer(k)
        send(outbox.at[peer], inbox.at[b], s_a.at[k], r_a.at[b], (g, peer))
    send(edge_out.at[0], edge_in.at[1], s_t.at[0], r_t.at[1], (g, band_peer(-1)))
    send(edge_out.at[1], edge_in.at[0], s_t.at[1], r_t.at[0], (g, band_peer(1)))
    inbox[b] = outbox[b]

    wide = (2 * LANES, 2 * LANES)
    row_id, col_id = iota(wide, 0), iota(wide, 1)
    base = (
        2 * (col_id % LANES) + col_id // LANES - row_id % LANES + CELL * (row_id // LANES)
    ).astype(F32)
    coefs = []
    for scale in range(4):
        ell = jnp.full((1, 2 * LANES), ell_ref[scale], F32)
        coefs.append(-0.5 / (ell * ell))

    def gauss_step(e, carry):
        gap = jnp.abs(base + (2 * CELL * e).astype(F32))
        gap = jnp.minimum(gap, LON - gap)
        square = gap * gap
        cols = pl.ds(pl.multiple_of(e * 2 * LANES, 2 * LANES), 2 * LANES)
        for scale in range(4):
            gauss[scale, :, cols] = jnp.exp(square * coefs[scale]).astype(BF16)
        return carry

    lax.fori_loop(0, SLABS // 2, gauss_step, 0)

    weave = (col_id == 2 * (row_id % LANES) + row_id // LANES).astype(F32).astype(BF16)

    left_id = iota((32, LANES), 0)
    left_row = (left_id % 4).astype(F32)
    with_obs = (left_id // 4) % 2 == 1
    left_coef = jnp.zeros((32, LANES), F32)
    for scale in range(4):
        left_coef = jnp.where(left_id // 8 == scale, coefs[scale][:, :LANES], left_coef)
    lane_cell = iota((LANES, LANES), 0).astype(F32)
    counted = None
    order = [0]
    for k in range(1, n_band // 2):
        order += [k, -k]
    order.append(n_band // 2)
    for first, last in ((0, 5), (5, 10), (10, 14), (14, 16)):
        lefts, rights = [], []
        for k in order[first:last]:
            peer = band_peer(-k)
            if k:
                arrive(inbox.at[peer], s_a.at[k % n_band], r_a.at[peer], (g, peer))
            fields = inbox[peer]
            for slot in range(CAP):
                row = fields[slot : slot + 1]
                lon = fields[CAP + slot : CAP + slot + 1]
                seen_value = fields[2 * CAP + slot : 2 * CAP + slot + 1]
                alive = fields[3 * CAP + slot : 3 * CAP + slot + 1]
                slab = jnp.floor((lon + 0.5) * (1.0 / CELL))
                cell = lon - CELL * slab
                gap = left_row - row
                factor = jnp.where(with_obs, alive * seen_value, alive)
                left = factor * jnp.exp(gap * gap * left_coef)
                lefts.append(
                    jnp.concatenate(
                        [jnp.where(slab == float(h), left, 0.0) for h in range(SLABS)], axis=0
                    ).astype(BF16)
                )
                rights.append(jnp.where(lane_cell == cell, 1.0, 0.0).astype(BF16))
        more = dot_t(jnp.concatenate(lefts, axis=1), jnp.concatenate(rights, axis=1))
        counted = more if counted is None else counted + more

    cuts = thirds(counted)
    for scale in range(4):
        lines = []
        for j in range(6):
            now, before = (2 * j) * 32 + 8 * scale, ((2 * j - 1) % SLABS) * 32 + 8 * scale
            for cut in cuts:
                lines.append(jnp.concatenate([cut[now : now + 8], cut[before : before + 8]], axis=1))
        spread = dot(jnp.concatenate(lines, axis=0).astype(BF16), gauss[scale])
        even, odd = [], []
        for j in range(6):
            total = None
            for e in range(6):
                at = 24 * ((j - e) % 6)
                for third in range(3):
                    piece = spread[at + 8 * third : at + 8 * third + 8, 256 * e : 256 * e + 256]
                    total = piece if total is None else total + piece
            even.append(total[:, :CELL])
            odd.append(total[:, LANES : LANES + CELL])
        for p, pieces in enumerate((even, odd)):
            sums = jnp.concatenate(pieces, axis=1)
            density, signal = sums[:4], sums[4:]
            base_p = 1.0 + density
            first, second = density / base_p, signal / base_p
            for r in range(ROWS):
                at = 8 * p + 2 * scale
                feats32[r, at : at + 1, :] = first[r : r + 1]
                feats32[r, at + 1 : at + 2, :] = second[r : r + 1]
    for r in range(ROWS):
        own_f[r] = feats32[r].astype(BF16)

    reach = (-2, -1, 1, 2)
    for n, k in enumerate(reach):
        send(own_f, far_f.at[3 - n], s_f.at[n], r_f.at[3 - n], (g, band_peer(k)))

    def feature_taps(source, scale):
        values = source.astype(F32) if scale is None else source.astype(F32) * scale
        even, odd = values[:8], values[8:]
        return jnp.concatenate([later(odd, 1), even, odd, earlier(even, 1)], axis=0).astype(BF16)

    for r in range(ROWS):
        x_f[8 + r] = feature_taps(own_f[r], None)
    for fetch in fetches[5:]:
        fetch.wait()
    for ref in (wb_in, wb_down, wb_mid, wb_up3, wb_up1, db_up, db_mid, db_down):
        ref[...] = jnp.zeros_like(ref)
    turned_in = dot_t(eye(32), w_in[...].astype(F32).reshape(72, 32).astype(BF16)).astype(BF16)
    turned_up = dot_t(eye(64), w_up[...].reshape(288, 64)).astype(BF16)
    turned_mid = dot_t(eye(32), w_mid[...].reshape(288, 32)).astype(BF16)
    turned_down = dot_t(eye(32), w_down[...].reshape(512, 32)).astype(BF16)
    for a in range(3):
        for t in range(3):
            at = (a * 3 + t) * 8
            block = turned_in[:, at : at + 8]
            for i in range(3):
                for p in range(2):
                    row, col = (2 * i + p) * 32, (i + a) * 32 + (t + p) * 8
                    wb_in[row : row + 32, col : col + 8] = block
            upper, lower = w_up[a, t, :, :32], w_up[a, t, :, 32:]
            at = ((2 - a) * 3 + 2 - t) * 32
            for i in range(2):
                for p in range(2):
                    row, col = (2 * i + p) * 32, (i + a) * 128 + (t + p) * 32
                    wb_up3[row : row + 32, col : col + 32] = upper
                    wb_up1[row : row + 32, col : col + 32] = lower
                    db_up[2 * row : 2 * row + 64, col : col + 32] = turned_up[:, at : at + 32]
            for m in range(4):
                row, col = m * 32, (m + 2 * a) * 96 + t * 32
                wb_mid[row : row + 32, col : col + 32] = w_mid[a, t]
                db_mid[row : row + 32, col : col + 32] = turned_mid[:, at : at + 32]
    for a in range(4):
        for t in range(4):
            for m in range(2):
                col = (2 * m + a) * 128 + t * 32
                wb_down[m * 32 : m * 32 + 32, col : col + 32] = w_down[a, t]
    for m in range(2):
        for s in range(2):
            for p in range(2):
                row = ((2 * m + s) * 2 + p) * 32
                for a, up_down in PHASES[s]:
                    for t, left_right in PHASES[p]:
                        col = (m + up_down + 1) * 96 + (left_right + 1) * 32
                        at = (a * 4 + t) * 32
                        db_down[row : row + 32, col : col + 32] = turned_down[:, at : at + 32]
    head_row, head_col = iota((16, 384), 0), iota((16, 384), 1)
    matches = (head_col // 32) == (head_row % 8) * 2 + head_row // 8
    own_match = jnp.logical_and(matches, jnp.logical_and(head_col >= 64, head_col < 320))
    parts = []
    for k in range(2):
        line = jnp.concatenate([w_head[k : k + 1, :].astype(F32)] * 12, axis=1)
        parts.append(jnp.where(matches, line, 0.0))
    wb_head = jnp.concatenate(parts, axis=0).astype(BF16)
    db_head = dot_t(eye(384), wb_head).astype(BF16)

    for n, k in enumerate((-1, 1)):
        arrive(edge_in.at[n], s_t.at[n], r_t.at[n], (g, band_peer(k)))
    truth = jnp.concatenate(
        [edge_in[0], truth_ref[0], edge_in[1], jnp.zeros((2, LON), F32)], axis=0
    )
    truth = jnp.concatenate([truth, jnp.zeros((8, 96), F32)], axis=1)
    cuts = thirds(truth)
    lines = [cut[:, 256 * j : 256 * j + 256] for j in range(6) for cut in cuts]
    split = dot_t(jnp.concatenate(lines, axis=0).astype(BF16), weave)
    even, odd = [], []
    for j in range(6):
        one = split[24 * j : 24 * j + 8] + split[24 * j + 8 : 24 * j + 16]
        one = one + split[24 * j + 16 : 24 * j + 24]
        even.append(one[:, :LANES])
        odd.append(one[:, LANES:])
    truth_eo = jnp.concatenate(
        [jnp.concatenate(even, axis=1), jnp.concatenate(odd, axis=1)], axis=0
    )[:, :HALF]

    for n, k in enumerate(reach):
        arrive(far_f.at[n], s_f.at[n], r_f.at[n], (g, band_peer(k)))
    for n, k in enumerate(reach):
        there = as_scale(jnp.logical_and(b + k >= 0, b + k < n_band))
        start = (0, 4, 12, 16)[n]
        for r in range(ROWS):
            x_f[start + r] = feature_taps(far_f[n, r], there)

    def one_step(it, carry):
        window = x_f[pl.ds(3 * it, 5)].reshape(160, HALF)
        value = dot(wb_in[...], window)
        for i in range(3):
            row = 3 * it + i
            place = ROWS * b + row - 7
            inside = as_scale(jnp.logical_and(place >= 0, place < ROWS * n_band))
            here = value[64 * i : 64 * i + 64]
            pre_one[row] = here
            hidden = (here * sigmoid(here) * inside).astype(BF16)
            even, odd = hidden[:32], hidden[32:]
            x_one[row, 0:32] = later(odd, 1)
            x_one[row, 32:64] = even
            x_one[row, 64:96] = odd
            x_one[row, 96:128] = earlier(even, 1)
        return carry

    lax.fori_loop(0, 6, one_step, 0, unroll=3)

    def two_step(it, carry):
        value = dot(wb_down[...], x_one[pl.ds(4 * it, 6)].reshape(768, HALF))
        for m in range(2):
            row = 2 * it + m
            place = 2 * b + row - 3
            inside = as_scale(jnp.logical_and(place >= 0, place < 2 * n_band))
            here = value[32 * m : 32 * m + 32]
            pre_two[row] = here
            hidden = (here * sigmoid(here) * inside).astype(BF16)
            x_two[row, 0:32] = later(hidden, 2)
            x_two[row, 32:64] = hidden
            x_two[row, 64:96] = earlier(hidden, 2)
        return carry

    lax.fori_loop(0, 4, two_step, 0, unroll=True)

    value = dot(wb_mid[...], x_two[...].reshape(768, HALF))
    for row in range(4):
        place = 2 * b + row - 1
        inside = as_scale(jnp.logical_and(place >= 0, place < 2 * n_band))
        here = value[32 * row : 32 * row + 32]
        pre_three[row] = here
        hidden = (here * sigmoid(here) * inside).astype(BF16)
        before, after = later(hidden, 1), earlier(hidden, 1)
        for target in (2 * row, 2 * row + 1):
            x_three[target, 0:32] = before
            x_three[target, 32:64] = hidden
            x_three[target, 64:96] = hidden
            x_three[target, 96:128] = after

    def four_step(it, carry):
        value = dot(wb_up3[...], x_three[pl.ds(2 * it, 4)].reshape(512, HALF))
        value = value + dot(wb_up1[...], x_one[pl.ds(2 * it + 5, 4)].reshape(512, HALF))
        rows = pl.ds(pl.multiple_of(128 * it, 128), 128)
        pre_four[rows, :] = value
        h_four[rows, :] = (value * sigmoid(value)).astype(BF16)
        return carry

    lax.fori_loop(0, 3, four_step, 0, unroll=True)

    head = dot(wb_head, h_four[...])
    mean, raw = head[:16], head[16:]
    noise = 0.1 + jnp.maximum(raw, 0.0) + jnp.log1p(jnp.exp(-jnp.abs(raw)))
    z = (mean - truth_eo) / noise
    per_cell = noise * CELLS
    head_place = iota((16, HALF), 0) % 8 + ROWS * b - 1
    on_grid = jnp.logical_and(head_place >= 0, head_place < ROWS * n_band)
    on_grid = jnp.logical_and(on_grid, iota((16, HALF), 0) % 8 < 6)
    g_mean = jnp.where(on_grid, z / per_cell, 0.0)
    g_raw = jnp.where(on_grid, (1.0 - z * z) / per_cell * sigmoid(raw), 0.0)
    g_head = jnp.concatenate([g_mean, g_raw], axis=0).astype(BF16)

    def taps_of(target_ref, row, even, odd):
        target_ref[row, 0:32] = later(odd, 1)
        target_ref[row, 32:64] = even
        target_ref[row, 64:96] = odd
        target_ref[row, 96:128] = earlier(even, 1)

    back = dot(db_head, g_head)
    for i in range(6):
        rows = slice(64 * i, 64 * i + 64)
        value = (back[rows] * slope(pre_four[rows, :])).astype(BF16)
        g_four[i] = value
        taps_of(x_gfour, i, value[:32], value[32:])

    for it in range(2):
        value = dot(db_up[...], x_gfour[2 * it : 2 * it + 4].reshape(512, HALF))
        pooled = None
        for s in range(2):
            for p in range(2):
                at = 128 * s + 64 * p
                rounded = value[at : at + 64].astype(BF16)
                gj_one[2 * it + s, 32 * p : 32 * p + 32] = rounded[32:]
                upper = rounded[:32].astype(F32)
                pooled = upper if pooled is None else pooled + upper
        g_three[it] = (pooled * slope(pre_three[it + 1])).astype(BF16)
        for slot, k in ((2, -1), (1, 1), (3, -2) if it == 0 else (0, 2)):
            send(
                g_three.at[it],
                far_three.at[slot, it],
                s_3.at[slot, it],
                r_3.at[slot, it],
                (g, band_peer(k)),
            )

    g_all = g_four[1:5].reshape(256, HALF)
    cross = dot_t(g_head, h_four[...])
    head_grad = []
    for k in range(2):
        line = jnp.sum(
            jnp.where(own_match, cross[16 * k : 16 * k + 16], 0.0), axis=0, keepdims=True
        )
        total = line[:, 0:32]
        for n in range(1, 12):
            total = total + line[:, 32 * n : 32 * n + 32]
        head_grad.append(total)
    head_grad = jnp.concatenate(head_grad + [jnp.zeros((30, 32), F32)], axis=0)
    up_grads = []
    for ref, source in ((big_a, x_three[1:7]), (big_b, x_one[6:12])):
        ref[...] = dot_t(g_all, source.reshape(768, HALF))
        for a in range(3):
            total = None
            for i in range(4):
                for p in range(2):
                    row, col = (2 * i + p) * 32, (i + a) * 128 + p * 32
                    piece = ref[row : row + 32, col : col + 96]
                    total = piece if total is None else total + piece
            up_grads.append(total)
    cross = dot_t(g_three[...].reshape(64, HALF), x_two[1:7].reshape(576, HALF))
    mid_grads = [
        cross[0:32, 192 * a : 192 * a + 96] + cross[32:64, 192 * a + 96 : 192 * a + 192]
        for a in range(3)
    ]
    pieces = [grad[:, 32 * t : 32 * t + 32] for grad in mid_grads for t in range(3)]
    for n in range(6):
        block = jnp.concatenate([up_grads[n], pieces[n]], axis=1)
        early[4 * n : 4 * n + 4] = block.reshape(4, 8, LANES)
    early[24:28] = jnp.concatenate(pieces[6:9] + [head_grad], axis=1).reshape(4, 8, LANES)
    early[28:32] = jnp.zeros((4, 8, LANES), F32)

    def scatter_group(source, size, target, send_sems, recv_sems):
        for k in FAR_GROUP[: n_group - 1]:
            peer = group_peer(k)
            send(
                source.at[pl.ds(size * peer, size)],
                target.at[g],
                send_sems.at[k],
                recv_sems.at[g],
                (peer, b),
            )
        target[g] = source[pl.ds(size * g, size)]

    def spread_group(target, send_sems, recv_sems):
        for k in FAR_GROUP[: n_group - 1]:
            send(target.at[g], target.at[g], send_sems.at[k], recv_sems.at[g], (group_peer(k), b))

    def spread_band(target, send_sems, recv_sems):
        for k in FAR_BAND:
            send(target.at[b], target.at[b], send_sems.at[k], recv_sems.at[b], (g, band_peer(k)))

    def await_group(target, send_sems, recv_sems):
        for k in range(1, n_group):
            peer = group_peer(-k)
            arrive(target.at[peer], send_sems.at[k], recv_sems.at[peer], (peer, b))

    def await_band(target, send_sems, recv_sems):
        for k in range(1, n_band):
            peer = band_peer(-k)
            arrive(target.at[peer], send_sems.at[k], recv_sems.at[peer], (g, peer))

    def added(ref, count):
        total = ref[0]
        for n in range(1, count):
            total = total + ref[n]
        return total

    early_size = 32 // n_group
    scatter_group(early, early_size, early_got, s_e1, r_e1)

    cuts = thirds(jnp.concatenate([mean, jnp.zeros((16, 48), F32)], axis=1))
    lines = []
    for j in range(6):
        for cut in cuts:
            block = cut[:, LANES * j : LANES * j + LANES]
            lines.append(jnp.concatenate([block[:8], block[8:]], axis=1))
    woven = dot(jnp.concatenate(lines, axis=0).astype(BF16), weave)
    joined = []
    for j in range(6):
        one = woven[24 * j : 24 * j + 8] + woven[24 * j + 8 : 24 * j + 16]
        joined.append(one + woven[24 * j + 16 : 24 * j + 24])
    mean_out[0] = jnp.concatenate(joined, axis=1)[1 : 1 + ROWS, :LON]

    def spread_taps(target_ref, row, value, count):
        target_ref[row, 0:32] = later(value, count)
        target_ref[row, 32:64] = value
        target_ref[row, 64:96] = earlier(value, count)

    for m in range(2):
        spread_taps(x_gthree, 3 + m, g_three[m], 2)
    for n, k, m in ((1, -1, 0), (2, 1, 0), (3, 2, 0), (0, -2, 1), (1, -1, 1), (2, 1, 1)):
        arrive(far_three.at[n, m], s_3.at[n, m], r_3.at[n, m], (g, band_peer(k)))
        there = as_scale(jnp.logical_and(b + k >= 0, b + k < n_band))
        value = (far_three[n, m].astype(F32) * there).astype(BF16)
        spread_taps(x_gthree, 3 + 2 * k + m, value, 2)
    value = dot(db_mid[...], x_gthree[...].reshape(768, HALF))
    for row in range(4):
        place = 2 * b + row - 1
        inside = as_scale(jnp.logical_and(place >= 0, place < 2 * n_band))
        here = value[32 * row : 32 * row + 32] * slope(pre_two[2 + row]) * inside
        g_two[row] = here.astype(BF16)
    cross = dot_t(g_two[1:3].reshape(64, HALF), x_one[6:12].reshape(768, HALF))
    down_grads = []
    for a in range(4):
        block = (
            cross[0:32, 128 * a : 128 * a + 128] + cross[32:64, 128 * a + 256 : 128 * a + 384]
        )
        down_grads.append(block)
    for m in range(4):
        spread_taps(x_gtwo, m, g_two[m], 1)
    value = dot(db_down[...], x_gtwo[...].reshape(384, HALF))
    for i in range(4):
        total = value[64 * i : 64 * i + 64] + gj_one[i].astype(F32)
        g_one[i] = (total * slope(pre_one[7 + i])).astype(BF16)
    cross = dot_t(x_f[7:13].reshape(192, HALF), g_one[...].reshape(256, HALF))
    in_grads = []
    for a in range(3):
        total = None
        for i in range(4):
            for p in range(2):
                row, col = (i + a) * 32 + p * 8, (2 * i + p) * 32
                piece = cross[row : row + 24, col : col + 32]
                total = piece if total is None else total + piece
        in_grads.append(total)
    in_block = jnp.concatenate(
        [
            jnp.concatenate([grad[:18] for grad in in_grads], axis=1),
            jnp.concatenate([grad[18:] for grad in in_grads], axis=0),
        ],
        axis=1,
    )
    lines = jnp.concatenate(down_grads + [in_block, jnp.zeros((14, LANES), F32)], axis=0)
    rows = 160 // n_group
    for n in range(n_group):
        late[n] = lines[rows * n : rows * n + rows]
    for k in FAR_GROUP[: n_group - 1]:
        peer = group_peer(k)
        send(late.at[peer], late_got.at[g], s_l1.at[k], r_l1.at[g], (peer, b))
    late_got[g] = late[g]
    await_group(early_got, s_e1, r_e1)
    early_part[b] = added(early_got, n_group)
    spread_band(early_part, s_e2, r_e2)
    await_group(late_got, s_l1, r_l1)
    late_part[b] = added(late_got, n_group)
    spread_band(late_part, s_l2, r_l2)
    await_band(early_part, s_e2, r_e2)
    early_full[g] = added(early_part, n_band)
    spread_group(early_full, s_e3, r_e3)
    await_band(late_part, s_l2, r_l2)
    late_full[g] = added(late_part, n_band)
    spread_group(late_full, s_l3, r_l3)
    await_group(early_full, s_e3, r_e3)
    early_out[...] = early_full[...].reshape(32, 8, LANES)
    await_group(late_full, s_l3, r_l3)
    late_out[...] = late_full[...]
    for copy in sent:
        copy.wait_send()


def outputs_kernel(
    mean_ref, early_ref, late_ref, mean_out, in_out, down_out, mid_out, up_out, head_out
):
    mean_out[...] = mean_ref[...]
    early = [early_ref[4 * n : 4 * n + 4].reshape(32, LANES) for n in range(7)]
    pieces = [early[n][:, 96:128] for n in range(6)]
    pieces += [early[6][:, 32 * t : 32 * t + 32] for t in range(3)]
    lines = jnp.concatenate([late_ref[n] for n in range(late_ref.shape[0])], axis=0)
    for a in range(4):
        block = lines[32 * a : 32 * a + 32]
        for t in range(4):
            down_out[a, t] = block[:, 32 * t : 32 * t + 32]
    for a in range(3):
        for t in range(3):
            up_out[a, t] = jnp.concatenate(
                [early[a][:, 32 * t : 32 * t + 32], early[3 + a][:, 32 * t : 32 * t + 32]], axis=1
            )
            mid_out[a, t] = pieces[3 * a + t]
    head_out[...] = early[6][0:2, 96:128]
    packed = lines[128:146]
    for a in range(3):
        whole = jnp.concatenate(
            [packed[:, 32 * a : 32 * a + 32], packed[6 * a : 6 * a + 6, 96:128]], axis=0
        )
        for t in range(3):
            in_out[a, t] = whole[8 * t : 8 * t + 8]


def local(
    station_rows,
    station_lons,
    station_obs,
    station_live,
    block_band,
    truth_field,
    length_scales,
    w_in,
    w_down,
    w_mid,
    w_up,
    w_head,
):
    n_group, n_band = lax.axis_size("group"), lax.axis_size("band")
    vmem = pl.BlockSpec(memory_space=pltpu.VMEM)
    smem = pl.BlockSpec(memory_space=pltpu.SMEM)
    dma = pltpu.SemaphoreType.DMA

    def space(dtype, *shape):
        return pltpu.VMEM(shape, dtype)

    w_in = jnp.transpose(w_in, (0, 1, 3, 2))
    early_size, late_size = 32 // n_group, 160 // n_group
    raw = (truth_field.shape, (32, 8, LANES), (n_group, late_size, LANES))
    summed = pl.pallas_call(
        functools.partial(step_kernel, n_group, n_band),
        out_shape=[pltpu.VMEM(shape, F32) for shape in raw],
        in_specs=[pl.BlockSpec(memory_space=pl.ANY)] * 10 + [smem] * 2,
        out_specs=[vmem] * 3,
        scratch_shapes=[
            pltpu.VMEM(part.shape, part.dtype)
            for part in (
                station_rows,
                station_lons,
                station_obs,
                station_live,
                truth_field,
                w_in,
                w_down,
                w_mid,
                w_up,
                w_head,
            )
        ]
        + [
            dma((10,)),
            space(F32, 4, n_band * CAP, LANES),
            space(F32, n_band, 4 * CAP, LANES),
            space(F32, n_band, 4 * CAP, LANES),
            space(BF16, 4, 2 * LANES, 6 * 2 * LANES),
            space(F32, ROWS, 16, HALF),
            space(BF16, ROWS, 16, HALF),
            space(BF16, 4, ROWS, 16, HALF),
            space(BF16, 20, 32, HALF),
            space(BF16, 18, 128, HALF),
            space(F32, 18, 64, HALF),
            space(BF16, 8, 96, HALF),
            space(F32, 8, 32, HALF),
            space(F32, 4, 32, HALF),
            space(BF16, 8, 128, HALF),
            space(F32, 384, HALF),
            space(BF16, 384, HALF),
            space(BF16, 6, 64, HALF),
            space(F32, 2, 1, LON),
            space(F32, 2, 1, LON),
            space(BF16, 6, 128, HALF),
            space(F32, 256, 768),
            space(F32, 256, 768),
            space(BF16, 4, 64, HALF),
            space(BF16, 2, 32, HALF),
            space(BF16, 4, 2, 32, HALF),
            space(BF16, 8, 96, HALF),
            space(BF16, 4, 32, HALF),
            space(BF16, 4, 96, HALF),
            space(BF16, 4, 64, HALF),
            space(BF16, 192, 160),
            space(BF16, 64, 768),
            space(BF16, 128, 768),
            space(BF16, 128, 512),
            space(BF16, 128, 512),
            space(BF16, 256, 512),
            space(BF16, 128, 768),
            space(BF16, 256, 384),
            space(F32, 32, 8, LANES),
            space(F32, n_group, early_size, 8, LANES),
            space(F32, n_band, early_size, 8, LANES),
            space(F32, n_group, early_size, 8, LANES),
            space(F32, n_group, late_size, LANES),
            space(F32, n_group, late_size, LANES),
            space(F32, n_band, late_size, LANES),
            space(F32, n_group, late_size, LANES),
            dma((n_band,)),
            dma((n_band,)),
            dma((4,)),
            dma((4,)),
            dma((2,)),
            dma((2,)),
            dma((4, 2)),
            dma((4, 2)),
        ]
        + [dma((count,)) for count in (n_group, n_band, n_group) * 2 for _ in range(2)],
        compiler_params=pltpu.CompilerParams(
            collective_id=0, has_side_effects=True, vmem_limit_bytes=VMEM_LIMIT
        ),
    )(
        station_rows,
        station_lons,
        station_obs,
        station_live,
        truth_field,
        w_in,
        w_down,
        w_mid,
        w_up,
        w_head,
        jnp.transpose(block_band, (0, 2, 1)),
        length_scales,
    )
    outs = (truth_field, w_in, w_down, w_mid, w_up, w_head)
    mean, grad_in, grad_down, grad_mid, grad_up, grad_head = pl.pallas_call(
        outputs_kernel,
        out_shape=[jax.ShapeDtypeStruct(out.shape, F32) for out in outs],
        in_specs=[vmem] * 3,
        out_specs=[vmem] * 6,
    )(*[pltpu.with_memory_space_constraint(part, pltpu.VMEM) for part in summed])
    return mean, jnp.transpose(grad_in, (0, 1, 3, 2)), grad_down, grad_mid, grad_up, grad_head


def solution(mesh):
    spread = P("group", "band", None)
    return jax.shard_map(
        local,
        mesh=mesh,
        in_specs=(spread,) * 6 + (P(),) * 6,
        out_specs=(spread,) + (P(),) * 5,
        check_vma=False,
    )
```
